256 devices in a mesh: sect: 64 (over z, y, core), tp: 4 (over x).
Axes of the slice: x: 4, y: 4, z: 8, core: 2. Of those that a mesh axis runs over, the one named last changes fastest.
Arguments:
- item_hidden: bfloat16 [4096, 4096], P('sect', 'tp'), may hold values from -40 to 40
- item_gain: bfloat16 [4096], P('tp'), may hold values from 0.25 to 1.75
- send_item: int32 [64, 64, 4], P('sect'), may hold values from -1 to 63, as said below
- pos_slot: int32 [256, 192], P('sect'), may hold values from 0 to 255, as said below
- hist_len: int32 [256], P('sect'), may hold values from 64 to 128, as said below
- user_gain: bfloat16 [4096], P('tp'), may hold values from 0.25 to 1.75
- query_weight: bfloat16 [4096, 4096], P('tp', 'sect'), may hold values from -0.09375 to 0.09375
Outputs:
- item_grad: float32 [4096, 4096], P('sect', 'tp')
- user_loss: float32 [256], P('sect')
The draws below stay inside these ranges and needn't reach their ends.
Inputs may be any that keep to these rules, and one draw needn't show every extreme that they name: `send_item`: entry [o, r, s] names item o * 64 + value, owned by device o and sent to reader r, or is -1 for an empty slot. Within one (o, r) block the named items are distinct and the filled slots come first; at least half of the 4 slots (rounded down, and at least one) are filled. In every draw some reader gets 4 filled slots from every owner. `pos_slot`: entry [u, j] names a filled slot of the buffer of the device holding user u, in the order o * 4 + s; every filled slot is named by some candidate or some history position below that user's length. `hist_len`: every device's block of 4 users holds a user of length 128.
All inputs are finite; a program needn't handle non-finite values.
Results may differ from the reference program's by a relative error of at most 0.015.
Values may be sent and summed in bfloat16 or wider, within the bound.
A program may use at most 128 MiB of HBM per device.

```python
import math
import jax
import jax.numpy as jnp
from jax import lax

D = 4096
HD = 128
ITEM_DEV = 64
SLOT = 4
USER_DEV = 4
HIST = 128
CAND = 64
ITEMS = 4096
USERS = 256
BUFFER = 256
SEQ = 192
N_SECT = 64
N_TP = 4


def shared_counts(key):
    count_key, full_key = jax.random.split(jax.random.fold_in(key, 11))
    lowest = max(1, SLOT // 2)
    counts = jax.random.randint(count_key, (N_SECT, N_SECT), lowest, SLOT + 1)
    full_reader = jax.random.randint(full_key, (), 0, N_SECT)
    reader_ids = jnp.arange(N_SECT)[None, :]
    return jnp.where(reader_ids == full_reader, SLOT, counts).astype(jnp.int32)


def shared_lengths(key):
    length_key, full_key = jax.random.split(jax.random.fold_in(key, 21))
    lengths = jax.random.randint(length_key, (N_SECT, USER_DEV), HIST // 2, HIST + 1)
    full_user = jax.random.randint(full_key, (N_SECT,), 0, USER_DEV)
    user_ids = jnp.arange(USER_DEV)[None, :]
    return jnp.where(user_ids == full_user[:, None], HIST, lengths).astype(jnp.int32)


def draw_send_item(key, part):
    counts = shared_counts(key)
    pair_keys = jax.random.split(jax.random.fold_in(key, 12), N_SECT * N_SECT)

    def first_items(pair_key):
        return jax.random.permutation(pair_key, ITEM_DEV)[:SLOT]
    chosen = jax.vmap(first_items)(pair_keys).reshape(N_SECT, N_SECT, SLOT)
    slot_ids = jnp.arange(SLOT)[None, None, :]
    return jnp.where(slot_ids < counts[:, :, None], chosen, -1).astype(jnp.int32)


def draw_hist_len(key, part):
    return shared_lengths(key).reshape(USERS).astype(jnp.int32)


def draw_pos_slot(key, part):
    counts = shared_counts(key)
    lengths = shared_lengths(key)
    reader_keys = jax.random.split(jax.random.fold_in(key, 31), N_SECT)
    position_count = USER_DEV * (HIST + CAND)

    def one_reader(reader_key, reader_counts, reader_lengths):
        order_key, extra_key = jax.random.split(reader_key)
        live = (jnp.arange(SLOT)[None, :] < reader_counts[:, None]).reshape(-1).astype(jnp.int32)
        live_order = jnp.argsort(1 - live, stable=True)
        total_live = jnp.sum(live)
        history_live = jnp.arange(HIST)[None, :] < reader_lengths[:, None]
        active = jnp.concatenate([history_live, jnp.ones((USER_DEV, CAND), bool)], axis=1).reshape(-1).astype(jnp.int32)
        shuffled = jax.random.permutation(order_key, position_count)
        order = shuffled[jnp.argsort(1 - active[shuffled], stable=True)]
        extra = jax.random.randint(extra_key, (position_count,), 0, total_live)
        ranks = jnp.arange(position_count)
        picks = jnp.where(ranks < total_live, ranks, extra)
        slots = live_order[picks]
        placed = jnp.zeros((position_count,), jnp.int32).at[order].set(slots.astype(jnp.int32))
        return placed.reshape(USER_DEV, HIST + CAND)
    result = jax.vmap(one_reader)(reader_keys, counts.T, lengths)
    return result.reshape(USERS, HIST + CAND).astype(jnp.int32)


def draw_item_hidden(key, part):
    base_key, row_key, column_key = jax.random.split(jax.random.fold_in(key, 41), 3)
    row_scales = jnp.exp(jax.random.uniform(row_key, (ITEMS, 1), jnp.float32, math.log(0.3), math.log(3.0)))
    column_scales = jnp.exp(jax.random.uniform(column_key, (1, D), jnp.float32, -1.2, 1.2))
    base = jnp.clip(jax.random.normal(base_key, (ITEMS, D), jnp.float32), -4.0, 4.0)
    return (base * row_scales * column_scales).astype(jnp.bfloat16)


def block_levels(key, extent, shards, smallest, largest):
    gain, own = 1.0, jax.random.fold_in(key, 6)
    for dim, blocks in shards:
        draws = jnp.exp(jax.random.uniform(jax.random.fold_in(own, dim), (blocks,), jnp.float32, smallest / len(shards), largest / len(shards)))
        gain = gain * jnp.repeat(draws, extent[dim] // blocks).reshape([-1 if axis == dim else 1 for axis in range(len(extent))])
    return gain


def normal_values(key, extent, spread, limit, cuts=(), kind=jnp.bfloat16):
    drawn = jax.random.normal(key, extent, jnp.float32) * spread
    if len(cuts) > 0:
        drawn = block_levels(key, extent, cuts, -0.22, 0.18) * drawn
    return jnp.clip(drawn, min=-limit, max=limit).astype(kind)


def setup_inputs(seed: int = 0) -> dict:
    splits = jax.random.split(jax.random.key(seed), 8)
    return {
        "item_hidden": draw_item_hidden(jax.random.fold_in(splits[7], 71), 0),
        "item_gain": jnp.clip(1.0 + 0.15 * jax.random.normal(splits[1], (D,), jnp.float32), 0.25, 1.75).astype(jnp.bfloat16),
        "send_item": draw_send_item(jax.random.fold_in(splits[7], 71), 0),
        "pos_slot": draw_pos_slot(jax.random.fold_in(splits[7], 71), 0),
        "hist_len": draw_hist_len(jax.random.fold_in(splits[7], 71), 0),
        "user_gain": jnp.clip(1.0 + 0.15 * jax.random.normal(splits[5], (D,), jnp.float32), 0.25, 1.75).astype(jnp.bfloat16),
        "query_weight": normal_values(splits[6], (D, D), D ** -0.5, 0.09375, ((0, 4), (1, 64))),
    }


NORM_FLOOR = 1e-06
LOGIT_SOFTNESS = 20.0

def rounded(values):
    return lax.optimization_barrier(values.astype(jnp.bfloat16)).astype(jnp.float32)

def head_norm(values, head_count):
    shaped = values.reshape(values.shape[:-1] + (head_count, values.shape[-1] // head_count))
    return shaped * lax.rsqrt(lax.optimization_barrier(jnp.mean(shaped * shaped, axis=-1, keepdims=True)) + NORM_FLOOR)

def causal_mask(lengths, history_span):
    position = jnp.arange(history_span)
    allowed = (position[None, :] <= position[:, None])[None] & (position[None, None, :] < lengths[:, None, None])
    return allowed.astype(jnp.float32)

def attend(query_rows, normed_rows, attend_mask):
    head_count = query_rows.shape[-1] // HD
    query_heads = rounded(head_norm(query_rows, head_count))
    key_heads = rounded(head_norm(normed_rows, head_count))
    value_heads = rounded(normed_rows).reshape(query_heads.shape)
    scores = jnp.einsum('uihd,ujhd->uhij', query_heads, key_heads, precision=lax.Precision.HIGHEST) * HD ** (-0.5)
    weights = jnp.exp(scores) * attend_mask[:, None]
    weights = weights / lax.optimization_barrier(jnp.sum(weights, axis=-1, keepdims=True))
    mixed_rows = jnp.einsum('uhij,ujhd->uihd', rounded(weights), value_heads, precision=lax.Precision.HIGHEST)
    return mixed_rows.reshape(query_rows.shape)

def score_parts(mixed_rows, history_rows, cand_rows):
    outputs = history_rows + mixed_rows
    follow = jnp.concatenate([history_rows[:, 1:], jnp.zeros_like(history_rows[:, :1])], axis=1)
    own_squares = lax.optimization_barrier(jnp.sum(outputs * outputs, axis=-1))
    positive_dot_products = lax.optimization_barrier(jnp.sum(outputs * follow, axis=-1))
    negative_dot_products = jnp.einsum('uif,ucf->uic', outputs, cand_rows, precision=lax.Precision.HIGHEST)
    return (own_squares, positive_dot_products, negative_dot_products)

def user_losses(own_squares, positive_dot_products, negative_dot_products, next_item_square_sums, candidate_square_sums, lengths):
    reciprocal_norm = lax.rsqrt(own_squares + NORM_FLOOR)
    positive_target_logit = LOGIT_SOFTNESS * positive_dot_products * reciprocal_norm * lax.rsqrt(next_item_square_sums + NORM_FLOOR)
    negative_score_logits = LOGIT_SOFTNESS * negative_dot_products * reciprocal_norm[..., None] * lax.rsqrt(candidate_square_sums + NORM_FLOOR)[:, None, :]
    partition = jnp.exp(positive_target_logit) + lax.optimization_barrier(jnp.sum(jnp.exp(negative_score_logits), axis=-1))
    terms = jnp.log(partition) - positive_target_logit
    position = jnp.arange(own_squares.shape[1])
    allowed = position[None, :] < lengths[:, None] - 1
    return lax.optimization_barrier(jnp.sum(jnp.where(allowed, terms, 0.0), axis=-1)) / (lengths - 1).astype(jnp.float32)

def slot_norm(slot_rows, slot_squares, gain_row):
    return slot_rows * lax.rsqrt(slot_squares / D + NORM_FLOOR)[:, None] * gain_row

def segment_rows(values, places, count):
    return jax.ops.segment_sum(values.reshape((-1,) + values.shape[2:]), places.reshape(-1), num_segments=count)

def reference(item_hidden, item_gain, send_item, pos_slot, hist_len, user_gain, query_weight):
    hidden = item_hidden.astype(jnp.float32)
    item_squares = lax.optimization_barrier(jnp.sum(hidden * hidden, axis=1, keepdims=True))
    embedded = (hidden * lax.rsqrt(item_squares / D + NORM_FLOOR) * item_gain.astype(jnp.float32)).astype(jnp.bfloat16)
    padded = jnp.concatenate([embedded, jnp.zeros((1, D), jnp.bfloat16)], axis=0)
    owner_base = (jnp.arange(N_SECT) * ITEM_DEV).astype(jnp.int32)[:, None]
    gain_row = user_gain.astype(jnp.float32)
    feature_count = D // N_TP
    weight_blocks = query_weight.reshape(N_TP, feature_count, D)

    def one_reader(running, inputs):
        send_slots, places, lengths = inputs
        flat = jnp.where(send_slots < 0, ITEMS, send_slots + owner_base).reshape(-1).astype(jnp.int32)
        slot_rows = padded[flat].astype(jnp.float32)
        slot_squares = lax.optimization_barrier(jnp.sum(slot_rows * slot_rows, axis=1))

        def norm_only(rows_in, squares_in):
            return slot_norm(rows_in, squares_in, gain_row)
        normed_slots, norm_back = jax.vjp(norm_only, slot_rows, slot_squares)
        normed_low = normed_slots.astype(jnp.bfloat16)
        normed_blocks = normed_low.reshape(BUFFER, N_TP, feature_count)
        query_slots = jnp.zeros((BUFFER, D), jnp.float32)
        for block_index in range(N_TP):
            block_term = jnp.dot(normed_blocks[:, block_index], weight_blocks[block_index], preferred_element_type=jnp.float32)
            query_slots = query_slots + rounded(block_term)
        hist_places = places[:, :HIST]
        cand_places = places[:, HIST:]
        follow_places = jnp.concatenate([hist_places[:, 1:], hist_places[:, :1]], axis=1)
        history_rows = slot_rows[hist_places]
        cand_rows = slot_rows[cand_places]
        normed_rows = normed_low[hist_places].astype(jnp.float32)
        query_rows = query_slots[hist_places]
        attend_mask = causal_mask(lengths, HIST)

        def attend_only(query_in, normed_in):
            return attend(query_in, normed_in, attend_mask)
        mixed_rows, attend_back = jax.vjp(attend_only, query_rows, normed_rows)
        stats, parts_back = jax.vjp(score_parts, mixed_rows, history_rows, cand_rows)
        next_item_square_sums = slot_squares[follow_places]
        candidate_square_sums = slot_squares[cand_places]

        def loss_only(own_in, hit_in, neg_in, follow_in, cand_in):
            return user_losses(own_in, hit_in, neg_in, follow_in, cand_in, lengths)
        losses, loss_back = jax.vjp(loss_only, stats[0], stats[1], stats[2], next_item_square_sums, candidate_square_sums)
        grad_own, grad_hit, grad_neg, grad_follow, grad_cand = loss_back(jnp.full(losses.shape, float(D), jnp.float32))
        grad_mixed, grad_history, grad_cands = parts_back((grad_own, grad_hit, grad_neg))
        grad_query, grad_normed = attend_back(grad_mixed)
        grad_slots = segment_rows(grad_history, hist_places, BUFFER) + segment_rows(grad_cands, cand_places, BUFFER)
        grad_squares = segment_rows(grad_follow, follow_places, BUFFER) + segment_rows(grad_cand, cand_places, BUFFER)
        grad_norm_slots = segment_rows(grad_normed, hist_places, BUFFER)
        grad_query_slots = segment_rows(grad_query, hist_places, BUFFER)
        grad_query_low = grad_query_slots.astype(jnp.bfloat16)
        grad_norm_slots = grad_norm_slots + jnp.dot(grad_query_low, query_weight.T, preferred_element_type=jnp.float32)
        back_rows, back_squares = norm_back(grad_norm_slots)
        grad_slots = grad_slots + back_rows + 2.0 * slot_rows * (grad_squares + back_squares)[:, None]
        running = running.at[flat].add(grad_slots)
        return (running, losses)
    sends_by_reader = jnp.transpose(send_item, (1, 0, 2))
    places_by_reader = pos_slot.reshape(N_SECT, USER_DEV, SEQ)
    lengths_by_reader = hist_len.reshape(N_SECT, USER_DEV)
    running, losses = lax.scan(one_reader, jnp.zeros((ITEMS + 1, D), jnp.float32), (sends_by_reader, places_by_reader, lengths_by_reader))
    return (running[:ITEMS], losses.reshape(USERS))
```

```python
import jax
import jax.numpy as jnp
from jax import lax
from jax.experimental import pallas as pl
from jax.experimental.pallas import tpu as pltpu
from jax.sharding import PartitionSpec as P

D = 4096
HD = 128
HIST = 128
CAND = 64
NZ, NY, NT = 8, 4, 4
NS = 64
EPS = 1e-06
SOFT = 20.0
F32, BF16 = jnp.float32, jnp.bfloat16
HI = lax.Precision.HIGHEST
MESH = pl.DeviceIdType.MESH
RING = (4, 3, 3, 4)


def mm(a, b, ca, cb, precision=None):
    return lax.dot_general(
        a, b, (((ca,), (cb,)), ((), ())), preferred_element_type=F32, precision=precision
    )


def columns(row):
    return mm(row, jnp.full((8, 128), 0.125, F32), 0, 0, HI)


def lane_sum(values):
    return jnp.sum(values, axis=1, keepdims=True)


def iota(shape, dim):
    return lax.broadcasted_iota(jnp.int32, shape, dim)


def one_hot(row, count):
    return jnp.where(iota((count, row.shape[1]), 0) == row, 1.0, 0.0)


def norm_heads(values):
    heads, roots = [], []
    for par in range(2):
        part = values[:, par * HD : (par + 1) * HD]
        root = lax.rsqrt(lane_sum(part * part) * (1.0 / HD) + EPS)
        heads.append(part * root)
        roots.append(root)
    return heads, roots


def norm_heads_back(values, grads):
    heads, roots = norm_heads(values)
    out = []
    for par in range(2):
        grad = grads[:, par * HD : (par + 1) * HD]
        out.append(
            roots[par] * (grad - heads[par] * (lane_sum(grad * heads[par]) * (1.0 / HD)))
        )
    return jnp.concatenate(out, axis=1)


def kernel(
    len_ref, hidden_ref, w_ref, gi_ref, gu_ref, sel_ref, pos_ref,
    grad_ref, loss_ref,
    hd, selb, wt, sqx, ps, pr, oute, outq, bufe, bufq, gt, nrm, knb, ssx, sqm, q32,
    rcol, rscol,
    rows_s, cand_s, kn_s, v_s, qn_s, w_s, o_s, st_r,
    aq, ak, av, ae, gsq, dqo, eo, rq, re, dqg, gws, gwr, es, er, nbx, nwx,
    xs, xr, ys, yr, ring_s, ring_r, par_s, par_r, a2a_s, a2a_r,
):
    me = lax.axis_index("sect")
    t = lax.axis_index("tp")
    z, y, c = me // 8, (me // 2) % 4, me % 2
    blk = z * 2 + c

    def send(src, dst, ssem, rsem, sect, tp):
        return pltpu.make_async_remote_copy(
            src_ref=src, dst_ref=dst, send_sem=ssem, recv_sem=rsem,
            device_id=(sect, tp), device_id_type=MESH,
        )

    def sect_of(zz, yy, cc):
        return zz * 8 + yy * 2 + cc

    def x_copy(k, src, dst, j):
        peer = (t + j) % NT
        return send(src(peer), dst.at[t], xs.at[k, j], xr.at[k, j], me, peer)

    def x_from(k, src, dst, j):
        sender = (t + NT - j) % NT
        return send(src(t), dst.at[sender], xs.at[k, j], xr.at[k, j], me, sender)

    def y_copy(k, src, dst, j):
        peer = (y + j) % NY
        return send(src(peer), dst.at[y], ys.at[k, j], yr.at[k, j], sect_of(z, peer, c), t)

    def y_from(k, src, dst, j):
        sender = (y + NY - j) % NY
        return send(src(y), dst.at[sender], ys.at[k, j], yr.at[k, j], sect_of(z, sender, c), t)

    def start3(copy, k, src, dst):
        for j in (2, 1, 3):
            copy(k, src, dst, j).start()

    def wait_in(came, k, src, dst):
        for j in (1, 3, 2):
            came(k, src, dst, j).wait_recv()

    def wait_out(copy, k, src, dst):
        for j in (1, 3, 2):
            copy(k, src, dst, j).wait_send()

    def rows_of(first):
        return pl.ds(pl.multiple_of(first * 16, 16), 16)

    def to_readers(k, out, buf):
        pltpu.make_async_copy(
            out.at[rows_of(me)], buf.at[y, rows_of(blk)], a2a_r.at[k]
        ).start()

        def step(j, carry):
            peer = (me + j) % NS
            send(
                out.at[rows_of(peer)], buf.at[y, rows_of(blk)], a2a_s.at[k], a2a_r.at[k], peer, t
            ).start()
            return carry

        lax.fori_loop(1, NS, step, 0)

    def to_groups(k, out, buf):
        pltpu.make_async_copy(
            out.at[y, rows_of(blk)], buf.at[rows_of(me)], a2a_r.at[k]
        ).start()

        def step(j, carry):
            peer = (me + j) % NS
            pz, py, pc = peer // 8, (peer // 2) % 4, peer % 2
            send(
                out.at[py, rows_of(pz * 2 + pc)], buf.at[rows_of(me)],
                a2a_s.at[k], a2a_r.at[k], peer, t,
            ).start()
            return carry

        lax.fori_loop(1, NS, step, 0)

    def all_in(k, buf):
        pltpu.make_async_copy(buf, buf, a2a_r.at[k]).wait()

    def all_out(k, flat):
        part = flat.at[pl.ds(0, (NS - 1) * 16)]
        pltpu.make_async_copy(part, part, a2a_s.at[k]).wait()

    def ring(stream, step):
        way = 1 if stream < 2 else NZ - 1
        block = (z + (NZ - way) * step) % NZ
        part = wt.at[block, c, pl.ds((stream % 2) * 32, 32)]
        return send(
            part, part, ring_s.at[stream, step], ring_r.at[stream, step],
            sect_of((z + way) % NZ, y, c), t,
        )

    def ring_from(stream, step):
        way = 1 if stream < 2 else NZ - 1
        block = (z + (NZ - way) * (step + 1)) % NZ
        part = wt.at[block, c, pl.ds((stream % 2) * 32, 32)]
        return block, send(
            part, part, ring_s.at[stream, step], ring_r.at[stream, step],
            sect_of((z + way) % NZ, y, c), t,
        )

    def partner(block, core, half):
        part = wt.at[block, core, pl.ds(half * 32, 32)]
        return send(
            part, part, par_s.at[block, half], par_r.at[block, half], sect_of(z, y, 1 - c), t
        )

    def advance(step):
        for stream in range(4):
            if step >= RING[stream]:
                continue
            block, came = ring_from(stream, step)
            came.wait_recv()
            if step + 1 < RING[stream]:
                ring(stream, step + 1).start()
            partner(block, c, stream % 2).start()

    barrier = pltpu.get_barrier_semaphore()

    def greet(j, carry):
        pl.semaphore_signal(barrier, inc=1, device_id=((me + j) % NS, t), device_id_type=MESH)
        return carry

    lax.fori_loop(1, NS, greet, 0)
    for j in range(1, NT):
        pl.semaphore_signal(barrier, inc=1, device_id=(me, (t + j) % NT), device_id_type=MESH)

    hd[y] = hidden_ref[...]
    selb[y] = sel_ref[...]
    eye = jnp.where(iota((64, 64), 0) == iota((64, 64), 1), 1.0, 0.0).astype(BF16)
    wt[z, c] = mm(eye, w_ref[...], 1, 1).astype(BF16)
    for ref in (aq, ak, av, ae):
        ref[...] = jnp.zeros(ref.shape, F32)
    gsq[...] = jnp.zeros(gsq.shape, F32)
    pl.semaphore_wait(barrier, NS - 1 + NT - 1)

    own_hd = lambda peer: hd.at[y]
    own_sel = lambda peer: selb.at[y]
    for stream in range(4):
        ring(stream, 0).start()
    start3(y_copy, 0, own_hd, hd)
    start3(y_copy, 1, own_sel, selb)
    for half in range(2):
        partner(z, c, half).start()
    advance(0)
    advance(1)

    wait_in(y_from, 0, own_hd, hd)
    gi = gi_ref[...].astype(F32)
    gu = gu_ref[...].astype(F32)
    ones = jnp.ones((8, 1024), F32)
    hidden = hd[...].reshape(256, 1024).astype(F32)
    gained = hidden * gi
    sqx[t, pl.ds(0, 8), :] = mm(ones, hidden * hidden, 1, 1, HI)
    sqx[t, pl.ds(8, 8), :] = mm(ones, gained * gained, 1, 1, HI)
    own_sqx = lambda peer: sqx.at[t]
    start3(x_copy, 0, own_sqx, sqx)
    wait_in(y_from, 1, own_sel, selb)
    picks = jnp.maximum(jnp.maximum(selb[0], selb[1]), jnp.maximum(selb[2], selb[3]))
    gt[...] = one_hot(picks, 256).astype(BF16)
    advance(2)
    wait_in(x_from, 0, own_sqx, sqx)
    sums = sqx[0] + sqx[1] + sqx[2] + sqx[3]
    r_row = lax.rsqrt(sums[0:8] * (1.0 / D) + EPS)
    rs_row = lax.rsqrt(r_row * r_row * sums[8:16] * (1.0 / D) + EPS)
    rcol[...] = columns(r_row)
    rscol[...] = columns(rs_row)
    pieces = []
    for par in range(2):
        lanes = pl.ds(pl.multiple_of((par * 4 + y) * HD, HD), HD)
        piece = hd[:, :, lanes].reshape(256, HD).astype(F32)
        gain = gi_ref[:, lanes].astype(F32)
        pieces.append((piece * rcol[...] * gain).astype(BF16))
    oute[...] = mm(gt[...], jnp.concatenate(pieces, axis=1), 0, 0).astype(BF16)
    to_readers(0, oute, bufe)

    lhs = (hd[...].reshape(256, 1024).astype(F32) * (gi * gu)).astype(BF16)
    advance(3)
    for b in range(NZ):
        for half in range(2):
            partner(b, 1 - c, half).wait_recv()
    ps_of = lambda peer: ps.at[peer]
    for tt in range(NT):
        block = wt[2 * tt : 2 * tt + 2].reshape(256, 1024)
        ps[tt] = mm(lhs, block, 1, 1).astype(BF16)
    start3(x_copy, 1, ps_of, pr)
    pr[t] = ps[t]
    wait_in(x_from, 1, ps_of, pr)
    total = (
        pr[0].astype(F32) + pr[1].astype(F32) + pr[2].astype(F32) + pr[3].astype(F32)
    ) * (rcol[...] * rscol[...])[:, 0:1]
    q32[...] = total
    heads, _ = norm_heads(total)
    outq[...] = mm(gt[...], jnp.concatenate(heads, axis=1).astype(BF16), 0, 0).astype(BF16)
    to_readers(1, outq, bufq)

    all_in(0, bufe)
    ones_q = jnp.ones((8, 256), F32)
    part = jnp.zeros((8, 256), F32)
    for q in range(4):
        rows = bufe[q].astype(F32)
        part = part + mm(ones_q, rows * rows, 1, 1, HI)
    ssx[t] = part
    own_ssx = lambda peer: ssx.at[t]
    start3(x_copy, 2, own_ssx, ssx)

    def gain_of(q):
        return jnp.concatenate(
            [gu[:, q * HD : (q + 1) * HD], gu[:, (4 + q) * HD : (5 + q) * HD]], axis=1
        )

    def hist_hot(u):
        return one_hot(pos_ref[u], 256)

    def cand_hot(u):
        return one_hot(pos_ref[4 + u], 256)

    wait_in(x_from, 2, own_ssx, ssx)
    sq_row = ssx[0] + ssx[1] + ssx[2] + ssx[3]
    sqm[...] = columns(sq_row)
    rs = lax.rsqrt(sqm[...] * (1.0 / D) + EPS)[:, 0:1]
    for q in range(4):
        low = (bufe[q].astype(F32) * rs * gain_of(q)).astype(BF16)
        nrm[q] = low
        heads, _ = norm_heads(low.astype(F32))
        knb[q] = jnp.concatenate(heads, axis=1).astype(BF16)

    def gather_user(u, carry):
        hot = hist_hot(u).astype(BF16)
        hot_c = cand_hot(u).astype(BF16)
        for q in range(4):
            rows_s[u, q] = mm(hot, bufe[q], 0, 0).astype(BF16)
            cand_s[u, q] = mm(hot_c, bufe[q], 0, 0).astype(BF16)
            kn_s[u, q] = mm(hot, knb[q], 0, 0).astype(BF16)
            v_s[u, q] = mm(hot, nrm[q], 0, 0).astype(BF16)
        return carry

    lax.fori_loop(0, 4, gather_user, 0)
    all_in(1, bufq)

    scale = HD ** (-0.5)
    row_id = iota((HIST, HIST), 0)
    col_id = iota((HIST, HIST), 1)

    def follow_of(rows):
        moved = pltpu.roll(rows, HIST - 1, 0)
        return jnp.where(iota(rows.shape, 0) < HIST - 1, moved, 0.0)

    def st_copy(u, j):
        peer = (t + j) % NT
        return send(st_r.at[t, u], st_r.at[t, u], xs.at[8 + u, j], xr.at[8 + u, j], me, peer)

    def st_from(u, j):
        sender = (t + NT - j) % NT
        return send(
            st_r.at[t, u], st_r.at[sender, u], xs.at[8 + u, j], xr.at[8 + u, j], me, sender
        )

    def forward_user(u, carry):
        hot = hist_hot(u).astype(BF16)
        mask = jnp.where((col_id <= row_id) & (col_id < len_ref[u]), 1.0, 0.0)
        own = jnp.zeros((HIST, 1), F32)
        hit = jnp.zeros((HIST, 1), F32)
        neg = jnp.zeros((HIST, HIST), F32)
        for q in range(4):
            qn = mm(hot, bufq[q], 0, 0).astype(BF16)
            qn_s[u, q] = qn
            kn = kn_s[u, q]
            val = v_s[u, q]
            mixed = []
            for par in range(2):
                lanes = slice(par * HD, (par + 1) * HD)
                weights = jnp.exp(mm(qn[:, lanes], kn[:, lanes], 1, 1) * scale) * mask
                weights = (weights / lane_sum(weights)).astype(BF16)
                w_s[u, 2 * q + par] = weights
                mixed.append(mm(weights, val[:, lanes], 1, 0))
            rows = rows_s[u, q].astype(F32)
            out = rows + jnp.concatenate(mixed, axis=1)
            o_s[u, q] = out
            own = own + lane_sum(out * out)
            hit = hit + lane_sum(out * follow_of(rows))
            high = out.astype(BF16)
            low = (out - high.astype(F32)).astype(BF16)
            cands = cand_s[u, q]
            neg = neg + mm(high, cands, 1, 1) + mm(low, cands, 1, 1)
        stats = neg + jnp.where(col_id == CAND, own, 0.0) + jnp.where(col_id == CAND + 1, hit, 0.0)
        st_r[t, u] = stats.astype(BF16)
        for j in (2, 1, 3):
            st_copy(u, j).start()
        return carry

    lax.fori_loop(0, 4, forward_user, 0)

    def backward_user(u, carry):
        for j in (1, 3, 2):
            st_from(u, j).wait_recv()
        hot32 = hist_hot(u)
        hot_c32 = cand_hot(u)
        hot = hot32.astype(BF16)
        hot_c = hot_c32.astype(BF16)
        stats = (
            st_r[0, u].astype(F32) + st_r[1, u].astype(F32)
            + st_r[2, u].astype(F32) + st_r[3, u].astype(F32)
        )
        is_cand = col_id < CAND
        neg = jnp.where(is_cand, stats, 0.0)
        own = lane_sum(jnp.where(col_id == CAND, stats, 0.0))
        hit = lane_sum(jnp.where(col_id == CAND + 1, stats, 0.0))
        sq_rows = ssx[0] + ssx[1] + ssx[2] + ssx[3]
        sq_follow = pltpu.roll(mm(hot32, sqm[...], 0, 0, HI), HIST - 1, 0)
        sq_cand = mm(sq_rows, hot_c32, 1, 0, HI)[0:1]
        rn = lax.rsqrt(own + EPS)
        rf = lax.rsqrt(sq_follow + EPS)[:, 0:1]
        rc = lax.rsqrt(sq_cand + EPS)
        tl = SOFT * hit * rn * rf
        nl = SOFT * neg * rn * rc
        en = jnp.where(is_cand, jnp.exp(nl), 0.0)
        et = jnp.exp(tl)
        whole = et + lane_sum(en)
        span = len_ref[u] - 1
        over = 1.0 / (jnp.full((HIST, 1), 0, jnp.int32) + span).astype(F32)
        valid = iota((HIST, 1), 0) < span
        terms = jnp.where(valid, (jnp.log(whole) - tl) * over, 0.0)
        loss_ref[u] = jnp.broadcast_to(jnp.sum(terms, axis=0, keepdims=True), (1, HIST))
        g = jnp.where(valid, float(D) * over, 0.0)
        dtl = g * (et / whole - 1.0)
        dnl = (g / whole) * en
        dhit = dtl * (SOFT * rn * rf)
        dneg = dnl * (SOFT * rn * rc)
        down = -0.5 * rn * rn * (dtl * tl + lane_sum(dnl * nl))
        dsqf = -0.5 * dtl * tl * rf * rf
        dsqc = -0.5 * rc * rc * jnp.sum(dnl * nl, axis=0, keepdims=True)
        gsq[...] += mm(
            hot32, pltpu.roll(jnp.broadcast_to(dsqf, (HIST, HIST)), 1, 0), 1, 0, HI
        ) + lane_sum(hot_c32 * dsqc)
        dneg_low = dneg.astype(BF16)
        for q in range(4):
            out = o_s[u, q]
            rows = rows_s[u, q].astype(F32)
            dout = (
                2.0 * down * out + dhit * follow_of(rows) + mm(dneg_low, cand_s[u, q], 1, 0)
            )
            dcand = mm(dneg_low, out.astype(BF16), 0, 0).astype(BF16)
            drows = (dout + pltpu.roll(dhit * out, 1, 0)).astype(BF16)
            ae[q] += mm(hot, drows, 1, 0) + mm(hot_c, dcand, 1, 0)
            qn = qn_s[u, q]
            kn = kn_s[u, q]
            val = v_s[u, q]
            dout_low = dout.astype(BF16)
            dqs, dks, dvs = [], [], []
            for par in range(2):
                lanes = slice(par * HD, (par + 1) * HD)
                weights = w_s[u, 2 * q + par]
                wide = weights.astype(F32)
                dw = mm(dout_low[:, lanes], val[:, lanes], 1, 1)
                ds = (wide * (dw - lane_sum(dw * wide)) * scale).astype(BF16)
                dqs.append(mm(ds, kn[:, lanes], 1, 0))
                dks.append(mm(ds, qn[:, lanes], 0, 0))
                dvs.append(mm(weights, dout_low[:, lanes], 0, 0))
            aq[q] += mm(hot, jnp.concatenate(dqs, axis=1).astype(BF16), 1, 0)
            ak[q] += mm(hot, jnp.concatenate(dks, axis=1).astype(BF16), 1, 0)
            av[q] += mm(hot, jnp.concatenate(dvs, axis=1).astype(BF16), 1, 0)
        return carry

    lax.fori_loop(0, 4, backward_user, 0)

    for q in range(4):
        dqo[q] = aq[q].astype(BF16)
    to_groups(2, dqo, rq)
    rs = lax.rsqrt(sqm[...] * (1.0 / D) + EPS)[:, 0:1]
    part = jnp.zeros((8, 256), F32)
    for q in range(4):
        dn = av[q] + norm_heads_back(nrm[q].astype(F32), ak[q])
        rows = bufe[q].astype(F32)
        dn = dn * gain_of(q)
        part = part + mm(ones_q, dn * rows, 1, 1, HI)
        av[q] = dn
    nbx[t] = part
    own_nbx = lambda peer: nbx.at[t]
    start3(x_copy, 3, own_nbx, nbx)
    wait_in(x_from, 3, own_nbx, nbx)
    nb = columns(nbx[0] + nbx[1] + nbx[2] + nbx[3])[:, 0:1]
    slot_term = 2.0 * (gsq[...][:, 0:1] - (0.5 / D) * rs * rs * rs * nb)
    for q in range(4):
        eo[q] = (ae[q] + av[q] * rs + bufe[q].astype(F32) * slot_term).astype(BF16)
    to_groups(3, eo, re)

    all_in(2, rq)
    dq_item = norm_heads_back(q32[...], mm(gt[...], rq[...], 1, 0))
    dqg[t] = dq_item.astype(BF16)
    own_dqg = lambda peer: dqg.at[t]
    start3(x_copy, 4, own_dqg, dqg)
    wait_in(x_from, 4, own_dqg, dqg)
    gws_of = lambda peer: gws.at[peer]
    acc = jnp.zeros((256, 1024), F32)
    for tt in range(NT):
        acc = acc + mm(dqg[tt], wt[2 * tt : 2 * tt + 2].reshape(256, 1024), 1, 0)
    gws[...] = acc.astype(BF16).reshape(4, 64, 1024)
    start3(y_copy, 2, gws_of, gwr)
    gwr[y] = gws[y]
    all_in(3, re)
    es[...] = mm(gt[...], re[...], 1, 0).reshape(4, 64, 256)
    es_of = lambda peer: es.at[peer]
    start3(y_copy, 3, es_of, er)
    er[y] = es[y]

    wait_in(y_from, 2, gws_of, gwr)
    gw = (
        gwr[0].astype(F32) + gwr[1].astype(F32) + gwr[2].astype(F32) + gwr[3].astype(F32)
    ) * gu
    mine = pl.ds(pl.multiple_of(y * 64, 64), 64)
    emb = (hidden_ref[...].astype(F32) * rcol[mine, 0:1] * gi).astype(BF16).astype(F32)
    prod = gw * emb
    nwx[t] = mm(ones, jnp.concatenate([prod, prod], axis=0), 1, 1, HI)
    own_nwx = lambda peer: nwx.at[t]
    start3(x_copy, 5, own_nwx, nwx)
    wait_in(y_from, 3, es_of, er)
    wait_in(x_from, 5, own_nwx, nwx)
    nw = columns(nwx[0] + nwx[1] + nwx[2] + nwx[3])[0:64, 0:1]
    rs_own = rscol[mine, 0:1]
    coef = (-1.0 / D) * rs_own * rs_own * rs_own * nw
    for h in range(8):
        lanes = slice(h * HD, (h + 1) * HD)
        par, q = h // 4, h % 4
        grad_ref[:, lanes] = (
            er[q][:, par * HD : (par + 1) * HD] + gw[:, lanes] * rs_own + emb[:, lanes] * coef
        )

    wait_out(y_copy, 0, own_hd, hd)
    wait_out(y_copy, 1, own_sel, selb)
    wait_out(y_copy, 2, gws_of, gwr)
    wait_out(y_copy, 3, es_of, er)
    wait_out(x_copy, 0, own_sqx, sqx)
    wait_out(x_copy, 1, ps_of, pr)
    wait_out(x_copy, 2, own_ssx, ssx)
    wait_out(x_copy, 3, own_nbx, nbx)
    wait_out(x_copy, 4, own_dqg, dqg)
    wait_out(x_copy, 5, own_nwx, nwx)
    for u in range(4):
        for j in (1, 3, 2):
            st_copy(u, j).wait_send()
    for stream in range(4):
        for step in range(RING[stream]):
            ring(stream, step).wait_send()
    for b in range(NZ):
        for half in range(2):
            partner(b, c, half).wait_send()
    for k, flat in ((0, oute), (1, outq), (2, rq), (3, re)):
        all_out(k, flat)


def local(item_hidden, item_gain, send_item, pos_slot, hist_len, user_gain, query_weight):
    me = lax.axis_index("sect")
    y = (me // 2) % 4
    picks = jnp.where(send_item[0] < 0, -1, send_item[0] + y * 64)
    sel = jnp.where(
        (jnp.arange(4) == y)[None, :, None], picks[:, None, :], -1
    ).reshape(1, 1024).astype(jnp.int32)
    owner, slot = pos_slot // 4, pos_slot % 4
    place = ((owner // 8 * 2 + owner % 2) * 4 + owner // 2 % 4) * 4 + slot
    cand = jnp.pad(place[:, HIST:], ((0, 0), (0, HIST - CAND)), constant_values=-1)
    pos = jnp.concatenate([place[:, :HIST], cand], axis=0).reshape(8, 1, HIST).astype(jnp.int32)
    vmem = pltpu.VMEM
    dma = pltpu.SemaphoreType.DMA
    quarter = lambda kind: vmem((4, 256, 256), kind)
    user = lambda kind: vmem((4, 4, HIST, 256), kind)
    grad, loss = pl.pallas_call(
        kernel,
        out_shape=(
            jax.ShapeDtypeStruct((64, 1024), F32),
            jax.ShapeDtypeStruct((4, 1, HIST), F32),
        ),
        in_specs=[pl.BlockSpec(memory_space=pltpu.SMEM)]
        + [pl.BlockSpec(memory_space=pltpu.VMEM)] * 6,
        out_specs=(
            pl.BlockSpec(memory_space=pltpu.VMEM),
            pl.BlockSpec(memory_space=pltpu.VMEM),
        ),
        scratch_shapes=[
            vmem((4, 64, 1024), BF16),
            vmem((4, 1, 1024), jnp.int32),
            vmem((8, 2, 64, 1024), BF16),
            vmem((4, 16, 256), F32),
            quarter(BF16),
            quarter(BF16),
            vmem((1024, 256), BF16),
            vmem((1024, 256), BF16),
            quarter(BF16),
            quarter(BF16),
            vmem((256, 1024), BF16),
            quarter(BF16),
            quarter(BF16),
            vmem((4, 8, 256), F32),
            vmem((256, HIST), F32),
            vmem((256, 256), F32),
            vmem((256, HIST), F32),
            vmem((256, HIST), F32),
            user(BF16),
            user(BF16),
            user(BF16),
            user(BF16),
            user(BF16),
            vmem((4, 8, HIST, HIST), BF16),
            user(F32),
            vmem((4, 4, HIST, HIST), BF16),
            quarter(F32),
            quarter(F32),
            quarter(F32),
            quarter(F32),
            vmem((256, HIST), F32),
            quarter(BF16),
            quarter(BF16),
            vmem((1024, 256), BF16),
            vmem((1024, 256), BF16),
            quarter(BF16),
            vmem((4, 64, 1024), BF16),
            vmem((4, 64, 1024), BF16),
            vmem((4, 64, 256), F32),
            vmem((4, 64, 256), F32),
            vmem((4, 8, 256), F32),
            vmem((4, 8, HIST), F32),
            dma((12, 4)),
            dma((12, 4)),
            dma((4, 4)),
            dma((4, 4)),
            dma((4, 4)),
            dma((4, 4)),
            dma((8, 2)),
            dma((8, 2)),
            dma((4,)),
            dma((4,)),
        ],
        compiler_params=pltpu.CompilerParams(
            collective_id=0, has_side_effects=True, vmem_limit_bytes=60 * 1024 * 1024
        ),
    )(
        hist_len, item_hidden, query_weight, item_gain.reshape(1, 1024),
        user_gain.reshape(1, 1024), sel, pos,
    )
    return (grad, loss[:, 0, 0])


def solution(mesh):
    placed = (
        P("sect", "tp"),
        P("tp"),
        P("sect", None, None),
        P("sect", None),
        P("sect"),
        P("tp"),
        P("tp", "sect"),
    )
    return jax.shard_map(
        local, mesh=mesh, in_specs=placed, out_specs=(P("sect", "tp"), P("sect")), check_vma=False
    )
```

```python
import jax
import jax.numpy as jnp
from jax import lax
from jax.experimental import pallas as pl
from jax.experimental.pallas import tpu as pltpu
from jax.sharding import PartitionSpec as P

D = 4096
HD = 128
HIST = 128
CAND = 64
NZ, NY, NT = 8, 4, 4
NS = 64
EPS = 1e-06
SOFT = 20.0
F32, BF16 = jnp.float32, jnp.bfloat16
MESH = pl.DeviceIdType.MESH
RING = (4, 3, 3, 4)


def mm(a, b, ca, cb, precision=None):
    return lax.dot_general(
        a, b, (((ca,), (cb,)), ((), ())), preferred_element_type=F32, precision=precision
    )


def split3(values):
    high = values.astype(BF16)
    rest = values - high.astype(F32)
    mid = rest.astype(BF16)
    return high, mid, (rest - mid.astype(F32)).astype(BF16)


def row_parts(row):
    parts = split3(jnp.broadcast_to(row, (8, row.shape[1])))
    index = iota((8, row.shape[1]), 0)
    out = jnp.where(index == 0, parts[0].astype(F32), 0.0)
    out = jnp.where(index == 1, parts[1].astype(F32), out)
    return jnp.where(index == 2, parts[2].astype(F32), out).astype(BF16)


def lane_parts(values):
    parts = split3(values)
    index = iota(values.shape, 1)
    out = jnp.where(index == 0, parts[0].astype(F32), 0.0)
    out = jnp.where(index == 1, parts[1].astype(F32), out)
    return jnp.where(index == 2, parts[2].astype(F32), out).astype(BF16)


def columns(row):
    return mm(row_parts(row), jnp.ones((8, 128), BF16), 0, 0)


def row_sums(values):
    ones = jnp.ones((8, values.shape[1]), BF16)
    high, mid, low = split3(values)
    return mm(ones, high, 1, 1) + mm(ones, mid, 1, 1) + mm(ones, low, 1, 1)


def lane_sum(values):
    return jnp.sum(values, axis=1, keepdims=True)


def iota(shape, dim):
    return lax.broadcasted_iota(jnp.int32, shape, dim)


def one_hot(row, count):
    return jnp.where(iota((count, row.shape[1]), 0) == row, 1.0, 0.0)


def norm_heads(values):
    heads, roots = [], []
    for par in range(2):
        part = values[:, par * HD : (par + 1) * HD]
        root = lax.rsqrt(lane_sum(part * part) * (1.0 / HD) + EPS)
        heads.append(part * root)
        roots.append(root)
    return heads, roots


def norm_heads_back(values, grads):
    heads, roots = norm_heads(values)
    out = []
    for par in range(2):
        grad = grads[:, par * HD : (par + 1) * HD]
        out.append(
            roots[par] * (grad - heads[par] * (lane_sum(grad * heads[par]) * (1.0 / HD)))
        )
    return jnp.concatenate(out, axis=1)


def kernel(
    len_ref, hidden_ref, w_ref, gi_ref, gu_ref, send_ref, pos_ref,
    grad_ref, loss_ref,
    hd, selb, wt, sqx, ps, pr, oute, outq, bufe, bufq, gt, nrm, knb, ssx, sqm, q32,
    rcol, rscol, pos_s, hot, hott, sqf_s, sqc_s,
    rc_s, kn_s, v_s, qn_s, w_s, o_s, st_r, dsc, dneg_s, gfol, grow,
    av, ae, dqo, eo, rq, re, dqg, gws, gwr, es, er, nbx, sdx, sdy,
    xs, xr, ys, yr, ring_s, ring_r, par_s, par_r, a2a_s, a2a_r,
):
    me = lax.axis_index("sect")
    t = lax.axis_index("tp")
    z, y, c = me // 8, (me // 2) % 4, me % 2
    blk = z * 2 + c

    def send(src, dst, ssem, rsem, sect, tp):
        return pltpu.make_async_remote_copy(
            src_ref=src, dst_ref=dst, send_sem=ssem, recv_sem=rsem,
            device_id=(sect, tp), device_id_type=MESH,
        )

    def sect_of(zz, yy, cc):
        return zz * 8 + yy * 2 + cc

    def x_copy(k, src, dst, j):
        peer = (t + j) % NT
        return send(src(peer), dst.at[t], xs.at[k, peer], xr.at[k, t], me, peer)

    def x_from(k, src, dst, j):
        sender = (t + NT - j) % NT
        return send(src(t), dst.at[sender], xs.at[k, sender], xr.at[k, sender], me, sender)

    def y_copy(k, src, dst, j):
        peer = (y + j) % NY
        return send(src(peer), dst.at[y], ys.at[k, peer], yr.at[k, y], sect_of(z, peer, c), t)

    def y_from(k, src, dst, j):
        sender = (y + NY - j) % NY
        return send(
            src(y), dst.at[sender], ys.at[k, sender], yr.at[k, sender], sect_of(z, sender, c), t
        )

    def start3(copy, k, src, dst):
        for j in (2, 1, 3):
            copy(k, src, dst, j).start()

    def wait_in(came, k, src, dst):
        for j in (1, 3, 2):
            came(k, src, dst, j).wait_recv()

    def wait_out(copy, k, src, dst):
        for j in (1, 3, 2):
            copy(k, src, dst, j).wait_send()

    def rows_of(first):
        return pl.ds(pl.multiple_of(first * 16, 16), 16)

    def to_readers(k, out, buf, lanes):
        pltpu.make_async_copy(
            out.at[rows_of(me), lanes], buf.at[y, rows_of(blk), lanes], a2a_r.at[k]
        ).start()

        def step(j, carry):
            peer = (me + j) % NS
            send(
                out.at[rows_of(peer), lanes], buf.at[y, rows_of(blk), lanes],
                a2a_s.at[k], a2a_r.at[k], peer, t,
            ).start()
            return carry

        lax.fori_loop(1, NS, step, 0)

    def to_group(k, out, buf, group, same):
        def copy(j):
            b = (blk + j) % 16
            return send(
                out.at[group, rows_of(b)], buf.at[rows_of(me)],
                a2a_s.at[k], a2a_r.at[k], sect_of(b // 2, group, b % 2), t,
            )

        @pl.when(same)
        def _():
            pltpu.make_async_copy(
                out.at[group, rows_of(blk)], buf.at[rows_of(me)], a2a_r.at[k]
            ).start()

        @pl.when(jnp.logical_not(same))
        def _():
            copy(0).start()

        def step(j, carry):
            copy(j).start()
            return carry

        lax.fori_loop(1, 16, step, 0)

    def all_in(k, view):
        pltpu.make_async_copy(view, view, a2a_r.at[k]).wait()

    def all_out(k, view):
        pltpu.make_async_copy(view, view, a2a_s.at[k]).wait()

    def ring(stream, step):
        way = 1 if stream < 2 else NZ - 1
        block = (z + (NZ - way) * step) % NZ
        part = wt.at[block, c, pl.ds((stream % 2) * 32, 32)]
        return send(
            part, part, ring_s.at[stream, step], ring_r.at[stream, step],
            sect_of((z + way) % NZ, y, c), t,
        )

    def ring_from(stream, step):
        way = 1 if stream < 2 else NZ - 1
        block = (z + (NZ - way) * (step + 1)) % NZ
        part = wt.at[block, c, pl.ds((stream % 2) * 32, 32)]
        return block, send(
            part, part, ring_s.at[stream, step], ring_r.at[stream, step],
            sect_of((z + way) % NZ, y, c), t,
        )

    def partner(block, core, half):
        part = wt.at[block, core, pl.ds(half * 32, 32)]
        return send(
            part, part, par_s.at[block, half], par_r.at[block, half], sect_of(z, y, 1 - c), t
        )

    def partner_in(block, half):
        partner(block, 1 - c, half).wait_recv()

    def advance(step):
        for stream in (0, 2, 1, 3):
            if step >= RING[stream]:
                continue
            block, came = ring_from(stream, step)
            came.wait_recv()
            if step + 1 < RING[stream]:
                ring(stream, step + 1).start()
            partner(block, c, stream % 2).start()

    barrier = pltpu.get_barrier_semaphore()
    for j in range(1, 8):
        pl.semaphore_signal(
            barrier, inc=1, device_id=(z * 8 + (me + j) % 8, t), device_id_type=MESH
        )
    for j in (1, NZ - 1):
        pl.semaphore_signal(
            barrier, inc=1, device_id=(sect_of((z + j) % NZ, y, c), t), device_id_type=MESH
        )
    for j in range(1, NT):
        pl.semaphore_signal(barrier, inc=1, device_id=(me, (t + j) % NT), device_id_type=MESH)

    hd[y] = hidden_ref[...]
    wt[z, c] = w_ref[...]
    spread = jnp.where((iota((64, 1024), 1) >> 4) == iota((64, 1024), 0), 1.0, 0.0).astype(BF16)
    named = mm(send_ref[...].astype(F32).astype(BF16), spread, 1, 0)
    lane = iota((1, 1024), 1)
    pick = jnp.full((1, 1024), -1.0, F32)
    for s in range(4):
        pick = jnp.where((lane & 3) == s, named[s : s + 1], pick)
    base = (jnp.zeros((1, 1024), jnp.int32) + y * 64).astype(F32)
    selb[y] = jnp.where((((lane >> 2) & 3) == y) & (pick >= 0.0), pick + base, -1.0)
    pl.semaphore_wait(barrier, 7 + 2 + NT - 1)

    own_hd = lambda peer: hd.at[y]
    own_sel = lambda peer: selb.at[y]
    for stream in (0, 2, 1, 3):
        ring(stream, 0).start()
    start3(y_copy, 0, own_hd, hd)
    start3(y_copy, 1, own_sel, selb)
    for half in range(2):
        partner(z, c, half).start()

    slots = pos_ref[...]
    owner = slots >> 2
    pos_s[...] = jnp.full(pos_s.shape, -1, jnp.int32)
    pos_s[:, 0 : HIST + CAND] = (
        ((owner >> 3) << 5) | ((owner & 1) << 4) | (((owner >> 1) & 3) << 2) | (slots & 3)
    )
    for u in range(4):
        for kind in range(2):
            row = pos_s[u : u + 1, kind * HIST : (kind + 1) * HIST]
            picked = one_hot(row, 256)
            first = (4 * kind + u) * HIST
            hot[:, first : first + HIST] = picked.astype(BF16)
            hott[first : first + HIST, :] = jnp.transpose(picked).astype(BF16)

    advance(0)
    wait_in(y_from, 0, own_hd, hd)
    gi = gi_ref[...].astype(F32).reshape(1, 1024)
    gu = gu_ref[...].astype(F32).reshape(1, 1024)
    lhs = (hd[...].reshape(256, 1024).astype(F32) * (gi * gu)).astype(BF16)

    near = z // 2
    turn = 2 * (z % 2) - 1
    order = (near, (near + turn + NT) % NT, (near - turn + NT) % NT, (near + 2) % NT)

    def ps_copy(peer):
        return send(ps.at[peer], pr.at[t], xs.at[1, peer], xr.at[1, t], me, peer)

    def project(index):
        part = order[index]
        block = wt[pl.ds(2 * part, 2)].reshape(256, 1024)
        ps[part] = mm(lhs, block, 1, 1).astype(BF16)

        @pl.when(part != t)
        def _():
            ps_copy(part).start()

    def partners_in(step):
        if step == 0:
            for half in range(2):
                partner_in(z, half)
        for stream in range(4):
            if step < RING[stream]:
                way = 1 if stream < 2 else NZ - 1
                partner_in((z + (NZ - way) * (step + 1)) % NZ, stream % 2)

    partners_in(0)
    project(0)
    hidden = hd[...].reshape(256, 1024).astype(F32)
    sqx[t, pl.ds(0, 8), :] = row_sums(hidden * hidden)
    gained = hidden * gi
    sqx[t, pl.ds(8, 8), :] = row_sums(gained * gained)
    own_sqx = lambda peer: sqx.at[t]
    start3(x_copy, 0, own_sqx, sqx)
    advance(1)
    partners_in(1)
    project(1)
    wait_in(y_from, 1, own_sel, selb)
    picks = jnp.maximum(jnp.maximum(selb[0], selb[1]), jnp.maximum(selb[2], selb[3]))
    gt[...] = one_hot(picks.astype(jnp.int32), 256).astype(BF16)
    advance(2)
    partners_in(2)
    project(2)
    wait_in(x_from, 0, own_sqx, sqx)
    sums = sqx[0] + sqx[1] + sqx[2] + sqx[3]
    r_row = lax.rsqrt(sums[0:1] * (1.0 / D) + EPS)
    rs_row = lax.rsqrt(r_row * r_row * sums[8:9] * (1.0 / D) + EPS)
    rcol[...] = columns(r_row)
    rscol[...] = columns(rs_row)
    pieces = []
    for par in range(2):
        head = par * 4 + y
        lanes = pl.ds(pl.multiple_of(head * HD, HD), HD)
        piece = hd[:, :, lanes].reshape(256, HD).astype(F32)
        gain = jnp.zeros((1, HD), F32)
        for h in range(8):
            gain = gain + jnp.where(head == h, gi[:, h * HD : (h + 1) * HD], 0.0)
        pieces.append((piece * rcol[...] * gain).astype(BF16))
    oute[...] = mm(gt[...], jnp.concatenate(pieces, axis=1), 0, 0).astype(BF16)
    advance(3)
    partners_in(3)
    project(3)
    both = slice(0, 256)
    to_readers(0, oute, bufe, both)
    pr[t] = ps[t]
    for j in (1, 3, 2):
        sender = (t + j) % NT
        send(
            ps.at[t], pr.at[sender], xs.at[1, sender], xr.at[1, sender], me, sender
        ).wait_recv()
    total = (
        pr[0].astype(F32) + pr[1].astype(F32) + pr[2].astype(F32) + pr[3].astype(F32)
    ) * (rcol[...] * rscol[...])[:, 0:1]
    q32[...] = total
    heads, _ = norm_heads(total)
    outq[...] = mm(gt[...], jnp.concatenate(heads, axis=1).astype(BF16), 0, 0).astype(BF16)
    halves = (slice(0, HD), slice(HD, 2 * HD))
    to_readers(1, outq, bufq, halves[0])
    to_readers(4, outq, bufq, halves[1])

    all_in(0, bufe)
    part = jnp.zeros((8, 256), F32)
    for q in range(4):
        rows = bufe[q].astype(F32)
        part = part + row_sums(rows * rows)
    ssx[t] = part
    own_ssx = lambda peer: ssx.at[t]
    start3(x_copy, 2, own_ssx, ssx)
    for q in range(4):
        rc_s[q] = mm(hott[...], bufe[q], 1, 0).astype(BF16)

    def gain_of(q):
        return jnp.concatenate(
            [gu[:, q * HD : (q + 1) * HD], gu[:, (4 + q) * HD : (5 + q) * HD]], axis=1
        )

    wait_in(x_from, 2, own_ssx, ssx)
    sq_row = (ssx[0] + ssx[1] + ssx[2] + ssx[3])[0:1]
    sqm[...] = columns(sq_row)
    rs = lax.rsqrt(sqm[...] * (1.0 / D) + EPS)[:, 0:1]
    for q in range(4):
        low = (bufe[q].astype(F32) * rs * gain_of(q)).astype(BF16)
        nrm[q] = low
        heads, _ = norm_heads(low.astype(F32))
        knb[q] = jnp.concatenate(heads, axis=1).astype(BF16)
    for q in range(4):
        kn_s[q] = mm(hott[0:512], knb[q], 1, 0).astype(BF16)
        v_s[q] = mm(hott[0:512], nrm[q], 1, 0).astype(BF16)
    sqf_s[...] = jnp.broadcast_to(
        lane_sum(mm(hott[0:512], lane_parts(sqm[...]), 1, 0)), (512, HIST)
    )
    sqc = jnp.sum(mm(row_parts(sq_row), hot[:, 512:1024], 1, 0), axis=0, keepdims=True)
    for u in range(4):
        sqc_s[u] = sqc[:, u * HIST : (u + 1) * HIST]

    scale = HD ** (-0.5)
    row_id = iota((HIST, HIST), 0)
    col_id = iota((HIST, HIST), 1)

    def follow_of(rows):
        moved = pltpu.roll(rows, HIST - 1, 0)
        return jnp.where(iota(rows.shape, 0) < HIST - 1, moved, 0.0)

    def st_copy(u, j):
        peer = (t + j) % NT
        return send(st_r.at[t, u], st_r.at[t, u], xs.at[6 + u, peer], xr.at[6 + u, t], me, peer)

    def st_from(u, j):
        sender = (t + NT - j) % NT
        return send(
            st_r.at[t, u], st_r.at[sender, u], xs.at[6 + u, sender], xr.at[6 + u, sender],
            me, sender,
        )

    def user_rows(u):
        return pl.ds(pl.multiple_of(u * HIST, HIST), HIST)

    def attend(u, par):
        span = user_rows(u)
        lanes = halves[par]
        mask = jnp.where((col_id <= row_id) & (col_id < len_ref[u]), 1.0, 0.0)
        for q in range(4):
            weights = jnp.exp(mm(qn_s[q, span, lanes], kn_s[q, span, lanes], 1, 1) * scale) * mask
            weights = (weights * (1.0 / lane_sum(weights))).astype(BF16)
            w_s[2 * q + par, span] = weights
            o_s[q, span, lanes] = rc_s[q, span, lanes].astype(F32) + mm(
                weights, v_s[q, span, lanes], 1, 0
            )

    def first_half(u, carry):
        attend(u, 0)
        return carry

    def second_half(u, carry):
        attend(u, 1)
        span = user_rows(u)
        cspan = user_rows(u + 4)
        own = jnp.zeros((HIST, 1), F32)
        hit = jnp.zeros((HIST, 1), F32)
        neg = jnp.zeros((HIST, HIST), F32)
        for q in range(4):
            out = o_s[q, span]
            own = own + lane_sum(out * out)
            hit = hit + lane_sum(out * follow_of(rc_s[q, span].astype(F32)))
            high = out.astype(BF16)
            low = (out - high.astype(F32)).astype(BF16)
            cands = rc_s[q, cspan]
            neg = neg + mm(high, cands, 1, 1) + mm(low, cands, 1, 1)
        stats = neg + jnp.where(col_id == CAND, own, 0.0) + jnp.where(col_id == CAND + 1, hit, 0.0)
        st_r[t, u] = stats.astype(BF16)
        for j in (2, 1, 3):
            st_copy(u, j).start()
        return carry

    for par, step in ((0, first_half), (1, second_half)):
        all_in(1 if par == 0 else 4, outq.at[:, halves[0]])
        for q in range(4):
            qn_s[q, :, halves[par]] = mm(hott[0:512], bufq[q, :, halves[par]], 1, 0).astype(BF16)
        lax.fori_loop(0, 4, step, 0)

    def losses(u, carry):
        for j in (1, 3, 2):
            st_from(u, j).wait_recv()
        stats = (
            st_r[0, u].astype(F32) + st_r[1, u].astype(F32)
            + st_r[2, u].astype(F32) + st_r[3, u].astype(F32)
        )
        is_cand = col_id < CAND
        neg = jnp.where(is_cand, stats, 0.0)
        own = lane_sum(jnp.where(col_id == CAND, stats, 0.0))
        hit = lane_sum(jnp.where(col_id == CAND + 1, stats, 0.0))
        sq_follow = pltpu.roll(sqf_s[user_rows(u)], HIST - 1, 0)[:, 0:1]
        rn = lax.rsqrt(own + EPS)
        rf = lax.rsqrt(sq_follow + EPS)
        rc = lax.rsqrt(sqc_s[u] + EPS)
        tl = SOFT * hit * rn * rf
        nl = SOFT * neg * rn * rc
        en = jnp.where(is_cand, jnp.exp(nl), 0.0)
        et = jnp.exp(tl)
        whole = et + lane_sum(en)
        span = len_ref[u] - 1
        over = 1.0 / (jnp.full((HIST, 1), 0, jnp.int32) + span).astype(F32)
        valid = iota((HIST, 1), 0) < span
        terms = jnp.where(valid, (jnp.log(whole) - tl) * over, 0.0)
        loss_ref[u] = jnp.broadcast_to(jnp.sum(terms, axis=0, keepdims=True), (1, HIST))
        g = jnp.where(valid, float(D) * over, 0.0)
        dtl = g * (et / whole - 1.0)
        dnl = (g / whole) * en
        dsc[u, 0] = jnp.broadcast_to(
            -rn * rn * (dtl * tl + lane_sum(dnl * nl)), (HIST, HIST)
        )
        dsc[u, 1] = jnp.broadcast_to(dtl * (SOFT * rn * rf), (HIST, HIST))
        dneg_s[u] = (dnl * (SOFT * rn * rc)).astype(BF16)
        dsqf = jnp.broadcast_to(-0.5 * dtl * tl * rf * rf, (HIST, HIST))
        gfol[user_rows(u)] = pltpu.roll(dsqf, 1, 0)
        grow[u] = -0.5 * rc * rc * jnp.sum(dnl * nl, axis=0, keepdims=True)
        return carry

    lax.fori_loop(0, 4, losses, 0)

    def backward_quarter(i, carry):
        q = (y + 1 + i) % 4
        for u in range(4):
            span = slice(u * HIST, (u + 1) * HIST)
            cspan = slice((4 + u) * HIST, (5 + u) * HIST)
            twice_down = jnp.concatenate([dsc[u, 0]] * 2, axis=1)
            dhit = jnp.concatenate([dsc[u, 1]] * 2, axis=1)
            out = o_s[q, span]
            rows = rc_s[q, span].astype(F32)
            cands = rc_s[q, cspan]
            dneg = dneg_s[u]
            dout = twice_down * out + dhit * follow_of(rows) + mm(dneg, cands, 1, 0)
            rc_s[q, cspan] = mm(dneg, out.astype(BF16), 0, 0).astype(BF16)
            rc_s[q, span] = (dout + pltpu.roll(dhit * out, 1, 0)).astype(BF16)
            dout_low = dout.astype(BF16)
            for par in range(2):
                lanes = halves[par]
                qn = qn_s[q, span, lanes]
                kn = kn_s[q, span, lanes]
                grad = dout_low[:, lanes]
                weights = w_s[2 * q + par, span]
                wide = weights.astype(F32)
                dw = mm(grad, v_s[q, span, lanes], 1, 1)
                ds = (wide * (dw - lane_sum(dw * wide)) * scale).astype(BF16)
                qn_s[q, span, lanes] = mm(ds, kn, 1, 0).astype(BF16)
                kn_s[q, span, lanes] = mm(ds, qn, 0, 0).astype(BF16)
                v_s[q, span, lanes] = mm(weights, grad, 0, 0).astype(BF16)
        dqo[q] = mm(hot[:, 0:512], qn_s[q], 1, 0).astype(BF16)
        to_group(2, dqo, rq, q, i == 3)
        return carry

    lax.fori_loop(0, 4, backward_quarter, 0)

    rs = lax.rsqrt(sqm[...] * (1.0 / D) + EPS)[:, 0:1]
    part = jnp.zeros((8, 256), F32)
    for q in range(4):
        dk = mm(hot[:, 0:512], kn_s[q], 1, 0)
        dn = mm(hot[:, 0:512], v_s[q], 1, 0) + norm_heads_back(nrm[q].astype(F32), dk)
        dn = dn * gain_of(q)
        part = part + row_sums(dn * bufe[q].astype(F32))
        av[q] = dn
    nbx[t] = part
    own_nbx = lambda peer: nbx.at[t]
    start3(x_copy, 3, own_nbx, nbx)
    gsq = lane_sum(mm(hot[:, 0:512], lane_parts(gfol[...]), 1, 0)) + lane_sum(
        mm(
            hot[:, 512:1024],
            row_parts(jnp.concatenate([grow[u] for u in range(4)], axis=1)), 1, 1,
        )
    )
    for q in range(4):
        ae[q] = mm(hot[...], rc_s[q], 1, 0) + av[q] * rs
    wait_in(x_from, 3, own_nbx, nbx)
    nb = columns((nbx[0] + nbx[1] + nbx[2] + nbx[3])[0:1])[:, 0:1]
    slot_term = 2.0 * (gsq - (0.5 / D) * rs * rs * rs * nb)
    for q in range(4):
        eo[q] = (ae[q] + bufe[q].astype(F32) * slot_term).astype(BF16)

    all_in(2, rq)
    dq_item = norm_heads_back(q32[...], mm(gt[...], rq[...], 1, 0)).astype(BF16)
    dqg[t] = dq_item
    own_dqg = lambda peer: dqg.at[t]
    start3(x_copy, 4, own_dqg, dqg)
    sdx[t] = row_sums(dq_item.astype(F32) * q32[...])
    own_sdx = lambda peer: sdx.at[t]
    start3(x_copy, 5, own_sdx, sdx)

    def return_group(i, carry):
        group = (y + 1 + i) % 4
        to_group(3, eo, re, group, i == 3)
        return carry

    lax.fori_loop(0, 4, return_group, 0)
    wait_in(x_from, 4, own_dqg, dqg)
    gws_of = lambda peer: gws.at[peer]
    acc = jnp.zeros((256, 1024), F32)
    for tt in range(NT):
        acc = acc + mm(dqg[tt], wt[2 * tt : 2 * tt + 2].reshape(256, 1024), 1, 0)
    gws[...] = acc.astype(BF16).reshape(4, 64, 1024)
    start3(y_copy, 2, gws_of, gwr)
    gwr[y] = gws[y]
    wait_in(x_from, 5, own_sdx, sdx)
    sdy[y] = sdx[0] + sdx[1] + sdx[2] + sdx[3]
    own_sdy = lambda peer: sdy.at[y]
    start3(y_copy, 4, own_sdy, sdy)
    all_in(3, re)
    es[...] = mm(gt[...], re[...], 1, 0).reshape(4, 64, 256)
    es_of = lambda peer: es.at[peer]
    start3(y_copy, 3, es_of, er)
    er[y] = es[y]

    mine = pl.ds(pl.multiple_of(y * 64, 64), 64)
    emb = (hidden_ref[...].astype(F32) * rcol[mine, 0:1] * gi).astype(BF16).astype(F32)
    rs_own = rscol[mine, 0:1]
    wait_in(y_from, 4, own_sdy, sdy)
    sqm[...] = columns((sdy[0] + sdy[1] + sdy[2] + sdy[3])[0:1])
    coef = (-1.0 / D) * rs_own * rs_own * sqm[mine, 0:1]
    direct = emb * coef
    wait_in(y_from, 2, gws_of, gwr)
    gw = (
        gwr[0].astype(F32) + gwr[1].astype(F32) + gwr[2].astype(F32) + gwr[3].astype(F32)
    ) * gu * rs_own + direct
    wait_in(y_from, 3, es_of, er)
    for h in range(8):
        lanes = slice(h * HD, (h + 1) * HD)
        par, q = h // 4, h % 4
        grad_ref[:, lanes] = er[q][:, par * HD : (par + 1) * HD] + gw[:, lanes]

    for k, src, dst in (
        (0, own_hd, hd), (1, own_sel, selb), (2, gws_of, gwr), (3, es_of, er), (4, own_sdy, sdy)
    ):
        wait_out(y_copy, k, src, dst)
    for k, src, dst in (
        (0, own_sqx, sqx), (2, own_ssx, ssx), (3, own_nbx, nbx), (4, own_dqg, dqg),
        (5, own_sdx, sdx),
    ):
        wait_out(x_copy, k, src, dst)
    for j in (1, 3, 2):
        ps_copy((t + j) % NT).wait_send()
    for u in range(4):
        for j in (1, 3, 2):
            st_copy(u, j).wait_send()
    for stream in range(4):
        for step in range(RING[stream]):
            ring(stream, step).wait_send()
    for b in range(NZ):
        for half in range(2):
            partner(b, c, half).wait_send()
    most = pl.ds(0, (NS - 1) * 16)
    all_out(0, oute.at[most])
    all_out(1, outq.at[most, halves[0]])
    all_out(4, outq.at[most, halves[1]])
    all_out(2, rq.at[most])
    all_out(3, re.at[most])


def local(item_hidden, item_gain, send_item, pos_slot, hist_len, user_gain, query_weight):
    vmem = pltpu.VMEM
    dma = pltpu.SemaphoreType.DMA
    quarter = lambda kind: vmem((4, 256, 256), kind)
    grad, loss = pl.pallas_call(
        kernel,
        out_shape=(
            jax.ShapeDtypeStruct((64, 1024), F32),
            jax.ShapeDtypeStruct((4, 1, HIST), F32),
        ),
        in_specs=[pl.BlockSpec(memory_space=pltpu.SMEM)]
        + [pl.BlockSpec(memory_space=pltpu.VMEM)] * 6,
        out_specs=(
            pl.BlockSpec(memory_space=pltpu.VMEM),
            pl.BlockSpec(memory_space=pltpu.VMEM),
        ),
        scratch_shapes=[
            vmem((4, 64, 1024), BF16),
            vmem((4, 1, 1024), F32),
            vmem((8, 2, 64, 1024), BF16),
            vmem((4, 16, 256), F32),
            quarter(BF16),
            quarter(BF16),
            vmem((1024, 256), BF16),
            vmem((1024, 256), BF16),
            quarter(BF16),
            quarter(BF16),
            vmem((256, 1024), BF16),
            quarter(BF16),
            quarter(BF16),
            vmem((4, 8, 256), F32),
            vmem((256, HIST), F32),
            vmem((256, 256), F32),
            vmem((256, HIST), F32),
            vmem((256, HIST), F32),
            vmem((4, 2 * HIST), jnp.int32),
            vmem((256, 1024), BF16),
            vmem((1024, 256), BF16),
            vmem((512, HIST), F32),
            vmem((4, 1, HIST), F32),
            vmem((4, 1024, 256), BF16),
            vmem((4, 512, 256), BF16),
            vmem((4, 512, 256), BF16),
            vmem((4, 512, 256), BF16),
            vmem((8, 512, HIST), BF16),
            vmem((4, 512, 256), F32),
            vmem((4, 4, HIST, HIST), BF16),
            vmem((4, 2, HIST, HIST), F32),
            vmem((4, HIST, HIST), BF16),
            vmem((512, HIST), F32),
            vmem((4, 1, HIST), F32),
            quarter(F32),
            quarter(F32),
            quarter(BF16),
            quarter(BF16),
            vmem((1024, 256), BF16),
            vmem((1024, 256), BF16),
            quarter(BF16),
            vmem((4, 64, 1024), BF16),
            vmem((4, 64, 1024), BF16),
            vmem((4, 64, 256), F32),
            vmem((4, 64, 256), F32),
            vmem((4, 8, 256), F32),
            vmem((4, 8, 256), F32),
            vmem((4, 8, 256), F32),
            dma((10, 4)),
            dma((10, 4)),
            dma((5, 4)),
            dma((5, 4)),
            dma((4, 4)),
            dma((4, 4)),
            dma((8, 2)),
            dma((8, 2)),
            dma((5,)),
            dma((5,)),
        ],
        compiler_params=pltpu.CompilerParams(
            collective_id=0, has_side_effects=True, vmem_limit_bytes=60 * 1024 * 1024
        ),
    )(
        hist_len, item_hidden, query_weight.T, item_gain, user_gain, send_item[0].T, pos_slot
    )
    return (grad, loss[:, 0, 0])


def solution(mesh):
    placed = (
        P("sect", "tp"),
        P("tp"),
        P("sect", None, None),
        P("sect", None),
        P("sect"),
        P("tp"),
        P("tp", "sect"),
    )
    return jax.shard_map(
        local, mesh=mesh, in_specs=placed, out_specs=(P("sect", "tp"), P("sect")), check_vma=False
    )
```

```python
import jax
import jax.numpy as jnp
from jax import lax
from jax.experimental import pallas as pl
from jax.experimental.pallas import tpu as pltpu
from jax.sharding import PartitionSpec as P

D = 4096
HD = 128
HIST = 128
CAND = 64
NZ, NY, NT = 8, 4, 4
NS = 64
EPS = 1e-06
SOFT = 20.0
F32, BF16 = jnp.float32, jnp.bfloat16
MESH = pl.DeviceIdType.MESH
RING = (4, 3, 3, 4)


def mm(a, b, ca, cb, precision=None):
    return lax.dot_general(
        a, b, (((ca,), (cb,)), ((), ())), preferred_element_type=F32, precision=precision
    )


def split3(values):
    high = values.astype(BF16)
    rest = values - high.astype(F32)
    mid = rest.astype(BF16)
    return high, mid, (rest - mid.astype(F32)).astype(BF16)


def row_parts(row):
    parts = split3(jnp.broadcast_to(row, (8, row.shape[1])))
    index = iota((8, row.shape[1]), 0)
    out = jnp.where(index == 0, parts[0].astype(F32), 0.0)
    out = jnp.where(index == 1, parts[1].astype(F32), out)
    return jnp.where(index == 2, parts[2].astype(F32), out).astype(BF16)


def lane_parts(values):
    parts = split3(values)
    index = iota(values.shape, 1)
    out = jnp.where(index == 0, parts[0].astype(F32), 0.0)
    out = jnp.where(index == 1, parts[1].astype(F32), out)
    return jnp.where(index == 2, parts[2].astype(F32), out).astype(BF16)


def columns(row):
    return mm(row_parts(row), jnp.ones((8, 128), BF16), 0, 0)


def row_sums(values):
    ones = jnp.ones((8, values.shape[1]), BF16)
    high, mid, low = split3(values)
    return mm(ones, high, 1, 1) + mm(ones, mid, 1, 1) + mm(ones, low, 1, 1)


def lane_sum(values):
    return jnp.sum(values, axis=1, keepdims=True)


def iota(shape, dim):
    return lax.broadcasted_iota(jnp.int32, shape, dim)


def one_hot(row, count):
    return jnp.where(iota((count, row.shape[1]), 0) == row, 1.0, 0.0)


def norm_heads(values):
    heads, roots = [], []
    for par in range(2):
        part = values[:, par * HD : (par + 1) * HD]
        root = lax.rsqrt(lane_sum(part * part) * (1.0 / HD) + EPS)
        heads.append(part * root)
        roots.append(root)
    return heads, roots


def norm_heads_back(values, grads):
    heads, roots = norm_heads(values)
    out = []
    for par in range(2):
        grad = grads[:, par * HD : (par + 1) * HD]
        out.append(
            roots[par] * (grad - heads[par] * (lane_sum(grad * heads[par]) * (1.0 / HD)))
        )
    return jnp.concatenate(out, axis=1)


def kernel(
    len_ref, hidden_ref, w_ref, gi_ref, gu_ref, send_ref, pos_ref,
    grad_ref, loss_ref,
    hd, selb, wt, sqx, ps, pr, oute, outq, bufe, bufq, gt, nrm, knb, sqo, sqi, sqm, rsm, q32,
    rcol, rscol, pos_s, hot, hott, sqf_s, sqc_s, gain_s,
    rc_s, kn_s, v_s, qn_s, w_s, o_s, st_r, dsc, dneg_s, dnegt_s, gfol, grow,
    dout_t, dq_t, dk_s, dv_s, drc_s, nbs, dqo, eo, rq, re, sco, sci,
    dqg, gws, gwr, es, er, sdx, sdy,
    xs, xr, ys, yr, ring_s, ring_r, par_s, par_r, a2a_s, a2a_r,
):
    me = lax.axis_index("sect")
    t = lax.axis_index("tp")
    z, y, c = me // 8, (me // 2) % 4, me % 2
    blk = z * 2 + c

    def send(src, dst, ssem, rsem, sect, tp):
        return pltpu.make_async_remote_copy(
            src_ref=src, dst_ref=dst, send_sem=ssem, recv_sem=rsem,
            device_id=(sect, tp), device_id_type=MESH,
        )

    def sect_of(zz, yy, cc):
        return zz * 8 + yy * 2 + cc

    def x_copy(k, src, dst, j):
        peer = (t + j) % NT
        return send(src(peer), dst.at[t], xs.at[k, peer], xr.at[k, t], me, peer)

    def x_from(k, src, dst, j):
        sender = (t + NT - j) % NT
        return send(src(t), dst.at[sender], xs.at[k, sender], xr.at[k, sender], me, sender)

    def y_copy(k, src, dst, j):
        peer = (y + j) % NY
        return send(src(peer), dst.at[y], ys.at[k, peer], yr.at[k, y], sect_of(z, peer, c), t)

    def y_from(k, src, dst, j):
        sender = (y + NY - j) % NY
        return send(
            src(y), dst.at[sender], ys.at[k, sender], yr.at[k, sender], sect_of(z, sender, c), t
        )

    def start3(copy, k, src, dst):
        for j in (2, 1, 3):
            copy(k, src, dst, j).start()

    def wait_in(came, k, src, dst):
        for j in (1, 3, 2):
            came(k, src, dst, j).wait_recv()

    def wait_out(copy, k, src, dst):
        for j in (1, 3, 2):
            copy(k, src, dst, j).wait_send()

    def rows_of(first):
        return pl.ds(pl.multiple_of(first * 16, 16), 16)

    def to_readers(k, out, buf, lanes):
        pltpu.make_async_copy(
            out.at[rows_of(me), lanes], buf.at[y, rows_of(blk), lanes], a2a_r.at[k]
        ).start()

        def step(j, carry):
            peer = (me + j) % NS
            send(
                out.at[rows_of(peer), lanes], buf.at[y, rows_of(blk), lanes],
                a2a_s.at[k], a2a_r.at[k], peer, t,
            ).start()
            return carry

        lax.fori_loop(1, NS, step, 0)

    def to_group(k, out, buf, group, same):
        def copy(j):
            b = (blk + j) % 16
            return send(
                out.at[group, rows_of(b)], buf.at[rows_of(me)],
                a2a_s.at[k], a2a_r.at[k], sect_of(b // 2, group, b % 2), t,
            )

        @pl.when(same)
        def _():
            pltpu.make_async_copy(
                out.at[group, rows_of(blk)], buf.at[rows_of(me)], a2a_r.at[k]
            ).start()

        @pl.when(jnp.logical_not(same))
        def _():
            copy(0).start()

        def step(j, carry):
            copy(j).start()
            return carry

        lax.fori_loop(1, 16, step, 0)

    def to_matched(k, src_of, dst):
        pltpu.make_async_copy(src_of(blk), dst.at[blk], a2a_r.at[k]).start()

        def step(j, carry):
            b = (blk + j) % 16
            send(
                src_of(b), dst.at[blk], a2a_s.at[k], a2a_r.at[k], sect_of(b // 2, y, b % 2), t
            ).start()
            return carry

        lax.fori_loop(1, 16, step, 0)

    def all_in(k, view):
        pltpu.make_async_copy(view, view, a2a_r.at[k]).wait()

    def all_out(k, view):
        pltpu.make_async_copy(view, view, a2a_s.at[k]).wait()

    def ring(stream, step):
        way = 1 if stream < 2 else NZ - 1
        block = (z + (NZ - way) * step) % NZ
        part = wt.at[block, c, pl.ds((stream % 2) * 32, 32)]
        return send(
            part, part, ring_s.at[stream, step], ring_r.at[stream, step],
            sect_of((z + way) % NZ, y, c), t,
        )

    def ring_from(stream, step):
        way = 1 if stream < 2 else NZ - 1
        block = (z + (NZ - way) * (step + 1)) % NZ
        part = wt.at[block, c, pl.ds((stream % 2) * 32, 32)]
        return block, send(
            part, part, ring_s.at[stream, step], ring_r.at[stream, step],
            sect_of((z + way) % NZ, y, c), t,
        )

    def partner(block, core, half):
        part = wt.at[block, core, pl.ds(half * 32, 32)]
        return send(
            part, part, par_s.at[block, half], par_r.at[block, half], sect_of(z, y, 1 - c), t
        )

    def partner_in(block, half):
        partner(block, 1 - c, half).wait_recv()

    def advance(step):
        for stream in (0, 2, 1, 3):
            if step >= RING[stream]:
                continue
            block, came = ring_from(stream, step)
            came.wait_recv()
            if step + 1 < RING[stream]:
                ring(stream, step + 1).start()
            partner(block, c, stream % 2).start()

    barrier = pltpu.get_barrier_semaphore()
    for j in range(1, 8):
        pl.semaphore_signal(
            barrier, inc=1, device_id=(z * 8 + (me + j) % 8, t), device_id_type=MESH
        )
    for j in (1, NZ - 1):
        pl.semaphore_signal(
            barrier, inc=1, device_id=(sect_of((z + j) % NZ, y, c), t), device_id_type=MESH
        )
    for j in range(1, NT):
        pl.semaphore_signal(barrier, inc=1, device_id=(me, (t + j) % NT), device_id_type=MESH)

    hd[y] = hidden_ref[...]
    wt[z, c] = w_ref[...]
    spread = jnp.where((iota((64, 1024), 1) >> 4) == iota((64, 1024), 0), 1.0, 0.0).astype(BF16)
    named = mm(send_ref[...].astype(F32).astype(BF16), spread, 1, 0)
    lane = iota((1, 1024), 1)
    pick = jnp.full((1, 1024), -1.0, F32)
    for s in range(4):
        pick = jnp.where((lane & 3) == s, named[s : s + 1], pick)
    base = (jnp.zeros((1, 1024), jnp.int32) + y * 64).astype(F32)
    selb[y] = jnp.where((((lane >> 2) & 3) == y) & (pick >= 0.0), pick + base, -1.0)
    pl.semaphore_wait(barrier, 7 + 2 + NT - 1)

    own_hd = lambda peer: hd.at[y]
    own_sel = lambda peer: selb.at[y]
    for stream in (0, 2, 1, 3):
        ring(stream, 0).start()
    start3(y_copy, 0, own_hd, hd)
    start3(y_copy, 1, own_sel, selb)
    for half in range(2):
        partner(z, c, half).start()

    slots = pos_ref[...]
    owner = slots >> 2
    pos_s[...] = jnp.full(pos_s.shape, -1, jnp.int32)
    pos_s[:, 0 : HIST + CAND] = (
        ((owner >> 3) << 5) | ((owner & 1) << 4) | (((owner >> 1) & 3) << 2) | (slots & 3)
    )
    for u in range(4):
        for kind in range(2):
            row = pos_s[u : u + 1, kind * HIST : (kind + 1) * HIST]
            picked = one_hot(row, 256)
            first = (4 * kind + u) * HIST
            hot[:, first : first + HIST] = picked.astype(BF16)
            hott[first : first + HIST, :] = jnp.transpose(picked).astype(BF16)

    advance(0)
    advance(1)
    wait_in(y_from, 0, own_hd, hd)
    gi = gi_ref[...].astype(F32).reshape(1, 1024)
    gu = gu_ref[...].astype(F32).reshape(1, 1024)
    lhs = (hd[...].reshape(256, 1024).astype(F32) * (gi * gu)).astype(BF16)

    near = z // 2
    turn = 2 * (z % 2) - 1
    order = (near, (near + turn + NT) % NT, (near - turn + NT) % NT, (near + 2) % NT)

    def ps_copy(peer):
        return send(ps.at[peer], pr.at[t], xs.at[1, peer], xr.at[1, t], me, peer)

    def project(index):
        part = order[index]
        block = wt[pl.ds(2 * part, 2)].reshape(256, 1024)
        ps[part] = mm(lhs, block, 1, 1).astype(BF16)

        @pl.when(part != t)
        def _():
            ps_copy(part).start()

    def partners_in(step):
        if step == 0:
            for half in range(2):
                partner_in(z, half)
        for stream in range(4):
            if step < RING[stream]:
                way = 1 if stream < 2 else NZ - 1
                partner_in((z + (NZ - way) * (step + 1)) % NZ, stream % 2)

    partners_in(0)
    project(0)
    partners_in(1)
    project(1)
    advance(2)
    hidden = hd[...].reshape(256, 1024).astype(F32)
    sqx[t, pl.ds(0, 8), :] = row_sums(hidden * hidden)
    gained = hidden * gi
    sqx[t, pl.ds(8, 8), :] = row_sums(gained * gained)
    own_sqx = lambda peer: sqx.at[t]
    start3(x_copy, 0, own_sqx, sqx)
    partners_in(2)
    project(2)
    wait_in(y_from, 1, own_sel, selb)
    picks = jnp.maximum(jnp.maximum(selb[0], selb[1]), jnp.maximum(selb[2], selb[3]))
    gt[...] = one_hot(picks.astype(jnp.int32), 256).astype(BF16)
    for q in range(4):
        gain_s[q] = jnp.concatenate(
            [gu[:, q * HD : (q + 1) * HD], gu[:, (4 + q) * HD : (5 + q) * HD]], axis=1
        )
    wait_in(x_from, 0, own_sqx, sqx)
    sums = sqx[0] + sqx[1] + sqx[2] + sqx[3]
    r_row = lax.rsqrt(sums[0:1] * (1.0 / D) + EPS)
    sq_item = r_row * r_row * sums[8:9]
    rs_row = lax.rsqrt(sq_item * (1.0 / D) + EPS)
    sq_out = jnp.sum(mm(row_parts(sq_item), gt[...], 1, 0), axis=0, keepdims=True)
    for b in range(NZ):
        sqo[b] = sq_out[:, b * HD : (b + 1) * HD]
    rcol[...] = columns(r_row)
    rscol[...] = columns(rs_row)
    pieces = []
    for par in range(2):
        head = par * 4 + y
        lanes = pl.ds(pl.multiple_of(head * HD, HD), HD)
        piece = hd[:, :, lanes].reshape(256, HD).astype(F32)
        gain = jnp.zeros((1, HD), F32)
        for h in range(8):
            gain = gain + jnp.where(head == h, gi[:, h * HD : (h + 1) * HD], 0.0)
        pieces.append((piece * rcol[...] * gain).astype(BF16))
    oute[...] = mm(gt[...], jnp.concatenate(pieces, axis=1), 0, 0).astype(BF16)
    advance(3)
    partners_in(3)
    project(3)
    both = slice(0, 256)
    to_matched(5, lambda b: sqo.at[b // 2], sqi)
    to_readers(0, oute, bufe, both)
    pr[t] = ps[t]
    for j in (1, 3, 2):
        sender = (t + j) % NT
        send(
            ps.at[t], pr.at[sender], xs.at[1, sender], xr.at[1, sender], me, sender
        ).wait_recv()
    total = (
        pr[0].astype(F32) + pr[1].astype(F32) + pr[2].astype(F32) + pr[3].astype(F32)
    ) * (rcol[...] * rscol[...])[:, 0:1]
    q32[...] = total
    heads, _ = norm_heads(total)
    outq[...] = mm(gt[...], jnp.concatenate(heads, axis=1).astype(BF16), 0, 0).astype(BF16)
    halves = (slice(0, HD), slice(HD, 2 * HD))
    to_readers(1, outq, bufq, halves[0])
    to_readers(4, outq, bufq, halves[1])

    off = (me % 8) * 16
    blocks = jnp.where((iota((256, 16), 0) >> 4) == iota((256, 16), 1), 1.0, 0.0).astype(BF16)
    in_lane = iota((256, HD), 1) == off + (iota((256, HD), 0) & 15)
    all_in(5, sqi)
    came = jnp.concatenate([sqi[b] for b in range(16)], axis=0)
    high, mid, low = split3(came)
    wide = mm(blocks, high, 1, 0) + mm(blocks, mid, 1, 0) + mm(blocks, low, 1, 0)
    sqm[...] = jnp.broadcast_to(lane_sum(jnp.where(in_lane, wide, 0.0)), (256, HD))
    rsm[...] = lax.rsqrt(sqm[...] * (1.0 / D) + EPS)
    sqf_s[...] = jnp.broadcast_to(
        lane_sum(mm(hott[0:512], lane_parts(sqm[...]), 1, 0)), (512, HIST)
    )
    sqc = jnp.sum(mm(lane_parts(sqm[...]), hot[:, 512:1024], 0, 0), axis=0, keepdims=True)
    for u in range(4):
        sqc_s[u] = sqc[:, u * HIST : (u + 1) * HIST]
    twice = lambda values: jnp.concatenate([values, values], axis=1)
    all_in(0, bufe)
    for q in range(4):
        low = (bufe[q].astype(F32) * twice(rsm[...]) * gain_s[q]).astype(BF16)
        nrm[q] = low
        heads, _ = norm_heads(low.astype(F32))
        knb[q] = jnp.concatenate(heads, axis=1).astype(BF16)
    for q in range(4):
        kn_s[q] = mm(hott[0:512], knb[q], 1, 0).astype(BF16)
        v_s[q] = mm(hott[0:512], nrm[q], 1, 0).astype(BF16)
    for q in range(4):
        rc_s[q] = mm(hott[...], bufe[q], 1, 0).astype(BF16)

    scale = HD ** (-0.5)
    row_id = iota((HIST, HIST), 0)
    col_id = iota((HIST, HIST), 1)

    def follow_of(rows):
        moved = pltpu.roll(rows, HIST - 1, 0)
        return jnp.where(iota(rows.shape, 0) < HIST - 1, moved, 0.0)

    def st_copy(u, j):
        peer = (t + j) % NT
        return send(st_r.at[t, u], st_r.at[t, u], xs.at[6 + u, peer], xr.at[6 + u, t], me, peer)

    def st_from(u, j):
        sender = (t + NT - j) % NT
        return send(
            st_r.at[t, u], st_r.at[sender, u], xs.at[6 + u, sender], xr.at[6 + u, sender],
            me, sender,
        )

    def user_rows(u):
        return pl.ds(pl.multiple_of(u * HIST, HIST), HIST)

    def attend(u, par):
        span = user_rows(u)
        lanes = halves[par]
        mask = jnp.where((col_id <= row_id) & (col_id < len_ref[u]), 1.0, 0.0)
        for q in range(4):
            weights = jnp.exp(mm(qn_s[q, span, lanes], kn_s[q, span, lanes], 1, 1) * scale) * mask
            weights = (weights * (1.0 / lane_sum(weights))).astype(BF16)
            w_s[2 * q + par, span] = weights
            o_s[q, span, lanes] = rc_s[q, span, lanes].astype(F32) + mm(
                weights, v_s[q, span, lanes], 1, 0
            )

    def first_half(u, carry):
        attend(u, 0)
        return carry

    def second_half(u, carry):
        attend(u, 1)
        span = user_rows(u)
        cspan = user_rows(u + 4)
        own = jnp.zeros((HIST, 1), F32)
        hit = jnp.zeros((HIST, 1), F32)
        neg = jnp.zeros((HIST, HIST), F32)
        for q in range(4):
            out = o_s[q, span]
            own = own + lane_sum(out * out)
            hit = hit + lane_sum(out * follow_of(rc_s[q, span].astype(F32)))
            high = out.astype(BF16)
            low = (out - high.astype(F32)).astype(BF16)
            cands = rc_s[q, cspan]
            neg = neg + mm(high, cands, 1, 1) + mm(low, cands, 1, 1)
        stats = neg + jnp.where(col_id == CAND, own, 0.0) + jnp.where(col_id == CAND + 1, hit, 0.0)
        st_r[t, u] = stats.astype(BF16)
        for j in (2, 1, 3):
            st_copy(u, j).start()
        return carry

    for par, step in ((0, first_half), (1, second_half)):
        all_in(1 if par == 0 else 4, outq.at[:, halves[0]])
        for q in range(4):
            qn_s[q, :, halves[par]] = mm(hott[0:512], bufq[q, :, halves[par]], 1, 0).astype(BF16)
        lax.fori_loop(0, 4, step, 0, unroll=2)

    def losses(u, carry):
        for j in (1, 3, 2):
            st_from(u, j).wait_recv()
        stats = (
            st_r[0, u].astype(F32) + st_r[1, u].astype(F32)
            + st_r[2, u].astype(F32) + st_r[3, u].astype(F32)
        )
        is_cand = col_id < CAND
        neg = jnp.where(is_cand, stats, 0.0)
        own = lane_sum(jnp.where(col_id == CAND, stats, 0.0))
        hit = lane_sum(jnp.where(col_id == CAND + 1, stats, 0.0))
        sq_follow = pltpu.roll(sqf_s[user_rows(u)], HIST - 1, 0)[:, 0:1]
        rn = lax.rsqrt(own + EPS)
        rf = lax.rsqrt(sq_follow + EPS)
        rc = lax.rsqrt(sqc_s[u] + EPS)
        tl = SOFT * hit * rn * rf
        nl = SOFT * neg * rn * rc
        en = jnp.where(is_cand, jnp.exp(nl), 0.0)
        et = jnp.exp(tl)
        whole = et + lane_sum(en)
        span = len_ref[u] - 1
        over = 1.0 / (jnp.full((HIST, 1), 0, jnp.int32) + span).astype(F32)
        valid = iota((HIST, 1), 0) < span
        terms = jnp.where(valid, (jnp.log(whole) - tl) * over, 0.0)
        loss_ref[u] = jnp.broadcast_to(jnp.sum(terms, axis=0, keepdims=True), (1, HIST))
        g = jnp.where(valid, float(D) * over, 0.0)
        dtl = g * (et / whole - 1.0)
        dnl = (g / whole) * en
        dsc[u, 0] = jnp.broadcast_to(
            -rn * rn * (dtl * tl + lane_sum(dnl * nl)), (HIST, HIST)
        )
        dsc[u, 1] = jnp.broadcast_to(dtl * (SOFT * rn * rf), (HIST, HIST))
        dneg = dnl * (SOFT * rn * rc)
        dneg_s[u] = dneg.astype(BF16)
        dnegt_s[u] = jnp.transpose(dneg).astype(BF16)
        dsqf = jnp.broadcast_to(-0.5 * dtl * tl * rf * rf, (HIST, HIST))
        gfol[user_rows(u)] = pltpu.roll(dsqf, 1, 0)
        grow[u] = -0.5 * rc * rc * jnp.sum(dnl * nl, axis=0, keepdims=True)
        return carry

    lax.fori_loop(0, 4, losses, 0)

    def backward_quarter(i, carry):
        q = (y + 1 + i) % 4
        for u in range(4):
            span = slice(u * HIST, (u + 1) * HIST)
            cspan = slice((4 + u) * HIST, (5 + u) * HIST)
            dhit = twice(dsc[u, 1])
            out = o_s[q, span]
            rows = rc_s[q, span].astype(F32)
            dout = (
                twice(dsc[u, 0]) * out
                + dhit * follow_of(rows)
                + mm(dneg_s[u], rc_s[q, cspan], 1, 0)
            )
            dout_t[span] = dout.astype(BF16)
            drc_s[q, span] = (dout + pltpu.roll(dhit * out, 1, 0)).astype(BF16)
            drc_s[q, cspan] = mm(dnegt_s[u], out.astype(BF16), 1, 0).astype(BF16)
        for u in range(4):
            span = slice(u * HIST, (u + 1) * HIST)
            for par in range(2):
                lanes = halves[par]
                grad = dout_t[span, lanes]
                weights = w_s[2 * q + par, span]
                wide = weights.astype(F32)
                dw = mm(grad, v_s[q, span, lanes], 1, 1)
                ds = (wide * (dw - lane_sum(dw * wide)) * scale).astype(BF16)
                dq_t[span, lanes] = mm(ds, kn_s[q, span, lanes], 1, 0).astype(BF16)
                dk_s[q, span, lanes] = mm(ds, qn_s[q, span, lanes], 0, 0).astype(BF16)
                dv_s[q, span, lanes] = mm(weights, grad, 0, 0).astype(BF16)
        dqo[q] = mm(hot[:, 0:512], dq_t[...], 1, 0).astype(BF16)
        to_group(2, dqo, rq, q, i == 3)
        return carry

    lax.fori_loop(0, 4, backward_quarter, 0)

    nbs[...] = jnp.zeros(nbs.shape, F32)

    def return_quarter(i, carry):
        q = (y + 1 + i) % 4
        dk = mm(hot[:, 0:512], dk_s[q], 1, 0)
        dn = mm(hot[:, 0:512], dv_s[q], 1, 0) + norm_heads_back(nrm[q].astype(F32), dk)
        dn = dn * gain_s[q]
        nbs[...] += jnp.broadcast_to(lane_sum(dn * bufe[q].astype(F32)), (256, HD))
        eo[q] = (mm(hot[...], drc_s[q], 1, 0) + dn * twice(rsm[...])).astype(BF16)
        to_group(3, eo, re, q, i == 3)
        return carry

    lax.fori_loop(0, 4, return_quarter, 0)
    gsq = lane_sum(mm(hot[:, 0:512], lane_parts(gfol[...]), 1, 0)) + lane_sum(
        mm(
            hot[:, 512:1024],
            row_parts(jnp.concatenate([grow[u] for u in range(4)], axis=1)), 1, 1,
        )
    )
    placed = []
    for values in (jnp.broadcast_to(gsq, (256, HD)), nbs[...]):
        high, mid, low = split3(jnp.where(in_lane, values, 0.0))
        placed.append(mm(blocks, high, 0, 0) + mm(blocks, mid, 0, 0) + mm(blocks, low, 0, 0))
    for b in range(16):
        sco[b] = jnp.concatenate([part[b : b + 1] for part in placed], axis=1)
    to_matched(6, lambda b: sco.at[b], sci)

    all_in(2, rq)
    dq_item = norm_heads_back(q32[...], mm(gt[...], rq[...], 1, 0)).astype(BF16)
    dqg[t] = dq_item
    own_dqg = lambda peer: dqg.at[t]
    start3(x_copy, 4, own_dqg, dqg)
    all_in(6, sci)
    pairs = [sci[2 * b] + sci[2 * b + 1] for b in range(NZ)]
    item_terms = []
    for lanes in (slice(0, HD), slice(HD, 2 * HD)):
        row = jnp.concatenate([pair[:, lanes] for pair in pairs], axis=1)
        item_terms.append(jnp.sum(mm(row_parts(row), gt[...], 1, 1), axis=0, keepdims=True))
    sdy[y, pl.ds(8, 8), :] = jnp.broadcast_to(item_terms[0], (8, 256))
    sdx[t] = row_sums(dq_item.astype(F32) * q32[...]) + rs_row * item_terms[1]
    own_sdx = lambda peer: sdx.at[t]
    start3(x_copy, 5, own_sdx, sdx)
    wait_in(x_from, 4, own_dqg, dqg)
    gws_of = lambda peer: gws.at[peer]
    acc = jnp.zeros((256, 1024), F32)
    for tt in range(NT):
        acc = acc + mm(dqg[tt], wt[2 * tt : 2 * tt + 2].reshape(256, 1024), 1, 0)
    gws[...] = acc.astype(BF16).reshape(4, 64, 1024)
    start3(y_copy, 2, gws_of, gwr)
    gwr[y] = gws[y]
    wait_in(x_from, 5, own_sdx, sdx)
    sdy[y, pl.ds(0, 8), :] = sdx[0] + sdx[1] + sdx[2] + sdx[3]
    own_sdy = lambda peer: sdy.at[y]
    start3(y_copy, 4, own_sdy, sdy)
    all_in(3, re)
    es[...] = mm(gt[...], re[...], 1, 0).astype(BF16).reshape(4, 64, 256)
    es_of = lambda peer: es.at[peer]
    start3(y_copy, 3, es_of, er)
    er[y] = es[y]

    mine = pl.ds(pl.multiple_of(y * 64, 64), 64)
    emb = (hidden_ref[...].astype(F32) * rcol[mine, 0:1] * gi).astype(BF16).astype(F32)
    rs_own = rscol[mine, 0:1]
    wait_in(y_from, 4, own_sdy, sdy)
    last = sdy[0] + sdy[1] + sdy[2] + sdy[3]
    sqm[...] = columns(2.0 * last[8:9] - (1.0 / D) * rs_row * rs_row * last[0:1])
    coef = sqm[mine, 0:1]
    direct = emb * coef
    wait_in(y_from, 2, gws_of, gwr)
    gw = (
        gwr[0].astype(F32) + gwr[1].astype(F32) + gwr[2].astype(F32) + gwr[3].astype(F32)
    ) * gu * rs_own + direct
    wait_in(y_from, 3, es_of, er)
    for h in range(8):
        lanes = slice(h * HD, (h + 1) * HD)
        par, q = h // 4, h % 4
        grad_ref[:, lanes] = er[q, :, halves[par]].astype(F32) + gw[:, lanes]

    for k, src, dst in (
        (0, own_hd, hd), (1, own_sel, selb), (2, gws_of, gwr), (3, es_of, er), (4, own_sdy, sdy)
    ):
        wait_out(y_copy, k, src, dst)
    for k, src, dst in (
        (0, own_sqx, sqx), (4, own_dqg, dqg), (5, own_sdx, sdx)
    ):
        wait_out(x_copy, k, src, dst)
    for j in (1, 3, 2):
        ps_copy((t + j) % NT).wait_send()
    for u in range(4):
        for j in (1, 3, 2):
            st_copy(u, j).wait_send()
    for stream in range(4):
        for step in range(RING[stream]):
            ring(stream, step).wait_send()
    for b in range(NZ):
        for half in range(2):
            partner(b, c, half).wait_send()
    most = pl.ds(0, (NS - 1) * 16)
    all_out(0, oute.at[most])
    all_out(1, outq.at[most, halves[0]])
    all_out(4, outq.at[most, halves[1]])
    all_out(2, rq.at[most])
    all_out(3, re.at[most])
    all_out(5, sqi.at[pl.ds(0, 15)])
    all_out(6, sci.at[pl.ds(0, 15)])


def local(item_hidden, item_gain, send_item, pos_slot, hist_len, user_gain, query_weight):
    vmem = pltpu.VMEM
    dma = pltpu.SemaphoreType.DMA
    quarter = lambda kind: vmem((4, 256, 256), kind)
    grad, loss = pl.pallas_call(
        kernel,
        out_shape=(
            jax.ShapeDtypeStruct((64, 1024), F32),
            jax.ShapeDtypeStruct((4, 1, HIST), F32),
        ),
        in_specs=[pl.BlockSpec(memory_space=pltpu.SMEM)]
        + [pl.BlockSpec(memory_space=pltpu.VMEM)] * 6,
        out_specs=(
            pl.BlockSpec(memory_space=pltpu.VMEM),
            pl.BlockSpec(memory_space=pltpu.VMEM),
        ),
        scratch_shapes=[
            vmem((4, 64, 1024), BF16),
            vmem((4, 1, 1024), F32),
            vmem((8, 2, 64, 1024), BF16),
            vmem((4, 16, 256), F32),
            quarter(BF16),
            quarter(BF16),
            vmem((1024, 256), BF16),
            vmem((1024, 256), BF16),
            quarter(BF16),
            quarter(BF16),
            vmem((256, 1024), BF16),
            quarter(BF16),
            quarter(BF16),
            vmem((8, 1, HIST), F32),
            vmem((16, 1, HIST), F32),
            vmem((256, HIST), F32),
            vmem((256, HIST), F32),
            vmem((256, 256), F32),
            vmem((256, HIST), F32),
            vmem((256, HIST), F32),
            vmem((4, 2 * HIST), jnp.int32),
            vmem((256, 1024), BF16),
            vmem((1024, 256), BF16),
            vmem((512, HIST), F32),
            vmem((4, 1, HIST), F32),
            vmem((4, 1, 256), F32),
            vmem((4, 1024, 256), BF16),
            vmem((4, 512, 256), BF16),
            vmem((4, 512, 256), BF16),
            vmem((4, 512, 256), BF16),
            vmem((8, 512, HIST), BF16),
            vmem((4, 512, 256), F32),
            vmem((4, 4, HIST, HIST), BF16),
            vmem((4, 2, HIST, HIST), F32),
            vmem((4, HIST, HIST), BF16),
            vmem((4, HIST, HIST), BF16),
            vmem((512, HIST), F32),
            vmem((4, 1, HIST), F32),
            vmem((512, 256), BF16),
            vmem((512, 256), BF16),
            vmem((4, 512, 256), BF16),
            vmem((4, 512, 256), BF16),
            vmem((4, 1024, 256), BF16),
            vmem((256, HIST), F32),
            quarter(BF16),
            quarter(BF16),
            vmem((1024, 256), BF16),
            vmem((1024, 256), BF16),
            vmem((16, 1, 256), F32),
            vmem((16, 1, 256), F32),
            quarter(BF16),
            vmem((4, 64, 1024), BF16),
            vmem((4, 64, 1024), BF16),
            vmem((4, 64, 256), BF16),
            vmem((4, 64, 256), BF16),
            vmem((4, 8, 256), F32),
            vmem((4, 16, 256), F32),
            dma((10, 4)),
            dma((10, 4)),
            dma((5, 4)),
            dma((5, 4)),
            dma((4, 4)),
            dma((4, 4)),
            dma((8, 2)),
            dma((8, 2)),
            dma((7,)),
            dma((7,)),
        ],
        compiler_params=pltpu.CompilerParams(
            collective_id=0, has_side_effects=True, vmem_limit_bytes=60 * 1024 * 1024
        ),
    )(
        hist_len, item_hidden, query_weight.T, item_gain, user_gain, send_item[0].T, pos_slot
    )
    return (grad, loss[:, 0, 0])


def solution(mesh):
    placed = (
        P("sect", "tp"),
        P("tp"),
        P("sect", None, None),
        P("sect", None),
        P("sect"),
        P("tp"),
        P("tp", "sect"),
    )
    return jax.shard_map(
        local, mesh=mesh, in_specs=placed, out_specs=(P("sect", "tp"), P("sect")), check_vma=False
    )
```

```python
import jax
import jax.numpy as jnp
from jax import lax
from jax.experimental import pallas as pl
from jax.experimental.pallas import tpu as pltpu
from jax.sharding import PartitionSpec as P

D = 4096
HD = 128
HIST = 128
CAND = 64
NZ, NY, NT = 8, 4, 4
NS = 64
EPS = 1e-06
SOFT = 20.0
F32, BF16 = jnp.float32, jnp.bfloat16
MESH = pl.DeviceIdType.MESH
RING = (4, 3, 3, 4)


def mm(a, b, ca, cb, precision=None):
    return lax.dot_general(
        a, b, (((ca,), (cb,)), ((), ())), preferred_element_type=F32, precision=precision
    )


def split3(values):
    high = values.astype(BF16)
    rest = values - high.astype(F32)
    mid = rest.astype(BF16)
    return high, mid, (rest - mid.astype(F32)).astype(BF16)


def row_parts(row):
    parts = split3(jnp.broadcast_to(row, (8, row.shape[1])))
    index = iota((8, row.shape[1]), 0)
    out = jnp.where(index == 0, parts[0].astype(F32), 0.0)
    out = jnp.where(index == 1, parts[1].astype(F32), out)
    return jnp.where(index == 2, parts[2].astype(F32), out).astype(BF16)


def lane_parts(values):
    parts = split3(values)
    index = iota(values.shape, 1)
    out = jnp.where(index == 0, parts[0].astype(F32), 0.0)
    out = jnp.where(index == 1, parts[1].astype(F32), out)
    return jnp.where(index == 2, parts[2].astype(F32), out).astype(BF16)


def columns(row):
    return mm(row_parts(row), jnp.ones((8, 128), BF16), 0, 0)


def row_sums(values):
    ones = jnp.ones((8, values.shape[1]), BF16)
    high, mid, low = split3(values)
    return mm(ones, high, 1, 1) + mm(ones, mid, 1, 1) + mm(ones, low, 1, 1)


def lane_sum(values):
    return jnp.sum(values, axis=1, keepdims=True)


def iota(shape, dim):
    return lax.broadcasted_iota(jnp.int32, shape, dim)


def one_hot(row, count):
    return jnp.where(iota((count, row.shape[1]), 0) == row, 1.0, 0.0)


def norm_heads(values):
    heads, roots = [], []
    for par in range(2):
        part = values[:, par * HD : (par + 1) * HD]
        root = lax.rsqrt(lane_sum(part * part) * (1.0 / HD) + EPS)
        heads.append(part * root)
        roots.append(root)
    return heads, roots


def norm_heads_back(values, grads):
    heads, roots = norm_heads(values)
    out = []
    for par in range(2):
        grad = grads[:, par * HD : (par + 1) * HD]
        out.append(
            roots[par] * (grad - heads[par] * (lane_sum(grad * heads[par]) * (1.0 / HD)))
        )
    return jnp.concatenate(out, axis=1)


def kernel(
    len_ref, hidden_ref, w_ref, gi_ref, gu_ref, send_ref, pos_ref,
    grad_ref, loss_ref,
    hd, selb, wt, sqx, sqy, ps, pr, oute, outq, bufe, bufq, gt, nrm, knb, sqo, sqi, sqm, rsm, q32,
    rcol, rscol, pos_s, hot, hott, sqf_s, sqc_s, gain_s,
    rc_s, kn_s, v_s, qn_s, w_s, wt_s, p_t, ds_t, o_s, st_r, dsc, dneg_s, dnegt_s, gfol, grow,
    dout_t, dq_t, dk_s, dv_s, drc_s, nbs, dqo, eo, rq, re, sco, sci,
    dqg, gws, gwr, es, er, sdx, sdy,
    xs, xr, ys, yr, ring_s, ring_r, par_s, par_r, a2a_s, a2a_r, hello,
):
    me = lax.axis_index("sect")
    t = lax.axis_index("tp")
    z, y, c = me // 8, (me // 2) % 4, me % 2
    blk = z * 2 + c

    def send(src, dst, ssem, rsem, sect, tp):
        return pltpu.make_async_remote_copy(
            src_ref=src, dst_ref=dst, send_sem=ssem, recv_sem=rsem,
            device_id=(sect, tp), device_id_type=MESH,
        )

    def sect_of(zz, yy, cc):
        return zz * 8 + yy * 2 + cc

    def x_copy(k, src, dst, j):
        peer = (t + j) % NT
        return send(src(peer), dst.at[t], xs.at[k, peer], xr.at[k, t], me, peer)

    def x_from(k, src, dst, j):
        sender = (t + NT - j) % NT
        return send(src(t), dst.at[sender], xs.at[k, sender], xr.at[k, sender], me, sender)

    def y_copy(k, src, dst, j):
        peer = (y + j) % NY
        return send(src(peer), dst.at[y], ys.at[k, peer], yr.at[k, y], sect_of(z, peer, c), t)

    def y_from(k, src, dst, j):
        sender = (y + NY - j) % NY
        return send(
            src(y), dst.at[sender], ys.at[k, sender], yr.at[k, sender], sect_of(z, sender, c), t
        )

    def start3(copy, k, src, dst):
        for j in (2, 1, 3):
            copy(k, src, dst, j).start()

    def wait_in(came, k, src, dst):
        for j in (1, 3, 2):
            came(k, src, dst, j).wait_recv()

    def wait_out(copy, k, src, dst):
        for j in (1, 3, 2):
            copy(k, src, dst, j).wait_send()

    def rows_of(first):
        return pl.ds(pl.multiple_of(first * 16, 16), 16)

    def to_readers(k, out, buf, lanes):
        pltpu.make_async_copy(
            out.at[rows_of(me), lanes], buf.at[y, rows_of(blk), lanes], a2a_r.at[k]
        ).start()

        def step(j, carry):
            peer = (me + j) % NS
            send(
                out.at[rows_of(peer), lanes], buf.at[y, rows_of(blk), lanes],
                a2a_s.at[k], a2a_r.at[k], peer, t,
            ).start()
            return carry

        lax.fori_loop(1, NS, step, 0)

    def to_group(k, out, buf, group, same):
        def copy(j):
            b = (blk + j) % 16
            return send(
                out.at[group, rows_of(b)], buf.at[rows_of(me)],
                a2a_s.at[k], a2a_r.at[k], sect_of(b // 2, group, b % 2), t,
            )

        @pl.when(same)
        def _():
            pltpu.make_async_copy(
                out.at[group, rows_of(blk)], buf.at[rows_of(me)], a2a_r.at[k]
            ).start()

        @pl.when(jnp.logical_not(same))
        def _():
            copy(0).start()

        def step(j, carry):
            copy(j).start()
            return carry

        lax.fori_loop(1, 16, step, 0)

    def to_matched(k, src_of, dst):
        pltpu.make_async_copy(src_of(blk), dst.at[blk], a2a_r.at[k]).start()

        def step(j, carry):
            b = (blk + j) % 16
            send(
                src_of(b), dst.at[blk], a2a_s.at[k], a2a_r.at[k], sect_of(b // 2, y, b % 2), t
            ).start()
            return carry

        lax.fori_loop(1, 16, step, 0)

    def all_in(k, view):
        pltpu.make_async_copy(view, view, a2a_r.at[k]).wait()

    def all_out(k, view):
        pltpu.make_async_copy(view, view, a2a_s.at[k]).wait()

    def ring(stream, step):
        way = 1 if stream < 2 else NZ - 1
        block = (z + (NZ - way) * step) % NZ
        part = wt.at[block, c, pl.ds((stream % 2) * 32, 32)]
        return send(
            part, part, ring_s.at[stream, step], ring_r.at[stream, step],
            sect_of((z + way) % NZ, y, c), t,
        )

    def ring_from(stream, step):
        way = 1 if stream < 2 else NZ - 1
        block = (z + (NZ - way) * (step + 1)) % NZ
        part = wt.at[block, c, pl.ds((stream % 2) * 32, 32)]
        return block, send(
            part, part, ring_s.at[stream, step], ring_r.at[stream, step],
            sect_of((z + way) % NZ, y, c), t,
        )

    def partner(block, core, half):
        part = wt.at[block, core, pl.ds(half * 32, 32)]
        return send(
            part, part, par_s.at[block, half], par_r.at[block, half], sect_of(z, y, 1 - c), t
        )

    def partner_in(block, half):
        partner(block, 1 - c, half).wait_recv()

    def advance(step):
        for stream in (0, 2, 1, 3):
            if step >= RING[stream]:
                continue
            block, came = ring_from(stream, step)
            came.wait_recv()
            if step + 1 < RING[stream]:
                ring(stream, step + 1).start()
            partner(block, c, stream % 2).start()

    barrier = pltpu.get_barrier_semaphore()
    for j in range(1, 8):
        pl.semaphore_signal(
            barrier, inc=1, device_id=(z * 8 + (me + j) % 8, t), device_id_type=MESH
        )
    for j in (1, NZ - 1):
        pl.semaphore_signal(
            barrier, inc=1, device_id=(sect_of((z + j) % NZ, y, c), t), device_id_type=MESH
        )
    for j in range(1, NT):
        pl.semaphore_signal(barrier, inc=1, device_id=(me, (t + j) % NT), device_id_type=MESH)

    hd[y] = hidden_ref[...]
    sqx[t] = jnp.zeros((16, HIST), F32)
    wt[z, c] = w_ref[...]
    spread = jnp.where((iota((64, 1024), 1) >> 4) == iota((64, 1024), 0), 1.0, 0.0).astype(BF16)
    named = mm(send_ref[...].astype(F32).astype(BF16), spread, 1, 0)
    lane = iota((1, 1024), 1)
    pick = jnp.full((1, 1024), -1.0, F32)
    for s in range(4):
        pick = jnp.where((lane & 3) == s, named[s : s + 1], pick)
    base = (jnp.zeros((1, 1024), jnp.int32) + y * 64).astype(F32)
    selb[y] = jnp.where((((lane >> 2) & 3) == y) & (pick >= 0.0), pick + base, -1.0)
    pl.semaphore_wait(barrier, 7 + 2 + NT - 1)

    def greet(step):
        for way in range(2):
            if step < 4 - way:
                peer = (z + 1) % NZ if way == 0 else (z + NZ - 1) % NZ
                pl.semaphore_signal(
                    hello.at[way, step], inc=1, device_id=(sect_of(peer, y, c), t),
                    device_id_type=MESH,
                )

    def relay(step):
        for way in range(2):
            if step < 4 - way:
                pl.semaphore_wait(hello.at[way, step], 1)
        greet(step + 1)

    greet(0)
    own_hd = lambda peer: hd.at[y]
    own_sel = lambda peer: selb.at[y]
    for stream in (0, 2, 1, 3):
        ring(stream, 0).start()
    start3(y_copy, 0, own_hd, hd)
    start3(y_copy, 1, own_sel, selb)
    for half in range(2):
        partner(z, c, half).start()

    gi = gi_ref[...].astype(F32).reshape(1, 1024)
    gu = gu_ref[...].astype(F32).reshape(1, 1024)
    hidden = hidden_ref[...].astype(F32)
    gained = hidden * gi
    sqx[t, pl.ds(0, 8), 0:64] = row_sums(hidden * hidden)
    sqx[t, pl.ds(8, 8), 0:64] = row_sums(gained * gained)
    own_sqx = lambda peer: sqx.at[t]
    start3(x_copy, 0, own_sqx, sqx)

    slots = pos_ref[...]
    owner = slots >> 2
    pos_s[...] = jnp.full(pos_s.shape, -1, jnp.int32)
    pos_s[:, 0 : HIST + CAND] = (
        ((owner >> 3) << 5) | ((owner & 1) << 4) | (((owner >> 1) & 3) << 2) | (slots & 3)
    )
    for u in range(4):
        for kind in range(2):
            row = pos_s[u : u + 1, kind * HIST : (kind + 1) * HIST]
            picked = one_hot(row, 256)
            first = (4 * kind + u) * HIST
            hot[:, first : first + HIST] = picked.astype(BF16)
            hott[first : first + HIST, :] = jnp.transpose(picked).astype(BF16)

    advance(0)
    relay(0)
    wait_in(x_from, 0, own_sqx, sqx)
    sums = sqx[0] + sqx[1] + sqx[2] + sqx[3]
    r_row = lax.rsqrt(sums[0:1] * (1.0 / D) + EPS)
    sq_item = r_row * r_row * sums[8:9]
    rs_row = lax.rsqrt(sq_item * (1.0 / D) + EPS)
    sqy[y] = jnp.concatenate([r_row, rs_row, sq_item] + [r_row] * 5, axis=0)
    own_sqy = lambda peer: sqy.at[y]
    start3(y_copy, 5, own_sqy, sqy)
    relay(1)
    advance(1)
    relay(2)
    wait_in(y_from, 0, own_hd, hd)
    lhs = (hd[...].reshape(256, 1024).astype(F32) * (gi * gu)).astype(BF16)

    near = z // 2
    turn = 2 * (z % 2) - 1
    order = (near, (near + turn + NT) % NT, (near - turn + NT) % NT, (near + 2) % NT)

    def ps_copy(peer):
        return send(ps.at[peer], pr.at[t], xs.at[1, peer], xr.at[1, t], me, peer)

    def project(index):
        part = order[index]
        block = wt[pl.ds(2 * part, 2)].reshape(256, 1024)
        ps[part] = mm(lhs, block, 1, 1).astype(BF16)

        @pl.when(part != t)
        def _():
            ps_copy(part).start()

    def partners_in(step):
        if step == 0:
            for half in range(2):
                partner_in(z, half)
        for stream in range(4):
            if step < RING[stream]:
                way = 1 if stream < 2 else NZ - 1
                partner_in((z + (NZ - way) * (step + 1)) % NZ, stream % 2)

    partners_in(0)
    project(0)
    wait_in(y_from, 1, own_sel, selb)
    picks = jnp.maximum(jnp.maximum(selb[0], selb[1]), jnp.maximum(selb[2], selb[3]))
    gt[...] = one_hot(picks.astype(jnp.int32), 256).astype(BF16)
    wait_in(y_from, 5, own_sqy, sqy)
    rcol[...] = jnp.concatenate([columns(sqy[b, 0:1])[0:64] for b in range(4)], axis=0)
    rscol[...] = jnp.concatenate([columns(sqy[b, 1:2])[0:64] for b in range(4)], axis=0)
    sq_out = jnp.zeros((8, 1024), F32)
    for b in range(4):
        sq_out = sq_out + mm(
            row_parts(sqy[b, 2:3])[:, 0:64], gt[b * 64 : (b + 1) * 64, :], 1, 0
        )
    sq_out = jnp.sum(sq_out, axis=0, keepdims=True)
    for b in range(NZ):
        sqo[b] = sq_out[:, b * HD : (b + 1) * HD]
    pieces = []
    for par in range(2):
        head = par * 4 + y
        lanes = pl.ds(pl.multiple_of(head * HD, HD), HD)
        piece = hd[:, :, lanes].reshape(256, HD).astype(F32)
        gain = jnp.zeros((1, HD), F32)
        for h in range(8):
            gain = gain + jnp.where(head == h, gi[:, h * HD : (h + 1) * HD], 0.0)
        pieces.append((piece * rcol[...] * gain).astype(BF16))
    oute[...] = mm(gt[...], jnp.concatenate(pieces, axis=1), 0, 0).astype(BF16)
    partners_in(1)
    project(1)
    advance(2)
    relay(3)
    both = slice(0, 256)
    to_matched(5, lambda b: sqo.at[b // 2], sqi)
    to_readers(0, oute, bufe, both)
    partners_in(2)
    project(2)
    advance(3)
    partners_in(3)
    project(3)
    for q in range(4):
        gain_s[q] = jnp.concatenate(
            [gu[:, q * HD : (q + 1) * HD], gu[:, (4 + q) * HD : (5 + q) * HD]], axis=1
        )
    pr[t] = ps[t]
    for j in (1, 3, 2):
        sender = (t + j) % NT
        send(
            ps.at[t], pr.at[sender], xs.at[1, sender], xr.at[1, sender], me, sender
        ).wait_recv()
    total = (
        pr[0].astype(F32) + pr[1].astype(F32) + pr[2].astype(F32) + pr[3].astype(F32)
    ) * (rcol[...] * rscol[...])[:, 0:1]
    q32[...] = total
    heads, _ = norm_heads(total)
    outq[...] = mm(gt[...], jnp.concatenate(heads, axis=1).astype(BF16), 0, 0).astype(BF16)
    halves = (slice(0, HD), slice(HD, 2 * HD))
    to_readers(1, outq, bufq, halves[0])
    to_readers(4, outq, bufq, halves[1])

    off = (me % 8) * 16
    blocks = jnp.where((iota((256, 16), 0) >> 4) == iota((256, 16), 1), 1.0, 0.0).astype(BF16)
    in_lane = iota((256, HD), 1) == off + (iota((256, HD), 0) & 15)
    all_in(5, sqi)
    came = jnp.concatenate([sqi[b] for b in range(16)], axis=0)
    high, mid, low = split3(came)
    wide = mm(blocks, high, 1, 0) + mm(blocks, mid, 1, 0) + mm(blocks, low, 1, 0)
    sqm[...] = jnp.broadcast_to(lane_sum(jnp.where(in_lane, wide, 0.0)), (256, HD))
    rsm[...] = lax.rsqrt(sqm[...] * (1.0 / D) + EPS)
    sqf_s[...] = jnp.broadcast_to(
        lane_sum(mm(hott[0:512], lane_parts(sqm[...]), 1, 0)), (512, HIST)
    )
    sqc = jnp.sum(mm(lane_parts(sqm[...]), hot[:, 512:1024], 0, 0), axis=0, keepdims=True)
    for u in range(4):
        sqc_s[u] = sqc[:, u * HIST : (u + 1) * HIST]
    twice = lambda values: jnp.concatenate([values, values], axis=1)
    all_in(0, bufe)
    for q in range(4):
        low = (bufe[q].astype(F32) * twice(rsm[...]) * gain_s[q]).astype(BF16)
        nrm[q] = low
        heads, _ = norm_heads(low.astype(F32))
        knb[q] = jnp.concatenate(heads, axis=1).astype(BF16)
    for q in range(4):
        kn_s[q] = mm(hott[0:512], knb[q], 1, 0).astype(BF16)
        v_s[q] = mm(hott[0:512], nrm[q], 1, 0).astype(BF16)
    for q in range(4):
        rc_s[q] = mm(hott[...], bufe[q], 1, 0).astype(BF16)

    scale = HD ** (-0.5)
    row_id = iota((HIST, HIST), 0)
    col_id = iota((HIST, HIST), 1)

    def follow_of(rows):
        moved = pltpu.roll(rows, HIST - 1, 0)
        return jnp.where(iota(rows.shape, 0) < HIST - 1, moved, 0.0)

    def st_copy(u, j):
        peer = (t + j) % NT
        return send(st_r.at[t, u], st_r.at[t, u], xs.at[6 + u, peer], xr.at[6 + u, t], me, peer)

    def st_from(u, j):
        sender = (t + NT - j) % NT
        return send(
            st_r.at[t, u], st_r.at[sender, u], xs.at[6 + u, sender], xr.at[6 + u, sender],
            me, sender,
        )

    def user_rows(u):
        return pl.ds(pl.multiple_of(u * HIST, HIST), HIST)

    def attend(first, par):
        lanes = halves[par]
        tasks = [(first + k, q, 4 * k + q) for k in range(2) for q in range(4)]
        for u, q, slot in tasks:
            span = user_rows(u)
            p_t[slot] = mm(qn_s[q, span, lanes], kn_s[q, span, lanes], 1, 1)
        for u, q, slot in tasks:
            mask = (col_id <= row_id) & (col_id < len_ref[u])
            weights = jnp.where(mask, jnp.exp(p_t[slot] * scale), 0.0)
            w_s[2 * q + par, user_rows(u)] = (weights * (1.0 / lane_sum(weights))).astype(BF16)
        for u, q, slot in tasks:
            span = user_rows(u)
            o_s[q, span, lanes] = rc_s[q, span, lanes].astype(F32) + mm(
                w_s[2 * q + par, span], v_s[q, span, lanes], 1, 0
            )

    def first_half(i, carry):
        attend(2 * i, 0)
        return carry

    def score(u):
        span = user_rows(u)
        cspan = user_rows(u + 4)
        own = jnp.zeros((HIST, 1), F32)
        hit = jnp.zeros((HIST, 1), F32)
        neg = jnp.zeros((HIST, HIST), F32)
        for q in range(4):
            out = o_s[q, span]
            own = own + lane_sum(out * out)
            hit = hit + lane_sum(out * follow_of(rc_s[q, span].astype(F32)))
            high = out.astype(BF16)
            low = (out - high.astype(F32)).astype(BF16)
            cands = rc_s[q, cspan]
            neg = neg + mm(high, cands, 1, 1) + mm(low, cands, 1, 1)
        stats = neg + jnp.where(col_id == CAND, own, 0.0) + jnp.where(col_id == CAND + 1, hit, 0.0)
        st_r[t, u] = stats.astype(BF16)
        for j in (2, 1, 3):
            st_copy(u, j).start()

    def second_half(i, carry):
        attend(2 * i, 1)
        score(2 * i)
        score(2 * i + 1)
        return carry

    def turn_weights(k, carry):
        for u in range(4):
            span = slice(u * HIST, (u + 1) * HIST)
            wt_s[k, span] = jnp.transpose(w_s[k, span].astype(F32)).astype(BF16)
        return carry

    for par, step in ((0, first_half), (1, second_half)):
        all_in(1 if par == 0 else 4, outq.at[:, halves[0]])
        for q in range(4):
            qn_s[q, :, halves[par]] = mm(hott[0:512], bufq[q, :, halves[par]], 1, 0).astype(BF16)
        lax.fori_loop(0, 2, step, 0)
    lax.fori_loop(0, 8, turn_weights, 0)

    def losses(u, carry):
        for j in (1, 3, 2):
            st_from(u, j).wait_recv()
        stats = (
            st_r[0, u].astype(F32) + st_r[1, u].astype(F32)
            + st_r[2, u].astype(F32) + st_r[3, u].astype(F32)
        )
        is_cand = col_id < CAND
        neg = jnp.where(is_cand, stats, 0.0)
        own = lane_sum(jnp.where(col_id == CAND, stats, 0.0))
        hit = lane_sum(jnp.where(col_id == CAND + 1, stats, 0.0))
        sq_follow = pltpu.roll(sqf_s[user_rows(u)], HIST - 1, 0)[:, 0:1]
        rn = lax.rsqrt(own + EPS)
        rf = lax.rsqrt(sq_follow + EPS)
        rc = lax.rsqrt(sqc_s[u] + EPS)
        tl = SOFT * hit * rn * rf
        nl = SOFT * neg * rn * rc
        en = jnp.where(is_cand, jnp.exp(nl), 0.0)
        et = jnp.exp(tl)
        whole = et + lane_sum(en)
        span = len_ref[u] - 1
        over = 1.0 / (jnp.full((HIST, 1), 0, jnp.int32) + span).astype(F32)
        valid = iota((HIST, 1), 0) < span
        terms = jnp.where(valid, (jnp.log(whole) - tl) * over, 0.0)
        loss_ref[u] = jnp.broadcast_to(jnp.sum(terms, axis=0, keepdims=True), (1, HIST))
        g = jnp.where(valid, float(D) * over, 0.0)
        dtl = g * (et / whole - 1.0)
        dnl = (g / whole) * en
        dsc[u, 0] = jnp.broadcast_to(
            -rn * rn * (dtl * tl + lane_sum(dnl * nl)), (HIST, HIST)
        )
        dsc[u, 1] = jnp.broadcast_to(dtl * (SOFT * rn * rf), (HIST, HIST))
        dneg = dnl * (SOFT * rn * rc)
        dneg_s[u] = dneg.astype(BF16)
        dnegt_s[u] = jnp.transpose(dneg).astype(BF16)
        dsqf = jnp.broadcast_to(-0.5 * dtl * tl * rf * rf, (HIST, HIST))
        gfol[user_rows(u)] = pltpu.roll(dsqf, 1, 0)
        grow[u] = -0.5 * rc * rc * jnp.sum(dnl * nl, axis=0, keepdims=True)
        return carry

    lax.fori_loop(0, 4, losses, 0)

    def backward_quarter(i, carry):
        q = (y + 1 + i) % 4
        for u in range(4):
            span = slice(u * HIST, (u + 1) * HIST)
            cspan = slice((4 + u) * HIST, (5 + u) * HIST)
            dhit = twice(dsc[u, 1])
            out = o_s[q, span]
            rows = rc_s[q, span].astype(F32)
            dout = (
                twice(dsc[u, 0]) * out
                + dhit * follow_of(rows)
                + mm(dneg_s[u], rc_s[q, cspan], 1, 0)
            )
            dout_t[span] = dout.astype(BF16)
            drc_s[q, span] = (dout + pltpu.roll(dhit * out, 1, 0)).astype(BF16)
            drc_s[q, cspan] = mm(dnegt_s[u], out.astype(BF16), 1, 0).astype(BF16)
        tasks = [
            (slice(u * HIST, (u + 1) * HIST), halves[par], par, 2 * u + par)
            for u in range(4)
            for par in range(2)
        ]
        for span, lanes, par, slot in tasks:
            p_t[slot] = mm(dout_t[span, lanes], v_s[q, span, lanes], 1, 1)
        for span, lanes, par, slot in tasks:
            dw = p_t[slot]
            wide = w_s[2 * q + par, span].astype(F32)
            ds_t[slot] = (wide * (dw - lane_sum(dw * wide)) * scale).astype(BF16)
        for span, lanes, par, slot in tasks:
            dq_t[span, lanes] = mm(ds_t[slot], kn_s[q, span, lanes], 1, 0).astype(BF16)
            dk_s[q, span, lanes] = mm(ds_t[slot], qn_s[q, span, lanes], 0, 0).astype(BF16)
            dv_s[q, span, lanes] = mm(wt_s[2 * q + par, span], dout_t[span, lanes], 1, 0).astype(
                BF16
            )
        dqo[q] = mm(hot[:, 0:512], dq_t[...], 1, 0).astype(BF16)
        to_group(2, dqo, rq, q, i == 3)
        return carry

    lax.fori_loop(0, 4, backward_quarter, 0)

    nbs[...] = jnp.zeros(nbs.shape, F32)

    def return_quarter(i, carry):
        q = (y + 1 + i) % 4
        dk = mm(hot[:, 0:512], dk_s[q], 1, 0)
        dn = mm(hot[:, 0:512], dv_s[q], 1, 0) + norm_heads_back(nrm[q].astype(F32), dk)
        dn = dn * gain_s[q]
        nbs[...] += jnp.broadcast_to(lane_sum(dn * bufe[q].astype(F32)), (256, HD))
        eo[q] = (mm(hot[...], drc_s[q], 1, 0) + dn * twice(rsm[...])).astype(BF16)
        return carry

    lax.fori_loop(0, 4, return_quarter, 0)
    gsq = lane_sum(mm(hot[:, 0:512], lane_parts(gfol[...]), 1, 0)) + lane_sum(
        mm(
            hot[:, 512:1024],
            row_parts(jnp.concatenate([grow[u] for u in range(4)], axis=1)), 1, 1,
        )
    )
    placed = []
    for values in (jnp.broadcast_to(gsq, (256, HD)), nbs[...]):
        high, mid, low = split3(jnp.where(in_lane, values, 0.0))
        placed.append(mm(blocks, high, 0, 0) + mm(blocks, mid, 0, 0) + mm(blocks, low, 0, 0))
    for b in range(16):
        sco[b] = jnp.concatenate([part[b : b + 1] for part in placed], axis=1)
    to_matched(6, lambda b: sco.at[b], sci)

    def return_group(i, carry):
        to_group(3, eo, re, (y + 1 + i) % 4, i == 3)
        return carry

    lax.fori_loop(0, 4, return_group, 0)

    all_in(2, rq)
    dq_item = norm_heads_back(q32[...], mm(gt[...], rq[...], 1, 0)).astype(BF16)
    dqg[t] = dq_item.reshape(4, 64, 256)
    chunks = (((y + 2) % NY, (y + 1) % NY), ((y + 3) % NY, y))

    def dq_copy(part, j):
        peer = (t + j) % NT
        return [
            send(
                dqg.at[t, b], dqg.at[t, b], xs.at[(2, 3, 4, 10)[2 * part + k], peer],
                xr.at[(2, 3, 4, 10)[2 * part + k], t], me, peer,
            )
            for k, b in enumerate(chunks[part])
        ]

    def dq_from(part, j):
        sender = (t + NT - j) % NT
        return [
            send(
                dqg.at[t, b], dqg.at[sender, b], xs.at[(2, 3, 4, 10)[2 * part + k], sender],
                xr.at[(2, 3, 4, 10)[2 * part + k], sender], me, sender,
            )
            for k, b in enumerate(chunks[part])
        ]

    for part in range(2):
        for j in (2, 1, 3):
            for copy in dq_copy(part, j):
                copy.start()
    dots = row_sums(dq_item.astype(F32) * q32[...])
    gws_of = lambda peer: gws.at[peer]
    for part in range(2):
        for j in (1, 3, 2):
            for copy in dq_from(part, j):
                copy.wait_recv()
        acc = jnp.zeros((128, 1024), F32)
        for tt in range(NT):
            acc = acc + mm(
                jnp.concatenate([dqg[tt, b] for b in chunks[part]], axis=0),
                wt[2 * tt : 2 * tt + 2].reshape(256, 1024), 1, 0,
            )
        acc = acc.astype(BF16)
        for k, b in enumerate(chunks[part]):
            gws[b] = acc[k * 64 : (k + 1) * 64]
        for j in ((2, 1), (3,))[part]:
            y_copy(2, gws_of, gwr, j).start()
    gwr[y] = gws[y]
    all_in(6, sci)
    pairs = [sci[2 * b] + sci[2 * b + 1] for b in range(NZ)]
    item_terms = []
    for lanes in (slice(0, HD), slice(HD, 2 * HD)):
        row = jnp.concatenate([pair[:, lanes] for pair in pairs], axis=1)
        item_terms.append(jnp.sum(mm(row_parts(row), gt[...], 1, 1), axis=0, keepdims=True))
    sdy[y, pl.ds(8, 8), :] = jnp.broadcast_to(item_terms[0], (8, 256))
    rs_all = mm(jnp.ones((8, HD), BF16), lane_parts(rscol[...]), 1, 1)[0:1]
    sdx[t] = dots + rs_all * item_terms[1]
    own_sdx = lambda peer: sdx.at[t]
    start3(x_copy, 5, own_sdx, sdx)
    wait_in(x_from, 5, own_sdx, sdx)
    sdy[y, pl.ds(0, 8), :] = sdx[0] + sdx[1] + sdx[2] + sdx[3]
    own_sdy = lambda peer: sdy.at[y]
    start3(y_copy, 4, own_sdy, sdy)
    all_in(3, re)
    es[...] = mm(gt[...], re[...], 1, 0).astype(BF16).reshape(4, 64, 256)
    es_of = lambda peer: es.at[peer]
    start3(y_copy, 3, es_of, er)
    er[y] = es[y]

    mine = pl.ds(pl.multiple_of(y * 64, 64), 64)
    emb = (hidden_ref[...].astype(F32) * rcol[mine, 0:1] * gi).astype(BF16).astype(F32)
    rs_own = rscol[mine, 0:1]
    wait_in(y_from, 4, own_sdy, sdy)
    last = sdy[0] + sdy[1] + sdy[2] + sdy[3]
    sqm[...] = columns(2.0 * last[8:9] - (1.0 / D) * rs_all * rs_all * last[0:1])
    coef = sqm[mine, 0:1]
    direct = emb * coef
    wait_in(y_from, 2, gws_of, gwr)
    gw = (
        gwr[0].astype(F32) + gwr[1].astype(F32) + gwr[2].astype(F32) + gwr[3].astype(F32)
    ) * gu * rs_own + direct
    wait_in(y_from, 3, es_of, er)
    for h in range(8):
        lanes = slice(h * HD, (h + 1) * HD)
        par, q = h // 4, h % 4
        grad_ref[:, lanes] = er[q, :, halves[par]].astype(F32) + gw[:, lanes]

    for k, src, dst in (
        (0, own_hd, hd), (1, own_sel, selb), (2, gws_of, gwr), (3, es_of, er), (4, own_sdy, sdy),
        (5, own_sqy, sqy),
    ):
        wait_out(y_copy, k, src, dst)
    for k, src, dst in (
        (0, own_sqx, sqx), (5, own_sdx, sdx)
    ):
        wait_out(x_copy, k, src, dst)
    for part in range(2):
        for j in (1, 3, 2):
            for copy in dq_copy(part, j):
                copy.wait_send()
    for j in (1, 3, 2):
        ps_copy((t + j) % NT).wait_send()
    for u in range(4):
        for j in (1, 3, 2):
            st_copy(u, j).wait_send()
    for stream in range(4):
        for step in range(RING[stream]):
            ring(stream, step).wait_send()
    for b in range(NZ):
        for half in range(2):
            partner(b, c, half).wait_send()
    most = pl.ds(0, (NS - 1) * 16)
    all_out(0, oute.at[most])
    all_out(1, outq.at[most, halves[0]])
    all_out(4, outq.at[most, halves[1]])
    all_out(2, rq.at[most])
    all_out(3, re.at[most])
    all_out(5, sqi.at[pl.ds(0, 15)])
    all_out(6, sci.at[pl.ds(0, 15)])


def local(item_hidden, item_gain, send_item, pos_slot, hist_len, user_gain, query_weight):
    vmem = pltpu.VMEM
    dma = pltpu.SemaphoreType.DMA
    quarter = lambda kind: vmem((4, 256, 256), kind)
    grad, loss = pl.pallas_call(
        kernel,
        out_shape=(
            jax.ShapeDtypeStruct((64, 1024), F32),
            jax.ShapeDtypeStruct((4, 1, HIST), F32),
        ),
        in_specs=[pl.BlockSpec(memory_space=pltpu.SMEM)]
        + [pl.BlockSpec(memory_space=pltpu.VMEM)] * 6,
        out_specs=(
            pl.BlockSpec(memory_space=pltpu.VMEM),
            pl.BlockSpec(memory_space=pltpu.VMEM),
        ),
        scratch_shapes=[
            vmem((4, 64, 1024), BF16),
            vmem((4, 1, 1024), F32),
            vmem((8, 2, 64, 1024), BF16),
            vmem((4, 16, HIST), F32),
            vmem((4, 8, HIST), F32),
            quarter(BF16),
            quarter(BF16),
            vmem((1024, 256), BF16),
            vmem((1024, 256), BF16),
            quarter(BF16),
            quarter(BF16),
            vmem((256, 1024), BF16),
            quarter(BF16),
            quarter(BF16),
            vmem((8, 1, HIST), F32),
            vmem((16, 1, HIST), F32),
            vmem((256, HIST), F32),
            vmem((256, HIST), F32),
            vmem((256, 256), F32),
            vmem((256, HIST), F32),
            vmem((256, HIST), F32),
            vmem((4, 2 * HIST), jnp.int32),
            vmem((256, 1024), BF16),
            vmem((1024, 256), BF16),
            vmem((512, HIST), F32),
            vmem((4, 1, HIST), F32),
            vmem((4, 1, 256), F32),
            vmem((4, 1024, 256), BF16),
            vmem((4, 512, 256), BF16),
            vmem((4, 512, 256), BF16),
            vmem((4, 512, 256), BF16),
            vmem((8, 512, HIST), BF16),
            vmem((8, 512, HIST), BF16),
            vmem((8, HIST, HIST), F32),
            vmem((8, HIST, HIST), BF16),
            vmem((4, 512, 256), F32),
            vmem((4, 4, HIST, HIST), BF16),
            vmem((4, 2, HIST, HIST), F32),
            vmem((4, HIST, HIST), BF16),
            vmem((4, HIST, HIST), BF16),
            vmem((512, HIST), F32),
            vmem((4, 1, HIST), F32),
            vmem((512, 256), BF16),
            vmem((512, 256), BF16),
            vmem((4, 512, 256), BF16),
            vmem((4, 512, 256), BF16),
            vmem((4, 1024, 256), BF16),
            vmem((256, HIST), F32),
            quarter(BF16),
            quarter(BF16),
            vmem((1024, 256), BF16),
            vmem((1024, 256), BF16),
            vmem((16, 1, 256), F32),
            vmem((16, 1, 256), F32),
            vmem((4, 4, 64, 256), BF16),
            vmem((4, 64, 1024), BF16),
            vmem((4, 64, 1024), BF16),
            vmem((4, 64, 256), BF16),
            vmem((4, 64, 256), BF16),
            vmem((4, 8, 256), F32),
            vmem((4, 16, 256), F32),
            dma((11, 4)),
            dma((11, 4)),
            dma((6, 4)),
            dma((6, 4)),
            dma((4, 4)),
            dma((4, 4)),
            dma((8, 2)),
            dma((8, 2)),
            dma((7,)),
            dma((7,)),
            pltpu.SemaphoreType.REGULAR((2, 4)),
        ],
        compiler_params=pltpu.CompilerParams(
            collective_id=0, has_side_effects=True, vmem_limit_bytes=60 * 1024 * 1024
        ),
    )(
        hist_len, item_hidden, query_weight.T, item_gain, user_gain, send_item[0].T, pos_slot
    )
    return (grad, loss[:, 0, 0])


def solution(mesh):
    placed = (
        P("sect", "tp"),
        P("tp"),
        P("sect", None, None),
        P("sect", None),
        P("sect"),
        P("tp"),
        P("tp", "sect"),
    )
    return jax.shard_map(
        local, mesh=mesh, in_specs=placed, out_specs=(P("sect", "tp"), P("sect")), check_vma=False
    )
```

```python
import jax
import jax.numpy as jnp
from jax import lax
from jax.experimental import pallas as pl
from jax.experimental.pallas import tpu as pltpu
from jax.sharding import PartitionSpec as P

D = 4096
HD = 128
HIST = 128
CAND = 64
NZ, NY, NT = 8, 4, 4
NS = 64
EPS = 1e-06
SOFT = 20.0
F32, BF16 = jnp.float32, jnp.bfloat16
MESH = pl.DeviceIdType.MESH
RING = (4, 3, 3, 4)


def mm(a, b, ca, cb, precision=None):
    return lax.dot_general(
        a, b, (((ca,), (cb,)), ((), ())), preferred_element_type=F32, precision=precision
    )


def split3(values):
    high = values.astype(BF16)
    rest = values - high.astype(F32)
    mid = rest.astype(BF16)
    return high, mid, (rest - mid.astype(F32)).astype(BF16)


def row_parts(row):
    parts = split3(jnp.broadcast_to(row, (8, row.shape[1])))
    index = iota((8, row.shape[1]), 0)
    out = jnp.where(index == 0, parts[0].astype(F32), 0.0)
    out = jnp.where(index == 1, parts[1].astype(F32), out)
    return jnp.where(index == 2, parts[2].astype(F32), out).astype(BF16)


def lane_parts(values):
    parts = split3(values)
    index = iota(values.shape, 1)
    out = jnp.where(index == 0, parts[0].astype(F32), 0.0)
    out = jnp.where(index == 1, parts[1].astype(F32), out)
    return jnp.where(index == 2, parts[2].astype(F32), out).astype(BF16)


def columns(row):
    return mm(row_parts(row), jnp.ones((8, 128), BF16), 0, 0)


def row_sums(values):
    ones = jnp.ones((8, values.shape[1]), BF16)
    high, mid, low = split3(values)
    return mm(ones, high, 1, 1) + mm(ones, mid, 1, 1) + mm(ones, low, 1, 1)


def lane_sum(values):
    return jnp.sum(values, axis=1, keepdims=True)


def iota(shape, dim):
    return lax.broadcasted_iota(jnp.int32, shape, dim)


def one_hot(row, count):
    return jnp.where(iota((count, row.shape[1]), 0) == row, 1.0, 0.0)


def norm_heads(values):
    heads, roots = [], []
    for par in range(2):
        part = values[:, par * HD : (par + 1) * HD]
        root = lax.rsqrt(lane_sum(part * part) * (1.0 / HD) + EPS)
        heads.append(part * root)
        roots.append(root)
    return heads, roots


def norm_heads_back(values, grads):
    heads, roots = norm_heads(values)
    out = []
    for par in range(2):
        grad = grads[:, par * HD : (par + 1) * HD]
        out.append(
            roots[par] * (grad - heads[par] * (lane_sum(grad * heads[par]) * (1.0 / HD)))
        )
    return jnp.concatenate(out, axis=1)


def kernel(
    len_ref, hidden_ref, w_ref, gi_ref, gu_ref, send_ref, pos_ref,
    grad_ref, loss_ref,
    hd, selb, wt, sqx, sqy, ps, pr, oute, outq, bufe, bufq, gt, nrm, knb, sqo, sqi, sqm, rsm, q32,
    rcol, rscol, pos_s, hot, hott, sqf_s, sqc_s, gain_s,
    rc_s, kn_s, v_s, qn_s, w_s, wt_s, p_t, ds_t, o_s, st_r, dsc, dneg_s, dnegt_s, gfol, grow,
    dout_t, dq_t, dk_s, dv_s, drc_s, nbs, dqo, eo, rq, re, sco, sci,
    dqg, gws, gwr, es, er, sdx, sdy,
    xs, xr, ys, yr, ring_s, ring_r, par_s, par_r, a2a_s, a2a_r, ps_s, ps_r, hello,
):
    me = lax.axis_index("sect")
    t = lax.axis_index("tp")
    z, y, c = me // 8, (me // 2) % 4, me % 2
    blk = z * 2 + c

    def send(src, dst, ssem, rsem, sect, tp):
        return pltpu.make_async_remote_copy(
            src_ref=src, dst_ref=dst, send_sem=ssem, recv_sem=rsem,
            device_id=(sect, tp), device_id_type=MESH,
        )

    def sect_of(zz, yy, cc):
        return zz * 8 + yy * 2 + cc

    def x_copy(k, src, dst, j):
        peer = (t + j) % NT
        return send(src(peer), dst.at[t], xs.at[k, peer], xr.at[k, t], me, peer)

    def x_from(k, src, dst, j):
        sender = (t + NT - j) % NT
        return send(src(t), dst.at[sender], xs.at[k, sender], xr.at[k, sender], me, sender)

    def y_copy(k, src, dst, j):
        peer = (y + j) % NY
        return send(src(peer), dst.at[y], ys.at[k, peer], yr.at[k, y], sect_of(z, peer, c), t)

    def y_from(k, src, dst, j):
        sender = (y + NY - j) % NY
        return send(
            src(y), dst.at[sender], ys.at[k, sender], yr.at[k, sender], sect_of(z, sender, c), t
        )

    def start3(copy, k, src, dst):
        for j in (2, 1, 3):
            copy(k, src, dst, j).start()

    def wait_in(came, k, src, dst):
        for j in (1, 3, 2):
            came(k, src, dst, j).wait_recv()

    def wait_out(copy, k, src, dst):
        for j in (1, 3, 2):
            copy(k, src, dst, j).wait_send()

    def rows_of(first):
        return pl.ds(pl.multiple_of(first * 16, 16), 16)

    def to_readers(k, out, buf, lanes):
        pltpu.make_async_copy(
            out.at[rows_of(me), lanes], buf.at[y, rows_of(blk), lanes], a2a_r.at[k]
        ).start()

        def step(j, carry):
            peer = (me + j) % NS
            send(
                out.at[rows_of(peer), lanes], buf.at[y, rows_of(blk), lanes],
                a2a_s.at[k], a2a_r.at[k], peer, t,
            ).start()
            return carry

        lax.fori_loop(1, NS, step, 0, unroll=7)

    def to_group(k, out, buf, group, same):
        def copy(j):
            b = (blk + j) % 16
            return send(
                out.at[group, rows_of(b)], buf.at[rows_of(me)],
                a2a_s.at[k], a2a_r.at[k], sect_of(b // 2, group, b % 2), t,
            )

        @pl.when(same)
        def _():
            pltpu.make_async_copy(
                out.at[group, rows_of(blk)], buf.at[rows_of(me)], a2a_r.at[k]
            ).start()

        @pl.when(jnp.logical_not(same))
        def _():
            copy(0).start()

        def step(j, carry):
            copy(j).start()
            return carry

        lax.fori_loop(1, 16, step, 0, unroll=5)

    def to_matched(k, src_of, dst):
        pltpu.make_async_copy(src_of(blk), dst.at[blk], a2a_r.at[k]).start()

        def step(j, carry):
            b = (blk + j) % 16
            send(
                src_of(b), dst.at[blk], a2a_s.at[k], a2a_r.at[k], sect_of(b // 2, y, b % 2), t
            ).start()
            return carry

        lax.fori_loop(1, 16, step, 0, unroll=5)

    def all_in(k, view):
        pltpu.make_async_copy(view, view, a2a_r.at[k]).wait()

    def all_out(k, view):
        pltpu.make_async_copy(view, view, a2a_s.at[k]).wait()

    def ring(stream, step):
        way = 1 if stream < 2 else NZ - 1
        block = (z + (NZ - way) * step) % NZ
        part = wt.at[block, c, pl.ds((stream % 2) * 32, 32)]
        return send(
            part, part, ring_s.at[stream, step], ring_r.at[stream, step],
            sect_of((z + way) % NZ, y, c), t,
        )

    def ring_from(stream, step):
        way = 1 if stream < 2 else NZ - 1
        block = (z + (NZ - way) * (step + 1)) % NZ
        part = wt.at[block, c, pl.ds((stream % 2) * 32, 32)]
        return block, send(
            part, part, ring_s.at[stream, step], ring_r.at[stream, step],
            sect_of((z + way) % NZ, y, c), t,
        )

    def partner(block, core, half):
        part = wt.at[block, core, pl.ds(half * 32, 32)]
        return send(
            part, part, par_s.at[block, half], par_r.at[block, half], sect_of(z, y, 1 - c), t
        )

    def partner_in(block, half):
        partner(block, 1 - c, half).wait_recv()

    def advance(step):
        for stream in (0, 2, 1, 3):
            if step >= RING[stream]:
                continue
            block, came = ring_from(stream, step)
            came.wait_recv()
            if step + 1 < RING[stream]:
                ring(stream, step + 1).start()
            partner(block, c, stream % 2).start()

    barrier = pltpu.get_barrier_semaphore()
    for j in range(1, 8):
        pl.semaphore_signal(
            barrier, inc=1, device_id=(z * 8 + (me + j) % 8, t), device_id_type=MESH
        )
    for j in (1, NZ - 1):
        pl.semaphore_signal(
            barrier, inc=1, device_id=(sect_of((z + j) % NZ, y, c), t), device_id_type=MESH
        )
    for j in range(1, NT):
        pl.semaphore_signal(barrier, inc=1, device_id=(me, (t + j) % NT), device_id_type=MESH)

    hd[y] = hidden_ref[...]
    sqx[t] = jnp.zeros((16, HIST), F32)
    wt[z, c] = w_ref[...]
    spread = jnp.where((iota((64, 1024), 1) >> 4) == iota((64, 1024), 0), 1.0, 0.0).astype(BF16)
    named = mm(send_ref[...].astype(F32).astype(BF16), spread, 1, 0)
    lane = iota((1, 1024), 1)
    pick = jnp.full((1, 1024), -1.0, F32)
    for s in range(4):
        pick = jnp.where((lane & 3) == s, named[s : s + 1], pick)
    base = (jnp.zeros((1, 1024), jnp.int32) + y * 64).astype(F32)
    selb[y] = jnp.where((((lane >> 2) & 3) == y) & (pick >= 0.0), pick + base, -1.0)
    pl.semaphore_wait(barrier, 7 + 2 + NT - 1)

    def greet(step):
        for way in range(2):
            if step < 4 - way:
                peer = (z + 1) % NZ if way == 0 else (z + NZ - 1) % NZ
                pl.semaphore_signal(
                    hello.at[way, step], inc=1, device_id=(sect_of(peer, y, c), t),
                    device_id_type=MESH,
                )

    def relay(step):
        for way in range(2):
            if step < 4 - way:
                pl.semaphore_wait(hello.at[way, step], 1)
        greet(step + 1)

    greet(0)
    own_hd = lambda peer: hd.at[y]
    own_sel = lambda peer: selb.at[y]
    for stream in (0, 2, 1, 3):
        ring(stream, 0).start()
    start3(y_copy, 0, own_hd, hd)
    start3(y_copy, 1, own_sel, selb)
    for half in range(2):
        partner(z, c, half).start()

    gi = gi_ref[...].astype(F32).reshape(1, 1024)
    gu = gu_ref[...].astype(F32).reshape(1, 1024)
    hidden = hidden_ref[...].astype(F32)
    gained = hidden * gi
    sqx[t, pl.ds(0, 8), 0:64] = row_sums(hidden * hidden)
    sqx[t, pl.ds(8, 8), 0:64] = row_sums(gained * gained)
    own_sqx = lambda peer: sqx.at[t]
    start3(x_copy, 0, own_sqx, sqx)

    slots = pos_ref[...]
    owner = slots >> 2
    pos_s[...] = jnp.full(pos_s.shape, -1, jnp.int32)
    pos_s[:, 0 : HIST + CAND] = (
        ((owner >> 3) << 5) | ((owner & 1) << 4) | (((owner >> 1) & 3) << 2) | (slots & 3)
    )
    for u in range(4):
        for kind in range(2):
            row = pos_s[u : u + 1, kind * HIST : (kind + 1) * HIST]
            picked = one_hot(row, 256)
            first = (4 * kind + u) * HIST
            hot[:, first : first + HIST] = picked.astype(BF16)
            hott[first : first + HIST, :] = jnp.transpose(picked).astype(BF16)

    advance(0)
    relay(0)
    wait_in(x_from, 0, own_sqx, sqx)
    sums = sqx[0] + sqx[1] + sqx[2] + sqx[3]
    r_row = lax.rsqrt(sums[0:1] * (1.0 / D) + EPS)
    sq_item = r_row * r_row * sums[8:9]
    rs_row = lax.rsqrt(sq_item * (1.0 / D) + EPS)
    sqy[y] = jnp.concatenate([r_row, rs_row, sq_item] + [r_row] * 5, axis=0)
    own_sqy = lambda peer: sqy.at[y]
    start3(y_copy, 5, own_sqy, sqy)
    relay(1)
    advance(1)
    relay(2)
    wait_in(y_from, 0, own_hd, hd)
    lhs = (hd[...].reshape(256, 1024).astype(F32) * (gi * gu)).astype(BF16)

    def ps_copy(block):
        part, par = block // 2, block % 2
        return send(
            ps.at[block], pr.at[t, par], ps_s.at[block], ps_r.at[t, par], me, part
        )

    def project(block):
        ps[block] = mm(lhs, wt[block].reshape(HD, 1024), 1, 1).astype(BF16)

        @pl.when(block // 2 != t)
        def _():
            ps_copy(block).start()

    def project_step(step):
        if step == 0:
            project(z)
        for way in (1, NZ - 1)[: 2 if step < 3 else 1]:
            project((z + way * (step + 1)) % NZ)

    def partners_in(step):
        if step == 0:
            for half in range(2):
                partner_in(z, half)
        for stream in range(4):
            if step < RING[stream]:
                way = 1 if stream < 2 else NZ - 1
                partner_in((z + (NZ - way) * (step + 1)) % NZ, stream % 2)

    partners_in(0)
    project_step(0)
    wait_in(y_from, 1, own_sel, selb)
    picks = jnp.maximum(jnp.maximum(selb[0], selb[1]), jnp.maximum(selb[2], selb[3]))
    gt[...] = one_hot(picks.astype(jnp.int32), 256).astype(BF16)
    wait_in(y_from, 5, own_sqy, sqy)
    rcol[...] = jnp.concatenate([columns(sqy[b, 0:1])[0:64] for b in range(4)], axis=0)
    rscol[...] = jnp.concatenate([columns(sqy[b, 1:2])[0:64] for b in range(4)], axis=0)
    sq_out = jnp.zeros((8, 1024), F32)
    for b in range(4):
        sq_out = sq_out + mm(
            row_parts(sqy[b, 2:3])[:, 0:64], gt[b * 64 : (b + 1) * 64, :], 1, 0
        )
    sq_out = jnp.sum(sq_out, axis=0, keepdims=True)
    for b in range(NZ):
        sqo[b] = sq_out[:, b * HD : (b + 1) * HD]
    pieces = []
    for par in range(2):
        head = par * 4 + y
        lanes = pl.ds(pl.multiple_of(head * HD, HD), HD)
        piece = hd[:, :, lanes].reshape(256, HD).astype(F32)
        gain = jnp.zeros((1, HD), F32)
        for h in range(8):
            gain = gain + jnp.where(head == h, gi[:, h * HD : (h + 1) * HD], 0.0)
        pieces.append((piece * rcol[...] * gain).astype(BF16))
    oute[...] = mm(gt[...], jnp.concatenate(pieces, axis=1), 0, 0).astype(BF16)
    partners_in(1)
    project_step(1)
    advance(2)
    relay(3)
    both = slice(0, 256)
    to_matched(5, lambda b: sqo.at[b // 2], sqi)
    to_readers(0, oute, bufe, both)
    partners_in(2)
    project_step(2)
    advance(3)
    partners_in(3)
    project_step(3)
    for q in range(4):
        gain_s[q] = jnp.concatenate(
            [gu[:, q * HD : (q + 1) * HD], gu[:, (4 + q) * HD : (5 + q) * HD]], axis=1
        )
    for par in range(2):
        pr[t, par] = ps[2 * t + par]
    for par in range(2):
        for j in (1, 3, 2):
            sender = (t + j) % NT
            send(
                ps.at[2 * t + par], pr.at[sender, par], ps_s.at[2 * t + par],
                ps_r.at[sender, par], me, sender,
            ).wait_recv()
    total = jnp.concatenate(
        [
            pr[0, par].astype(F32) + pr[1, par].astype(F32)
            + pr[2, par].astype(F32) + pr[3, par].astype(F32)
            for par in range(2)
        ],
        axis=1,
    ) * (rcol[...] * rscol[...])[:, 0:1]
    q32[...] = total
    heads, _ = norm_heads(total)
    outq[...] = mm(gt[...], jnp.concatenate(heads, axis=1).astype(BF16), 0, 0).astype(BF16)
    halves = (slice(0, HD), slice(HD, 2 * HD))
    to_readers(1, outq, bufq, halves[0])
    to_readers(4, outq, bufq, halves[1])

    off = (me % 8) * 16
    blocks = jnp.where((iota((256, 16), 0) >> 4) == iota((256, 16), 1), 1.0, 0.0).astype(BF16)
    in_lane = iota((256, HD), 1) == off + (iota((256, HD), 0) & 15)
    all_in(5, sqi)
    came = jnp.concatenate([sqi[b] for b in range(16)], axis=0)
    high, mid, low = split3(came)
    wide = mm(blocks, high, 1, 0) + mm(blocks, mid, 1, 0) + mm(blocks, low, 1, 0)
    sqm[...] = jnp.broadcast_to(lane_sum(jnp.where(in_lane, wide, 0.0)), (256, HD))
    rsm[...] = lax.rsqrt(sqm[...] * (1.0 / D) + EPS)
    sqf_s[...] = jnp.broadcast_to(
        lane_sum(mm(hott[0:512], lane_parts(sqm[...]), 1, 0)), (512, HIST)
    )
    sqc = jnp.sum(mm(lane_parts(sqm[...]), hot[:, 512:1024], 0, 0), axis=0, keepdims=True)
    for u in range(4):
        sqc_s[u] = sqc[:, u * HIST : (u + 1) * HIST]
    twice = lambda values: jnp.concatenate([values, values], axis=1)
    all_in(0, bufe)
    for q in range(4):
        low = (bufe[q].astype(F32) * twice(rsm[...]) * gain_s[q]).astype(BF16)
        nrm[q] = low
        heads, _ = norm_heads(low.astype(F32))
        knb[q] = jnp.concatenate(heads, axis=1).astype(BF16)
    for q in range(4):
        kn_s[q] = mm(hott[0:512], knb[q], 1, 0).astype(BF16)
        v_s[q] = mm(hott[0:512], nrm[q], 1, 0).astype(BF16)
    for q in range(4):
        rc_s[q] = mm(hott[...], bufe[q], 1, 0).astype(BF16)

    scale = HD ** (-0.5)
    row_id = iota((HIST, HIST), 0)
    col_id = iota((HIST, HIST), 1)

    def follow_of(rows):
        moved = pltpu.roll(rows, HIST - 1, 0)
        return jnp.where(iota(rows.shape, 0) < HIST - 1, moved, 0.0)

    def st_copy(u, j):
        peer = (t + j) % NT
        return send(st_r.at[t, u], st_r.at[t, u], xs.at[6 + u, peer], xr.at[6 + u, t], me, peer)

    def st_from(u, j):
        sender = (t + NT - j) % NT
        return send(
            st_r.at[t, u], st_r.at[sender, u], xs.at[6 + u, sender], xr.at[6 + u, sender],
            me, sender,
        )

    def user_rows(u):
        return pl.ds(pl.multiple_of(u * HIST, HIST), HIST)

    def attend(first, par):
        lanes = halves[par]
        tasks = [(first + k, q, 4 * k + q) for k in range(2) for q in range(4)]
        for u, q, slot in tasks:
            span = user_rows(u)
            p_t[slot] = mm(qn_s[q, span, lanes], kn_s[q, span, lanes], 1, 1)
        for u, q, slot in tasks:
            mask = (col_id <= row_id) & (col_id < len_ref[u])
            weights = jnp.where(mask, jnp.exp(p_t[slot] * scale), 0.0)
            w_s[2 * q + par, user_rows(u)] = (weights * (1.0 / lane_sum(weights))).astype(BF16)
        for u, q, slot in tasks:
            span = user_rows(u)
            o_s[q, span, lanes] = rc_s[q, span, lanes].astype(F32) + mm(
                w_s[2 * q + par, span], v_s[q, span, lanes], 1, 0
            )

    def first_half(i, carry):
        attend(2 * i, 0)
        return carry

    def score(u):
        span = user_rows(u)
        cspan = user_rows(u + 4)
        own = jnp.zeros((HIST, 1), F32)
        hit = jnp.zeros((HIST, 1), F32)
        neg = jnp.zeros((HIST, HIST), F32)
        for q in range(4):
            out = o_s[q, span]
            own = own + lane_sum(out * out)
            hit = hit + lane_sum(out * follow_of(rc_s[q, span].astype(F32)))
            high = out.astype(BF16)
            low = (out - high.astype(F32)).astype(BF16)
            cands = rc_s[q, cspan]
            neg = neg + mm(high, cands, 1, 1) + mm(low, cands, 1, 1)
        stats = neg + jnp.where(col_id == CAND, own, 0.0) + jnp.where(col_id == CAND + 1, hit, 0.0)
        st_r[t, u] = stats.astype(BF16)
        for j in (2, 1, 3):
            st_copy(u, j).start()

    def second_half(i, carry):
        attend(2 * i, 1)
        score(2 * i)
        score(2 * i + 1)
        return carry

    def turn_weights(k, carry):
        for u in range(4):
            span = slice(u * HIST, (u + 1) * HIST)
            wt_s[k, span] = jnp.transpose(w_s[k, span].astype(F32)).astype(BF16)
        return carry

    for par, step in ((0, first_half), (1, second_half)):
        all_in(1 if par == 0 else 4, outq.at[:, halves[0]])
        for q in range(4):
            qn_s[q, :, halves[par]] = mm(hott[0:512], bufq[q, :, halves[par]], 1, 0).astype(BF16)
        lax.fori_loop(0, 2, step, 0)
    lax.fori_loop(0, 8, turn_weights, 0)

    def losses(u, carry):
        for j in (1, 3, 2):
            st_from(u, j).wait_recv()
        stats = (
            st_r[0, u].astype(F32) + st_r[1, u].astype(F32)
            + st_r[2, u].astype(F32) + st_r[3, u].astype(F32)
        )
        is_cand = col_id < CAND
        neg = jnp.where(is_cand, stats, 0.0)
        own = lane_sum(jnp.where(col_id == CAND, stats, 0.0))
        hit = lane_sum(jnp.where(col_id == CAND + 1, stats, 0.0))
        sq_follow = pltpu.roll(sqf_s[user_rows(u)], HIST - 1, 0)[:, 0:1]
        rn = lax.rsqrt(own + EPS)
        rf = lax.rsqrt(sq_follow + EPS)
        rc = lax.rsqrt(sqc_s[u] + EPS)
        tl = SOFT * hit * rn * rf
        nl = SOFT * neg * rn * rc
        en = jnp.where(is_cand, jnp.exp(nl), 0.0)
        et = jnp.exp(tl)
        whole = et + lane_sum(en)
        span = len_ref[u] - 1
        over = 1.0 / (jnp.full((HIST, 1), 0, jnp.int32) + span).astype(F32)
        valid = iota((HIST, 1), 0) < span
        terms = jnp.where(valid, (jnp.log(whole) - tl) * over, 0.0)
        loss_ref[u] = jnp.broadcast_to(jnp.sum(terms, axis=0, keepdims=True), (1, HIST))
        g = jnp.where(valid, float(D) * over, 0.0)
        dtl = g * (et / whole - 1.0)
        dnl = (g / whole) * en
        dsc[u, 0] = jnp.broadcast_to(
            -rn * rn * (dtl * tl + lane_sum(dnl * nl)), (HIST, HIST)
        )
        dsc[u, 1] = jnp.broadcast_to(dtl * (SOFT * rn * rf), (HIST, HIST))
        dneg = dnl * (SOFT * rn * rc)
        dneg_s[u] = dneg.astype(BF16)
        dnegt_s[u] = jnp.transpose(dneg).astype(BF16)
        dsqf = jnp.broadcast_to(-0.5 * dtl * tl * rf * rf, (HIST, HIST))
        gfol[user_rows(u)] = pltpu.roll(dsqf, 1, 0)
        grow[u] = -0.5 * rc * rc * jnp.sum(dnl * nl, axis=0, keepdims=True)
        return carry

    lax.fori_loop(0, 4, losses, 0)

    def backward_quarter(i, carry):
        q = (y + 1 + i) % 4
        for u in range(4):
            span = slice(u * HIST, (u + 1) * HIST)
            cspan = slice((4 + u) * HIST, (5 + u) * HIST)
            dhit = twice(dsc[u, 1])
            out = o_s[q, span]
            rows = rc_s[q, span].astype(F32)
            dout = (
                twice(dsc[u, 0]) * out
                + dhit * follow_of(rows)
                + mm(dneg_s[u], rc_s[q, cspan], 1, 0)
            )
            dout_t[span] = dout.astype(BF16)
            drc_s[q, span] = (dout + pltpu.roll(dhit * out, 1, 0)).astype(BF16)
            drc_s[q, cspan] = mm(dnegt_s[u], out.astype(BF16), 1, 0).astype(BF16)
        tasks = [
            (slice(u * HIST, (u + 1) * HIST), halves[par], par, 2 * u + par)
            for u in range(4)
            for par in range(2)
        ]
        for span, lanes, par, slot in tasks:
            p_t[slot] = mm(dout_t[span, lanes], v_s[q, span, lanes], 1, 1)
        for span, lanes, par, slot in tasks:
            dw = p_t[slot]
            wide = w_s[2 * q + par, span].astype(F32)
            ds_t[slot] = (wide * (dw - lane_sum(dw * wide)) * scale).astype(BF16)
        for span, lanes, par, slot in tasks:
            dq_t[span, lanes] = mm(ds_t[slot], kn_s[q, span, lanes], 1, 0).astype(BF16)
            dk_s[q, span, lanes] = mm(ds_t[slot], qn_s[q, span, lanes], 0, 0).astype(BF16)
            dv_s[q, span, lanes] = mm(wt_s[2 * q + par, span], dout_t[span, lanes], 1, 0).astype(
                BF16
            )
        dqo[q] = mm(hot[:, 0:512], dq_t[...], 1, 0).astype(BF16)
        to_group(2, dqo, rq, q, i == 3)
        return carry

    lax.fori_loop(0, 4, backward_quarter, 0)

    nbs[...] = jnp.zeros(nbs.shape, F32)

    def return_quarter(i, carry):
        q = (y + 1 + i) % 4
        dk = mm(hot[:, 0:512], dk_s[q], 1, 0)
        dn = mm(hot[:, 0:512], dv_s[q], 1, 0) + norm_heads_back(nrm[q].astype(F32), dk)
        dn = dn * gain_s[q]
        nbs[...] += jnp.broadcast_to(lane_sum(dn * bufe[q].astype(F32)), (256, HD))
        eo[q] = (mm(hot[...], drc_s[q], 1, 0) + dn * twice(rsm[...])).astype(BF16)
        return carry

    lax.fori_loop(0, 4, return_quarter, 0)
    gsq = lane_sum(mm(hot[:, 0:512], lane_parts(gfol[...]), 1, 0)) + lane_sum(
        mm(
            hot[:, 512:1024],
            row_parts(jnp.concatenate([grow[u] for u in range(4)], axis=1)), 1, 1,
        )
    )
    placed = []
    for values in (jnp.broadcast_to(gsq, (256, HD)), nbs[...]):
        high, mid, low = split3(jnp.where(in_lane, values, 0.0))
        placed.append(mm(blocks, high, 0, 0) + mm(blocks, mid, 0, 0) + mm(blocks, low, 0, 0))
    for b in range(16):
        sco[b] = jnp.concatenate([part[b : b + 1] for part in placed], axis=1)
    to_matched(6, lambda b: sco.at[b], sci)

    def return_group(i, carry):
        to_group(3, eo, re, (y + 1 + i) % 4, i == 3)
        return carry

    lax.fori_loop(0, 4, return_group, 0)

    all_in(6, sci)
    pairs = [sci[2 * b] + sci[2 * b + 1] for b in range(NZ)]
    item_terms = []
    for lanes in (slice(0, HD), slice(HD, 2 * HD)):
        row = jnp.concatenate([pair[:, lanes] for pair in pairs], axis=1)
        item_terms.append(jnp.sum(mm(row_parts(row), gt[...], 1, 1), axis=0, keepdims=True))
    sdy[y, pl.ds(8, 8), :] = jnp.broadcast_to(item_terms[0], (8, 256))
    rs_all = mm(jnp.ones((8, HD), BF16), lane_parts(rscol[...]), 1, 1)[0:1]
    all_in(2, rq)
    dq_item = norm_heads_back(q32[...], mm(gt[...], rq[...], 1, 0)).astype(BF16)
    dqg[t] = dq_item.reshape(4, 64, 256)
    chunks = (((y + 2) % NY, (y + 1) % NY), ((y + 3) % NY, y))

    def dq_copy(part, j):
        peer = (t + j) % NT
        return [
            send(
                dqg.at[t, b], dqg.at[t, b], xs.at[(2, 3, 4, 10)[2 * part + k], peer],
                xr.at[(2, 3, 4, 10)[2 * part + k], t], me, peer,
            )
            for k, b in enumerate(chunks[part])
        ]

    def dq_from(part, j):
        sender = (t + NT - j) % NT
        return [
            send(
                dqg.at[t, b], dqg.at[sender, b], xs.at[(2, 3, 4, 10)[2 * part + k], sender],
                xr.at[(2, 3, 4, 10)[2 * part + k], sender], me, sender,
            )
            for k, b in enumerate(chunks[part])
        ]

    sdx[t] = row_sums(dq_item.astype(F32) * q32[...]) + rs_all * item_terms[1]
    own_sdx = lambda peer: sdx.at[t]
    start3(x_copy, 5, own_sdx, sdx)
    for part in range(2):
        for j in (2, 1, 3):
            for copy in dq_copy(part, j):
                copy.start()
    gws_of = lambda peer: gws.at[peer]
    for part in range(2):
        for j in (1, 3, 2):
            for copy in dq_from(part, j):
                copy.wait_recv()
        acc = jnp.zeros((128, 1024), F32)
        for tt in range(NT):
            acc = acc + mm(
                jnp.concatenate([dqg[tt, b] for b in chunks[part]], axis=0),
                wt[2 * tt : 2 * tt + 2].reshape(256, 1024), 1, 0,
            )
        acc = acc.astype(BF16)
        for k, b in enumerate(chunks[part]):
            gws[b] = acc[k * 64 : (k + 1) * 64]
        for j in ((2, 1), (3,))[part]:
            y_copy(2, gws_of, gwr, j).start()
        if part == 0:
            wait_in(x_from, 5, own_sdx, sdx)
            sdy[y, pl.ds(0, 8), :] = sdx[0] + sdx[1] + sdx[2] + sdx[3]
            own_sdy = lambda peer: sdy.at[y]
            start3(y_copy, 4, own_sdy, sdy)
    gwr[y] = gws[y]
    all_in(3, re)
    es[...] = mm(gt[...], re[...], 1, 0).astype(BF16).reshape(4, 64, 256)
    es_of = lambda peer: es.at[peer]
    start3(y_copy, 3, es_of, er)
    er[y] = es[y]

    mine = pl.ds(pl.multiple_of(y * 64, 64), 64)
    emb = (hidden_ref[...].astype(F32) * rcol[mine, 0:1] * gi).astype(BF16).astype(F32)
    rs_own = rscol[mine, 0:1]
    wait_in(y_from, 4, own_sdy, sdy)
    last = sdy[0] + sdy[1] + sdy[2] + sdy[3]
    sqm[...] = columns(2.0 * last[8:9] - (1.0 / D) * rs_all * rs_all * last[0:1])
    coef = sqm[mine, 0:1]
    direct = emb * coef
    wait_in(y_from, 2, gws_of, gwr)
    gw = (
        gwr[0].astype(F32) + gwr[1].astype(F32) + gwr[2].astype(F32) + gwr[3].astype(F32)
    ) * gu * rs_own + direct
    wait_in(y_from, 3, es_of, er)
    for h in range(8):
        lanes = slice(h * HD, (h + 1) * HD)
        par, q = h // 4, h % 4
        grad_ref[:, lanes] = er[q, :, halves[par]].astype(F32) + gw[:, lanes]

    for k, src, dst in (
        (0, own_hd, hd), (1, own_sel, selb), (2, gws_of, gwr), (3, es_of, er), (4, own_sdy, sdy),
        (5, own_sqy, sqy),
    ):
        wait_out(y_copy, k, src, dst)
    for k, src, dst in (
        (0, own_sqx, sqx), (5, own_sdx, sdx)
    ):
        wait_out(x_copy, k, src, dst)
    for part in range(2):
        for j in (1, 3, 2):
            for copy in dq_copy(part, j):
                copy.wait_send()
    for j in (1, 3, 2):
        for par in range(2):
            ps_copy((t + j) % NT * 2 + par).wait_send()
    for u in range(4):
        for j in (1, 3, 2):
            st_copy(u, j).wait_send()
    for stream in range(4):
        for step in range(RING[stream]):
            ring(stream, step).wait_send()
    for b in range(NZ):
        for half in range(2):
            partner(b, c, half).wait_send()
    most = pl.ds(0, (NS - 1) * 16)
    all_out(0, oute.at[most])
    all_out(1, outq.at[most, halves[0]])
    all_out(4, outq.at[most, halves[1]])
    all_out(2, rq.at[most])
    all_out(3, re.at[most])
    all_out(5, sqi.at[pl.ds(0, 15)])
    all_out(6, sci.at[pl.ds(0, 15)])


def local(item_hidden, item_gain, send_item, pos_slot, hist_len, user_gain, query_weight):
    vmem = pltpu.VMEM
    dma = pltpu.SemaphoreType.DMA
    quarter = lambda kind: vmem((4, 256, 256), kind)
    grad, loss = pl.pallas_call(
        kernel,
        out_shape=(
            jax.ShapeDtypeStruct((64, 1024), F32),
            jax.ShapeDtypeStruct((4, 1, HIST), F32),
        ),
        in_specs=[pl.BlockSpec(memory_space=pltpu.SMEM)]
        + [pl.BlockSpec(memory_space=pltpu.VMEM)] * 6,
        out_specs=(
            pl.BlockSpec(memory_space=pltpu.VMEM),
            pl.BlockSpec(memory_space=pltpu.VMEM),
        ),
        scratch_shapes=[
            vmem((4, 64, 1024), BF16),
            vmem((4, 1, 1024), F32),
            vmem((8, 2, 64, 1024), BF16),
            vmem((4, 16, HIST), F32),
            vmem((4, 8, HIST), F32),
            vmem((8, 256, HD), BF16),
            vmem((4, 2, 256, HD), BF16),
            vmem((1024, 256), BF16),
            vmem((1024, 256), BF16),
            quarter(BF16),
            quarter(BF16),
            vmem((256, 1024), BF16),
            quarter(BF16),
            quarter(BF16),
            vmem((8, 1, HIST), F32),
            vmem((16, 1, HIST), F32),
            vmem((256, HIST), F32),
            vmem((256, HIST), F32),
            vmem((256, 256), F32),
            vmem((256, HIST), F32),
            vmem((256, HIST), F32),
            vmem((4, 2 * HIST), jnp.int32),
            vmem((256, 1024), BF16),
            vmem((1024, 256), BF16),
            vmem((512, HIST), F32),
            vmem((4, 1, HIST), F32),
            vmem((4, 1, 256), F32),
            vmem((4, 1024, 256), BF16),
            vmem((4, 512, 256), BF16),
            vmem((4, 512, 256), BF16),
            vmem((4, 512, 256), BF16),
            vmem((8, 512, HIST), BF16),
            vmem((8, 512, HIST), BF16),
            vmem((8, HIST, HIST), F32),
            vmem((8, HIST, HIST), BF16),
            vmem((4, 512, 256), F32),
            vmem((4, 4, HIST, HIST), BF16),
            vmem((4, 2, HIST, HIST), F32),
            vmem((4, HIST, HIST), BF16),
            vmem((4, HIST, HIST), BF16),
            vmem((512, HIST), F32),
            vmem((4, 1, HIST), F32),
            vmem((512, 256), BF16),
            vmem((512, 256), BF16),
            vmem((4, 512, 256), BF16),
            vmem((4, 512, 256), BF16),
            vmem((4, 1024, 256), BF16),
            vmem((256, HIST), F32),
            quarter(BF16),
            quarter(BF16),
            vmem((1024, 256), BF16),
            vmem((1024, 256), BF16),
            vmem((16, 1, 256), F32),
            vmem((16, 1, 256), F32),
            vmem((4, 4, 64, 256), BF16),
            vmem((4, 64, 1024), BF16),
            vmem((4, 64, 1024), BF16),
            vmem((4, 64, 256), BF16),
            vmem((4, 64, 256), BF16),
            vmem((4, 8, 256), F32),
            vmem((4, 16, 256), F32),
            dma((11, 4)),
            dma((11, 4)),
            dma((6, 4)),
            dma((6, 4)),
            dma((4, 4)),
            dma((4, 4)),
            dma((8, 2)),
            dma((8, 2)),
            dma((7,)),
            dma((7,)),
            dma((8,)),
            dma((4, 2)),
            pltpu.SemaphoreType.REGULAR((2, 4)),
        ],
        compiler_params=pltpu.CompilerParams(
            collective_id=0, has_side_effects=True, vmem_limit_bytes=40 * 1024 * 1024
        ),
    )(
        hist_len, item_hidden, query_weight.T, item_gain, user_gain, send_item[0].T, pos_slot
    )
    return (grad, loss[:, 0, 0])


def solution(mesh):
    placed = (
        P("sect", "tp"),
        P("tp"),
        P("sect", None, None),
        P("sect", None),
        P("sect"),
        P("tp"),
        P("tp", "sect"),
    )
    return jax.shard_map(
        local, mesh=mesh, in_specs=placed, out_specs=(P("sect", "tp"), P("sect")), check_vma=False
    )
```

```python
import jax
import jax.numpy as jnp
from jax import lax
from jax.experimental import pallas as pl
from jax.experimental.pallas import tpu as pltpu
from jax.sharding import PartitionSpec as P

D = 4096
HD = 128
HIST = 128
CAND = 64
NZ, NY, NT = 8, 4, 4
NS = 64
EPS = 1e-06
SOFT = 20.0
F32, BF16 = jnp.float32, jnp.bfloat16
MESH = pl.DeviceIdType.MESH
RING = (4, 3, 3, 4)


def mm(a, b, ca, cb, precision=None):
    return lax.dot_general(
        a, b, (((ca,), (cb,)), ((), ())), preferred_element_type=F32, precision=precision
    )


def split3(values):
    high = values.astype(BF16)
    rest = values - high.astype(F32)
    mid = rest.astype(BF16)
    return high, mid, (rest - mid.astype(F32)).astype(BF16)


def row_parts(row):
    parts = split3(jnp.broadcast_to(row, (8, row.shape[1])))
    index = iota((8, row.shape[1]), 0)
    out = jnp.where(index == 0, parts[0].astype(F32), 0.0)
    out = jnp.where(index == 1, parts[1].astype(F32), out)
    return jnp.where(index == 2, parts[2].astype(F32), out).astype(BF16)


def lane_parts(values):
    parts = split3(values)
    index = iota(values.shape, 1)
    out = jnp.where(index == 0, parts[0].astype(F32), 0.0)
    out = jnp.where(index == 1, parts[1].astype(F32), out)
    return jnp.where(index == 2, parts[2].astype(F32), out).astype(BF16)


def columns(row):
    return mm(row_parts(row), jnp.ones((8, 128), BF16), 0, 0)


def row_sums(values):
    ones = jnp.ones((8, values.shape[1]), BF16)
    high, mid, low = split3(values)
    return mm(ones, high, 1, 1) + mm(ones, mid, 1, 1) + mm(ones, low, 1, 1)


def lane_sum(values):
    return jnp.sum(values, axis=1, keepdims=True)


def iota(shape, dim):
    return lax.broadcasted_iota(jnp.int32, shape, dim)


def one_hot(row, count):
    return jnp.where(iota((count, row.shape[1]), 0) == row, 1.0, 0.0)


def norm_heads(values):
    heads, roots = [], []
    for par in range(2):
        part = values[:, par * HD : (par + 1) * HD]
        root = lax.rsqrt(lane_sum(part * part) * (1.0 / HD) + EPS)
        heads.append(part * root)
        roots.append(root)
    return heads, roots


def norm_heads_back(values, grads):
    heads, roots = norm_heads(values)
    out = []
    for par in range(2):
        grad = grads[:, par * HD : (par + 1) * HD]
        out.append(
            roots[par] * (grad - heads[par] * (lane_sum(grad * heads[par]) * (1.0 / HD)))
        )
    return jnp.concatenate(out, axis=1)


def kernel(
    len_in, hidden_in, w_in, gi_in, gu_in, send_in, pos_in,
    grad_ref, loss_ref,
    len_ref, hidden_ref, gi_ref, gu_ref, send_ref, pos_ref, in_sem,
    hd, selb, wt, sqx, sqy, ps, pr, oute, outq, bufe, bufq, gt, nrm, knb, sqo, sqi, sqm, rsm, q32,
    rcol, rscol, pos_s, hot, hott, sqf_s, sqc_s, gain_s,
    rc_s, kn_s, v_s, qn_s, w_s, wt_s, p_t, ds_t, o_s, st_r, dsc, dneg_s, dnegt_s, gfol, grow,
    dout_t, dq_t, dk_s, dv_s, drc_s, nbs, dqo, eo, rq, re, sco, sci,
    dqg, gws, gwr, es, er, sdx, sdy,
    xs, xr, ys, yr, ring_s, ring_r, par_s, par_r, a2a_s, a2a_r, ps_s, ps_r, hello,
):
    me = lax.axis_index("sect")
    t = lax.axis_index("tp")
    z, y, c = me // 8, (me // 2) % 4, me % 2
    blk = z * 2 + c

    def send(src, dst, ssem, rsem, sect, tp):
        return pltpu.make_async_remote_copy(
            src_ref=src, dst_ref=dst, send_sem=ssem, recv_sem=rsem,
            device_id=(sect, tp), device_id_type=MESH,
        )

    def sect_of(zz, yy, cc):
        return zz * 8 + yy * 2 + cc

    def x_copy(k, src, dst, j):
        peer = (t + j) % NT
        return send(src(peer), dst.at[t], xs.at[k, peer], xr.at[k, t], me, peer)

    def x_from(k, src, dst, j):
        sender = (t + NT - j) % NT
        return send(src(t), dst.at[sender], xs.at[k, sender], xr.at[k, sender], me, sender)

    def y_copy(k, src, dst, j):
        peer = (y + j) % NY
        return send(src(peer), dst.at[y], ys.at[k, peer], yr.at[k, y], sect_of(z, peer, c), t)

    def y_from(k, src, dst, j):
        sender = (y + NY - j) % NY
        return send(
            src(y), dst.at[sender], ys.at[k, sender], yr.at[k, sender], sect_of(z, sender, c), t
        )

    def start3(copy, k, src, dst):
        for j in (2, 1, 3):
            copy(k, src, dst, j).start()

    def wait_in(came, k, src, dst):
        for j in (1, 3, 2):
            came(k, src, dst, j).wait_recv()

    def wait_out(copy, k, src, dst):
        for j in (1, 3, 2):
            copy(k, src, dst, j).wait_send()

    def rows_of(first):
        return pl.ds(pl.multiple_of(first * 16, 16), 16)

    def to_readers(k, out, buf, lanes):
        pltpu.make_async_copy(
            out.at[rows_of(me), lanes], buf.at[y, rows_of(blk), lanes], a2a_r.at[k]
        ).start()

        def step(j, carry):
            peer = (me + j) % NS
            send(
                out.at[rows_of(peer), lanes], buf.at[y, rows_of(blk), lanes],
                a2a_s.at[k], a2a_r.at[k], peer, t,
            ).start()
            return carry

        lax.fori_loop(1, NS, step, 0, unroll=7)

    def to_group(k, out, buf, group, same):
        def copy(j):
            b = (blk + j) % 16
            return send(
                out.at[group, rows_of(b)], buf.at[rows_of(me)],
                a2a_s.at[k], a2a_r.at[k], sect_of(b // 2, group, b % 2), t,
            )

        @pl.when(same)
        def _():
            pltpu.make_async_copy(
                out.at[group, rows_of(blk)], buf.at[rows_of(me)], a2a_r.at[k]
            ).start()

        @pl.when(jnp.logical_not(same))
        def _():
            copy(0).start()

        def step(j, carry):
            copy(j).start()
            return carry

        lax.fori_loop(1, 16, step, 0, unroll=5)

    def to_matched(k, src_of, dst):
        pltpu.make_async_copy(src_of(blk), dst.at[blk], a2a_r.at[k]).start()

        def step(j, carry):
            b = (blk + j) % 16
            send(
                src_of(b), dst.at[blk], a2a_s.at[k], a2a_r.at[k], sect_of(b // 2, y, b % 2), t
            ).start()
            return carry

        lax.fori_loop(1, 16, step, 0, unroll=5)

    def all_in(k, view):
        pltpu.make_async_copy(view, view, a2a_r.at[k]).wait()

    def all_out(k, view):
        pltpu.make_async_copy(view, view, a2a_s.at[k]).wait()

    def ring(stream, step):
        way = 1 if stream < 2 else NZ - 1
        block = (z + (NZ - way) * step) % NZ
        part = wt.at[block, c, pl.ds((stream % 2) * 32, 32)]
        return send(
            part, part, ring_s.at[stream, step], ring_r.at[stream, step],
            sect_of((z + way) % NZ, y, c), t,
        )

    def ring_from(stream, step):
        way = 1 if stream < 2 else NZ - 1
        block = (z + (NZ - way) * (step + 1)) % NZ
        part = wt.at[block, c, pl.ds((stream % 2) * 32, 32)]
        return block, send(
            part, part, ring_s.at[stream, step], ring_r.at[stream, step],
            sect_of((z + way) % NZ, y, c), t,
        )

    def partner(block, core, half):
        part = wt.at[block, core, pl.ds(half * 32, 32)]
        return send(
            part, part, par_s.at[block, half], par_r.at[block, half], sect_of(z, y, 1 - c), t
        )

    def partner_in(block, half):
        partner(block, 1 - c, half).wait_recv()

    def advance(step):
        for stream in (0, 2, 1, 3):
            if step >= RING[stream]:
                continue
            block, came = ring_from(stream, step)
            came.wait_recv()
            if step + 1 < RING[stream]:
                ring(stream, step + 1).start()
            partner(block, c, stream % 2).start()

    barrier = pltpu.get_barrier_semaphore()
    for j in range(1, 8):
        pl.semaphore_signal(
            barrier, inc=1, device_id=(z * 8 + (me + j) % 8, t), device_id_type=MESH
        )
    for j in (1, NZ - 1):
        pl.semaphore_signal(
            barrier, inc=1, device_id=(sect_of((z + j) % NZ, y, c), t), device_id_type=MESH
        )
    for j in range(1, NT):
        pl.semaphore_signal(barrier, inc=1, device_id=(me, (t + j) % NT), device_id_type=MESH)

    loads = [
        pltpu.make_async_copy(src, dst, in_sem.at[k])
        for k, (src, dst) in enumerate(
            (
                (send_in, send_ref), (w_in, wt.at[z, c]), (hidden_in, hd.at[y]),
                (gi_in, gi_ref), (gu_in, gu_ref), (hidden_in, hidden_ref), (pos_in, pos_ref),
                (len_in, len_ref),
            )
        )
    ]
    for load in loads:
        load.start()
    for load in loads:
        load.wait()
    sqx[t] = jnp.zeros((16, HIST), F32)
    spread = jnp.where((iota((64, 1024), 1) >> 4) == iota((64, 1024), 0), 1.0, 0.0).astype(BF16)
    named = mm(send_ref[...].astype(F32).astype(BF16), spread, 1, 0)
    lane = iota((1, 1024), 1)
    pick = jnp.full((1, 1024), -1.0, F32)
    for s in range(4):
        pick = jnp.where((lane & 3) == s, named[s : s + 1], pick)
    base = (jnp.zeros((1, 1024), jnp.int32) + y * 64).astype(F32)
    selb[y] = jnp.where((((lane >> 2) & 3) == y) & (pick >= 0.0), pick + base, -1.0)
    pl.semaphore_wait(barrier, 7 + 2 + NT - 1)

    def greet(step):
        for way in range(2):
            if step < 4 - way:
                peer = (z + 1) % NZ if way == 0 else (z + NZ - 1) % NZ
                pl.semaphore_signal(
                    hello.at[way, step], inc=1, device_id=(sect_of(peer, y, c), t),
                    device_id_type=MESH,
                )

    def relay(step):
        for way in range(2):
            if step < 4 - way:
                pl.semaphore_wait(hello.at[way, step], 1)
        greet(step + 1)

    greet(0)
    own_hd = lambda peer: hd.at[y]
    own_sel = lambda peer: selb.at[y]
    for stream in (0, 2, 1, 3):
        ring(stream, 0).start()
    start3(y_copy, 0, own_hd, hd)
    start3(y_copy, 1, own_sel, selb)
    for half in range(2):
        partner(z, c, half).start()

    gi = gi_ref[...].astype(F32).reshape(1, 1024)
    gu = gu_ref[...].astype(F32).reshape(1, 1024)
    hidden = hidden_ref[...].astype(F32)
    gained = hidden * gi
    sqx[t, pl.ds(0, 8), 0:64] = row_sums(hidden * hidden)
    sqx[t, pl.ds(8, 8), 0:64] = row_sums(gained * gained)
    own_sqx = lambda peer: sqx.at[t]
    start3(x_copy, 0, own_sqx, sqx)

    slots = pos_ref[...]
    owner = slots >> 2
    pos_s[...] = jnp.full(pos_s.shape, -1, jnp.int32)
    pos_s[:, 0 : HIST + CAND] = (
        ((owner >> 3) << 5) | ((owner & 1) << 4) | (((owner >> 1) & 3) << 2) | (slots & 3)
    )
    for u in range(4):
        for kind in range(2):
            row = pos_s[u : u + 1, kind * HIST : (kind + 1) * HIST]
            picked = one_hot(row, 256)
            first = (4 * kind + u) * HIST
            hot[:, first : first + HIST] = picked.astype(BF16)
            hott[first : first + HIST, :] = jnp.transpose(picked).astype(BF16)

    advance(0)
    relay(0)
    wait_in(x_from, 0, own_sqx, sqx)
    sums = sqx[0] + sqx[1] + sqx[2] + sqx[3]
    r_row = lax.rsqrt(sums[0:1] * (1.0 / D) + EPS)
    sq_item = r_row * r_row * sums[8:9]
    rs_row = lax.rsqrt(sq_item * (1.0 / D) + EPS)
    sqy[y] = jnp.concatenate([r_row, rs_row, sq_item] + [r_row] * 5, axis=0)
    own_sqy = lambda peer: sqy.at[y]
    start3(y_copy, 5, own_sqy, sqy)
    relay(1)
    advance(1)
    relay(2)
    wait_in(y_from, 0, own_hd, hd)
    lhs = (hd[...].reshape(256, 1024).astype(F32) * (gi * gu)).astype(BF16)

    def ps_copy(block):
        part, par = block // 2, block % 2
        return send(
            ps.at[block], pr.at[t, par], ps_s.at[block], ps_r.at[t, par], me, part
        )

    def project(block):
        ps[block] = mm(lhs, wt[block].reshape(HD, 1024), 1, 1).astype(BF16)

        @pl.when(block // 2 != t)
        def _():
            ps_copy(block).start()

    def project_step(step):
        if step == 0:
            project(z)
        for way in (1, NZ - 1)[: 2 if step < 3 else 1]:
            project((z + way * (step + 1)) % NZ)

    def partners_in(step):
        if step == 0:
            for half in range(2):
                partner_in(z, half)
        for stream in range(4):
            if step < RING[stream]:
                way = 1 if stream < 2 else NZ - 1
                partner_in((z + (NZ - way) * (step + 1)) % NZ, stream % 2)

    partners_in(0)
    project_step(0)
    wait_in(y_from, 1, own_sel, selb)
    picks = jnp.maximum(jnp.maximum(selb[0], selb[1]), jnp.maximum(selb[2], selb[3]))
    gt[...] = one_hot(picks.astype(jnp.int32), 256).astype(BF16)
    wait_in(y_from, 5, own_sqy, sqy)
    rcol[...] = jnp.concatenate([columns(sqy[b, 0:1])[0:64] for b in range(4)], axis=0)
    rscol[...] = jnp.concatenate([columns(sqy[b, 1:2])[0:64] for b in range(4)], axis=0)
    sq_out = jnp.zeros((8, 1024), F32)
    for b in range(4):
        sq_out = sq_out + mm(
            row_parts(sqy[b, 2:3])[:, 0:64], gt[b * 64 : (b + 1) * 64, :], 1, 0
        )
    sq_out = jnp.sum(sq_out, axis=0, keepdims=True)
    for b in range(NZ):
        sqo[b] = sq_out[:, b * HD : (b + 1) * HD]
    pieces = []
    for par in range(2):
        head = par * 4 + y
        lanes = pl.ds(pl.multiple_of(head * HD, HD), HD)
        piece = hd[:, :, lanes].reshape(256, HD).astype(F32)
        gain = jnp.zeros((1, HD), F32)
        for h in range(8):
            gain = gain + jnp.where(head == h, gi[:, h * HD : (h + 1) * HD], 0.0)
        pieces.append((piece * rcol[...] * gain).astype(BF16))
    oute[...] = mm(gt[...], jnp.concatenate(pieces, axis=1), 0, 0).astype(BF16)
    partners_in(1)
    project_step(1)
    advance(2)
    relay(3)
    both = slice(0, 256)
    to_matched(5, lambda b: sqo.at[b // 2], sqi)
    to_readers(0, oute, bufe, both)
    partners_in(2)
    project_step(2)
    advance(3)
    partners_in(3)
    project_step(3)
    for q in range(4):
        gain_s[q] = jnp.concatenate(
            [gu[:, q * HD : (q + 1) * HD], gu[:, (4 + q) * HD : (5 + q) * HD]], axis=1
        )
    for par in range(2):
        pr[t, par] = ps[2 * t + par]
    for par in range(2):
        for j in (1, 3, 2):
            sender = (t + j) % NT
            send(
                ps.at[2 * t + par], pr.at[sender, par], ps_s.at[2 * t + par],
                ps_r.at[sender, par], me, sender,
            ).wait_recv()
    total = jnp.concatenate(
        [
            pr[0, par].astype(F32) + pr[1, par].astype(F32)
            + pr[2, par].astype(F32) + pr[3, par].astype(F32)
            for par in range(2)
        ],
        axis=1,
    ) * (rcol[...] * rscol[...])[:, 0:1]
    q32[...] = total
    heads, _ = norm_heads(total)
    outq[...] = mm(gt[...], jnp.concatenate(heads, axis=1).astype(BF16), 0, 0).astype(BF16)
    halves = (slice(0, HD), slice(HD, 2 * HD))
    to_readers(1, outq, bufq, halves[0])
    to_readers(4, outq, bufq, halves[1])

    off = (me % 8) * 16
    blocks = jnp.where((iota((256, 16), 0) >> 4) == iota((256, 16), 1), 1.0, 0.0).astype(BF16)
    in_lane = iota((256, HD), 1) == off + (iota((256, HD), 0) & 15)
    all_in(5, sqi)
    came = jnp.concatenate([sqi[b] for b in range(16)], axis=0)
    high, mid, low = split3(came)
    wide = mm(blocks, high, 1, 0) + mm(blocks, mid, 1, 0) + mm(blocks, low, 1, 0)
    sqm[...] = jnp.broadcast_to(lane_sum(jnp.where(in_lane, wide, 0.0)), (256, HD))
    rsm[...] = lax.rsqrt(sqm[...] * (1.0 / D) + EPS)
    sqf_s[...] = jnp.broadcast_to(
        lane_sum(mm(hott[0:512], lane_parts(sqm[...]), 1, 0)), (512, HIST)
    )
    sqc = jnp.sum(mm(lane_parts(sqm[...]), hot[:, 512:1024], 0, 0), axis=0, keepdims=True)
    for u in range(4):
        sqc_s[u] = sqc[:, u * HIST : (u + 1) * HIST]
    twice = lambda values: jnp.concatenate([values, values], axis=1)
    all_in(0, bufe)
    for q in range(4):
        low = (bufe[q].astype(F32) * twice(rsm[...]) * gain_s[q]).astype(BF16)
        nrm[q] = low
        heads, _ = norm_heads(low.astype(F32))
        knb[q] = jnp.concatenate(heads, axis=1).astype(BF16)
    for q in range(4):
        kn_s[q] = mm(hott[0:512], knb[q], 1, 0).astype(BF16)
        v_s[q] = mm(hott[0:512], nrm[q], 1, 0).astype(BF16)
    for q in range(4):
        rc_s[q] = mm(hott[...], bufe[q], 1, 0).astype(BF16)

    scale = HD ** (-0.5)
    row_id = iota((HIST, HIST), 0)
    col_id = iota((HIST, HIST), 1)

    def follow_of(rows):
        moved = pltpu.roll(rows, HIST - 1, 0)
        return jnp.where(iota(rows.shape, 0) < HIST - 1, moved, 0.0)

    def st_copy(u, j):
        peer = (t + j) % NT
        return send(st_r.at[t, u], st_r.at[t, u], xs.at[6 + u, peer], xr.at[6 + u, t], me, peer)

    def st_from(u, j):
        sender = (t + NT - j) % NT
        return send(
            st_r.at[t, u], st_r.at[sender, u], xs.at[6 + u, sender], xr.at[6 + u, sender],
            me, sender,
        )

    def user_rows(u):
        return pl.ds(pl.multiple_of(u * HIST, HIST), HIST)

    def attend(first, par):
        lanes = halves[par]
        tasks = [(first + k, q, 4 * k + q) for k in range(2) for q in range(4)]
        for u, q, slot in tasks:
            span = user_rows(u)
            p_t[slot] = mm(qn_s[q, span, lanes], kn_s[q, span, lanes], 1, 1)
        for u, q, slot in tasks:
            mask = (col_id <= row_id) & (col_id < len_ref[u])
            weights = jnp.where(mask, jnp.exp(p_t[slot] * scale), 0.0)
            w_s[2 * q + par, user_rows(u)] = (weights * (1.0 / lane_sum(weights))).astype(BF16)
        for u, q, slot in tasks:
            span = user_rows(u)
            o_s[q, span, lanes] = rc_s[q, span, lanes].astype(F32) + mm(
                w_s[2 * q + par, span], v_s[q, span, lanes], 1, 0
            )

    def first_half(i, carry):
        attend(2 * i, 0)
        return carry

    def score(u):
        span = user_rows(u)
        cspan = user_rows(u + 4)
        own = jnp.zeros((HIST, 1), F32)
        hit = jnp.zeros((HIST, 1), F32)
        neg = jnp.zeros((HIST, HIST), F32)
        for q in range(4):
            out = o_s[q, span]
            own = own + lane_sum(out * out)
            hit = hit + lane_sum(out * follow_of(rc_s[q, span].astype(F32)))
            high = out.astype(BF16)
            low = (out - high.astype(F32)).astype(BF16)
            cands = rc_s[q, cspan]
            neg = neg + mm(high, cands, 1, 1) + mm(low, cands, 1, 1)
        stats = neg + jnp.where(col_id == CAND, own, 0.0) + jnp.where(col_id == CAND + 1, hit, 0.0)
        st_r[t, u] = stats.astype(BF16)
        for j in (2, 1, 3):
            st_copy(u, j).start()

    def second_half(i, carry):
        attend(2 * i, 1)
        score(2 * i)
        score(2 * i + 1)
        return carry

    def turn_weights(k, carry):
        for u in range(4):
            span = slice(u * HIST, (u + 1) * HIST)
            wt_s[k, span] = jnp.transpose(w_s[k, span].astype(F32)).astype(BF16)
        return carry

    for par, step in ((0, first_half), (1, second_half)):
        all_in(1 if par == 0 else 4, outq.at[:, halves[0]])
        for q in range(4):
            qn_s[q, :, halves[par]] = mm(hott[0:512], bufq[q, :, halves[par]], 1, 0).astype(BF16)
        lax.fori_loop(0, 2, step, 0)
    lax.fori_loop(0, 8, turn_weights, 0)

    def losses(u, carry):
        for j in (1, 3, 2):
            st_from(u, j).wait_recv()
        stats = (
            st_r[0, u].astype(F32) + st_r[1, u].astype(F32)
            + st_r[2, u].astype(F32) + st_r[3, u].astype(F32)
        )
        is_cand = col_id < CAND
        neg = jnp.where(is_cand, stats, 0.0)
        own = lane_sum(jnp.where(col_id == CAND, stats, 0.0))
        hit = lane_sum(jnp.where(col_id == CAND + 1, stats, 0.0))
        sq_follow = pltpu.roll(sqf_s[user_rows(u)], HIST - 1, 0)[:, 0:1]
        rn = lax.rsqrt(own + EPS)
        rf = lax.rsqrt(sq_follow + EPS)
        rc = lax.rsqrt(sqc_s[u] + EPS)
        tl = SOFT * hit * rn * rf
        nl = SOFT * neg * rn * rc
        en = jnp.where(is_cand, jnp.exp(nl), 0.0)
        et = jnp.exp(tl)
        whole = et + lane_sum(en)
        span = len_ref[u] - 1
        over = 1.0 / (jnp.full((HIST, 1), 0, jnp.int32) + span).astype(F32)
        valid = iota((HIST, 1), 0) < span
        terms = jnp.where(valid, (jnp.log(whole) - tl) * over, 0.0)
        loss_ref[u] = jnp.broadcast_to(jnp.sum(terms, axis=0, keepdims=True), (1, HIST))
        g = jnp.where(valid, float(D) * over, 0.0)
        dtl = g * (et / whole - 1.0)
        dnl = (g / whole) * en
        dsc[u, 0] = jnp.broadcast_to(
            -rn * rn * (dtl * tl + lane_sum(dnl * nl)), (HIST, HIST)
        )
        dsc[u, 1] = jnp.broadcast_to(dtl * (SOFT * rn * rf), (HIST, HIST))
        dneg = dnl * (SOFT * rn * rc)
        dneg_s[u] = dneg.astype(BF16)
        dnegt_s[u] = jnp.transpose(dneg).astype(BF16)
        dsqf = jnp.broadcast_to(-0.5 * dtl * tl * rf * rf, (HIST, HIST))
        gfol[user_rows(u)] = pltpu.roll(dsqf, 1, 0)
        grow[u] = -0.5 * rc * rc * jnp.sum(dnl * nl, axis=0, keepdims=True)
        return carry

    lax.fori_loop(0, 4, losses, 0)

    def backward_quarter(i, carry):
        q = (y + 1 + i) % 4
        for u in range(4):
            span = slice(u * HIST, (u + 1) * HIST)
            cspan = slice((4 + u) * HIST, (5 + u) * HIST)
            dhit = twice(dsc[u, 1])
            out = o_s[q, span]
            rows = rc_s[q, span].astype(F32)
            dout = (
                twice(dsc[u, 0]) * out
                + dhit * follow_of(rows)
                + mm(dneg_s[u], rc_s[q, cspan], 1, 0)
            )
            dout_t[span] = dout.astype(BF16)
            drc_s[q, span] = (dout + pltpu.roll(dhit * out, 1, 0)).astype(BF16)
            drc_s[q, cspan] = mm(dnegt_s[u], out.astype(BF16), 1, 0).astype(BF16)
        tasks = [
            (slice(u * HIST, (u + 1) * HIST), halves[par], par, 2 * u + par)
            for u in range(4)
            for par in range(2)
        ]
        for span, lanes, par, slot in tasks:
            p_t[slot] = mm(dout_t[span, lanes], v_s[q, span, lanes], 1, 1)
        for span, lanes, par, slot in tasks:
            dw = p_t[slot]
            wide = w_s[2 * q + par, span].astype(F32)
            ds_t[slot] = (wide * (dw - lane_sum(dw * wide)) * scale).astype(BF16)
        for span, lanes, par, slot in tasks:
            dq_t[span, lanes] = mm(ds_t[slot], kn_s[q, span, lanes], 1, 0).astype(BF16)
            dk_s[q, span, lanes] = mm(ds_t[slot], qn_s[q, span, lanes], 0, 0).astype(BF16)
            dv_s[q, span, lanes] = mm(wt_s[2 * q + par, span], dout_t[span, lanes], 1, 0).astype(
                BF16
            )
        dqo[q] = mm(hot[:, 0:512], dq_t[...], 1, 0).astype(BF16)
        to_group(2, dqo, rq, q, i == 3)
        return carry

    lax.fori_loop(0, 4, backward_quarter, 0)

    nbs[...] = jnp.zeros(nbs.shape, F32)

    def return_quarter(i, carry):
        q = (y + 1 + i) % 4
        dk = mm(hot[:, 0:512], dk_s[q], 1, 0)
        dn = mm(hot[:, 0:512], dv_s[q], 1, 0) + norm_heads_back(nrm[q].astype(F32), dk)
        dn = dn * gain_s[q]
        nbs[...] += jnp.broadcast_to(lane_sum(dn * bufe[q].astype(F32)), (256, HD))
        eo[q] = (mm(hot[...], drc_s[q], 1, 0) + dn * twice(rsm[...])).astype(BF16)
        return carry

    lax.fori_loop(0, 4, return_quarter, 0)
    gsq = lane_sum(mm(hot[:, 0:512], lane_parts(gfol[...]), 1, 0)) + lane_sum(
        mm(
            hot[:, 512:1024],
            row_parts(jnp.concatenate([grow[u] for u in range(4)], axis=1)), 1, 1,
        )
    )
    placed = []
    for values in (jnp.broadcast_to(gsq, (256, HD)), nbs[...]):
        high, mid, low = split3(jnp.where(in_lane, values, 0.0))
        placed.append(mm(blocks, high, 0, 0) + mm(blocks, mid, 0, 0) + mm(blocks, low, 0, 0))
    for b in range(16):
        sco[b] = jnp.concatenate([part[b : b + 1] for part in placed], axis=1)
    to_matched(6, lambda b: sco.at[b], sci)

    def return_group(i, carry):
        to_group(3, eo, re, (y + 1 + i) % 4, i == 3)
        return carry


    all_in(6, sci)
    pairs = [sci[2 * b] + sci[2 * b + 1] for b in range(NZ)]
    item_terms = []
    for lanes in (slice(0, HD), slice(HD, 2 * HD)):
        row = jnp.concatenate([pair[:, lanes] for pair in pairs], axis=1)
        item_terms.append(jnp.sum(mm(row_parts(row), gt[...], 1, 1), axis=0, keepdims=True))
    sdy[y, pl.ds(8, 8), :] = jnp.broadcast_to(item_terms[0], (8, 256))
    rs_all = mm(jnp.ones((8, HD), BF16), lane_parts(rscol[...]), 1, 1)[0:1]
    all_in(2, rq)
    lax.fori_loop(0, 4, return_group, 0)
    dq_item = norm_heads_back(q32[...], mm(gt[...], rq[...], 1, 0)).astype(BF16)
    dqg[t] = dq_item.reshape(4, 64, 256)
    chunks = (((y + 2) % NY, (y + 1) % NY), ((y + 3) % NY, y))

    def dq_copy(part, j):
        peer = (t + j) % NT
        return [
            send(
                dqg.at[t, b], dqg.at[t, b], xs.at[(2, 3, 4, 10)[2 * part + k], peer],
                xr.at[(2, 3, 4, 10)[2 * part + k], t], me, peer,
            )
            for k, b in enumerate(chunks[part])
        ]

    def dq_from(part, j):
        sender = (t + NT - j) % NT
        return [
            send(
                dqg.at[t, b], dqg.at[sender, b], xs.at[(2, 3, 4, 10)[2 * part + k], sender],
                xr.at[(2, 3, 4, 10)[2 * part + k], sender], me, sender,
            )
            for k, b in enumerate(chunks[part])
        ]

    sdx[t] = row_sums(dq_item.astype(F32) * q32[...]) + rs_all * item_terms[1]
    own_sdx = lambda peer: sdx.at[t]
    start3(x_copy, 5, own_sdx, sdx)
    for part in range(2):
        for j in (2, 1, 3):
            for copy in dq_copy(part, j):
                copy.start()
    gws_of = lambda peer: gws.at[peer]
    for part in range(2):
        for j in (1, 3, 2):
            for copy in dq_from(part, j):
                copy.wait_recv()
        acc = jnp.zeros((128, 1024), F32)
        for tt in range(NT):
            acc = acc + mm(
                jnp.concatenate([dqg[tt, b] for b in chunks[part]], axis=0),
                wt[2 * tt : 2 * tt + 2].reshape(256, 1024), 1, 0,
            )
        acc = acc.astype(BF16)
        for k, b in enumerate(chunks[part]):
            gws[b] = acc[k * 64 : (k + 1) * 64]
        if part == 0:
            wait_in(x_from, 5, own_sdx, sdx)
            sdy[y, pl.ds(0, 8), :] = sdx[0] + sdx[1] + sdx[2] + sdx[3]
            own_sdy = lambda peer: sdy.at[y]
            start3(y_copy, 4, own_sdy, sdy)
        for j in ((2, 1), (3,))[part]:
            y_copy(2, gws_of, gwr, j).start()
    gwr[y] = gws[y]
    all_in(3, re)
    es[...] = mm(gt[...], re[...], 1, 0).astype(BF16).reshape(4, 64, 256)
    es_of = lambda peer: es.at[peer]
    start3(y_copy, 3, es_of, er)
    er[y] = es[y]

    mine = pl.ds(pl.multiple_of(y * 64, 64), 64)
    emb = (hidden_ref[...].astype(F32) * rcol[mine, 0:1] * gi).astype(BF16).astype(F32)
    rs_own = rscol[mine, 0:1]
    wait_in(y_from, 4, own_sdy, sdy)
    last = sdy[0] + sdy[1] + sdy[2] + sdy[3]
    sqm[...] = columns(2.0 * last[8:9] - (1.0 / D) * rs_all * rs_all * last[0:1])
    coef = sqm[mine, 0:1]
    direct = emb * coef
    wait_in(y_from, 2, gws_of, gwr)
    gw = (
        gwr[0].astype(F32) + gwr[1].astype(F32) + gwr[2].astype(F32) + gwr[3].astype(F32)
    ) * gu * rs_own + direct
    wait_in(y_from, 3, es_of, er)
    for h in range(8):
        lanes = slice(h * HD, (h + 1) * HD)
        par, q = h // 4, h % 4
        grad_ref[:, lanes] = er[q, :, halves[par]].astype(F32) + gw[:, lanes]

    for k, src, dst in (
        (0, own_hd, hd), (1, own_sel, selb), (2, gws_of, gwr), (3, es_of, er), (4, own_sdy, sdy),
        (5, own_sqy, sqy),
    ):
        wait_out(y_copy, k, src, dst)
    for k, src, dst in (
        (0, own_sqx, sqx), (5, own_sdx, sdx)
    ):
        wait_out(x_copy, k, src, dst)
    for part in range(2):
        for j in (1, 3, 2):
            for copy in dq_copy(part, j):
                copy.wait_send()
    for j in (1, 3, 2):
        for par in range(2):
            ps_copy((t + j) % NT * 2 + par).wait_send()
    for u in range(4):
        for j in (1, 3, 2):
            st_copy(u, j).wait_send()
    for stream in range(4):
        for step in range(RING[stream]):
            ring(stream, step).wait_send()
    for b in range(NZ):
        for half in range(2):
            partner(b, c, half).wait_send()
    most = pl.ds(0, (NS - 1) * 16)
    all_out(0, oute.at[most])
    all_out(1, outq.at[most, halves[0]])
    all_out(4, outq.at[most, halves[1]])
    all_out(2, rq.at[most])
    all_out(3, re.at[most])
    all_out(5, sqi.at[pl.ds(0, 15)])
    all_out(6, sci.at[pl.ds(0, 15)])


def local(item_hidden, item_gain, send_item, pos_slot, hist_len, user_gain, query_weight):
    vmem = pltpu.VMEM
    dma = pltpu.SemaphoreType.DMA
    quarter = lambda kind: vmem((4, 256, 256), kind)
    grad, loss = pl.pallas_call(
        kernel,
        out_shape=(
            jax.ShapeDtypeStruct((64, 1024), F32),
            jax.ShapeDtypeStruct((4, 1, HIST), F32),
        ),
        in_specs=[pl.BlockSpec(memory_space=pltpu.HBM)] * 7,
        out_specs=(
            pl.BlockSpec(memory_space=pltpu.VMEM),
            pl.BlockSpec(memory_space=pltpu.VMEM),
        ),
        scratch_shapes=[
            pltpu.SMEM((4,), jnp.int32),
            vmem((64, 1024), BF16),
            vmem((1024,), BF16),
            vmem((1024,), BF16),
            vmem((4, 64), jnp.int32),
            vmem((4, HIST + CAND), jnp.int32),
            dma((8,)),
            vmem((4, 64, 1024), BF16),
            vmem((4, 1, 1024), F32),
            vmem((8, 2, 64, 1024), BF16),
            vmem((4, 16, HIST), F32),
            vmem((4, 8, HIST), F32),
            vmem((8, 256, HD), BF16),
            vmem((4, 2, 256, HD), BF16),
            vmem((1024, 256), BF16),
            vmem((1024, 256), BF16),
            quarter(BF16),
            quarter(BF16),
            vmem((256, 1024), BF16),
            quarter(BF16),
            quarter(BF16),
            vmem((8, 1, HIST), F32),
            vmem((16, 1, HIST), F32),
            vmem((256, HIST), F32),
            vmem((256, HIST), F32),
            vmem((256, 256), F32),
            vmem((256, HIST), F32),
            vmem((256, HIST), F32),
            vmem((4, 2 * HIST), jnp.int32),
            vmem((256, 1024), BF16),
            vmem((1024, 256), BF16),
            vmem((512, HIST), F32),
            vmem((4, 1, HIST), F32),
            vmem((4, 1, 256), F32),
            vmem((4, 1024, 256), BF16),
            vmem((4, 512, 256), BF16),
            vmem((4, 512, 256), BF16),
            vmem((4, 512, 256), BF16),
            vmem((8, 512, HIST), BF16),
            vmem((8, 512, HIST), BF16),
            vmem((8, HIST, HIST), F32),
            vmem((8, HIST, HIST), BF16),
            vmem((4, 512, 256), F32),
            vmem((4, 4, HIST, HIST), BF16),
            vmem((4, 2, HIST, HIST), F32),
            vmem((4, HIST, HIST), BF16),
            vmem((4, HIST, HIST), BF16),
            vmem((512, HIST), F32),
            vmem((4, 1, HIST), F32),
            vmem((512, 256), BF16),
            vmem((512, 256), BF16),
            vmem((4, 512, 256), BF16),
            vmem((4, 512, 256), BF16),
            vmem((4, 1024, 256), BF16),
            vmem((256, HIST), F32),
            quarter(BF16),
            quarter(BF16),
            vmem((1024, 256), BF16),
            vmem((1024, 256), BF16),
            vmem((16, 1, 256), F32),
            vmem((16, 1, 256), F32),
            vmem((4, 4, 64, 256), BF16),
            vmem((4, 64, 1024), BF16),
            vmem((4, 64, 1024), BF16),
            vmem((4, 64, 256), BF16),
            vmem((4, 64, 256), BF16),
            vmem((4, 8, 256), F32),
            vmem((4, 16, 256), F32),
            dma((11, 4)),
            dma((11, 4)),
            dma((6, 4)),
            dma((6, 4)),
            dma((4, 4)),
            dma((4, 4)),
            dma((8, 2)),
            dma((8, 2)),
            dma((7,)),
            dma((7,)),
            dma((8,)),
            dma((4, 2)),
            pltpu.SemaphoreType.REGULAR((2, 4)),
        ],
        compiler_params=pltpu.CompilerParams(
            collective_id=0, has_side_effects=True, vmem_limit_bytes=40 * 1024 * 1024
        ),
    )(
        *[
            pltpu.with_memory_space_constraint(value, pltpu.HBM)
            for value in (
                hist_len, item_hidden, query_weight.T, item_gain, user_gain, send_item[0].T,
                pos_slot,
            )
        ]
    )
    return (grad, loss[:, 0, 0])


def solution(mesh):
    placed = (
        P("sect", "tp"),
        P("tp"),
        P("sect", None, None),
        P("sect", None),
        P("sect"),
        P("tp"),
        P("tp", "sect"),
    )
    return jax.shard_map(
        local, mesh=mesh, in_specs=placed, out_specs=(P("sect", "tp"), P("sect")), check_vma=False
    )
```

```python
import jax
import jax.numpy as jnp
from jax import lax
from jax.experimental import pallas as pl
from jax.experimental.pallas import tpu as pltpu
from jax.sharding import PartitionSpec as P

D = 4096
HD = 128
HIST = 128
CAND = 64
NZ, NY, NT = 8, 4, 4
NS = 64
EPS = 1e-06
SOFT = 20.0
F32, BF16 = jnp.float32, jnp.bfloat16
MESH = pl.DeviceIdType.MESH
RING = (4, 3, 3, 4)


def mm(a, b, ca, cb, precision=None):
    return lax.dot_general(
        a, b, (((ca,), (cb,)), ((), ())), preferred_element_type=F32, precision=precision
    )


def split3(values):
    high = values.astype(BF16)
    rest = values - high.astype(F32)
    mid = rest.astype(BF16)
    return high, mid, (rest - mid.astype(F32)).astype(BF16)


def row_parts(row):
    parts = split3(jnp.broadcast_to(row, (8, row.shape[1])))
    index = iota((8, row.shape[1]), 0)
    out = jnp.where(index == 0, parts[0].astype(F32), 0.0)
    out = jnp.where(index == 1, parts[1].astype(F32), out)
    return jnp.where(index == 2, parts[2].astype(F32), out).astype(BF16)


def lane_parts(values):
    parts = split3(values)
    index = iota(values.shape, 1)
    out = jnp.where(index == 0, parts[0].astype(F32), 0.0)
    out = jnp.where(index == 1, parts[1].astype(F32), out)
    return jnp.where(index == 2, parts[2].astype(F32), out).astype(BF16)


def columns(row):
    return mm(row_parts(row), jnp.ones((8, 128), BF16), 0, 0)


def row_sums(values):
    ones = jnp.ones((8, values.shape[1]), BF16)
    high, mid, low = split3(values)
    return mm(ones, high, 1, 1) + mm(ones, mid, 1, 1) + mm(ones, low, 1, 1)


def lane_sum(values):
    return jnp.sum(values, axis=1, keepdims=True)


def iota(shape, dim):
    return lax.broadcasted_iota(jnp.int32, shape, dim)


def one_hot(row, count):
    return jnp.where(iota((count, row.shape[1]), 0) == row, 1.0, 0.0)


def norm_heads(values):
    heads, roots = [], []
    for par in range(2):
        part = values[:, par * HD : (par + 1) * HD]
        root = lax.rsqrt(lane_sum(part * part) * (1.0 / HD) + EPS)
        heads.append(part * root)
        roots.append(root)
    return heads, roots


def head_back(values, grad):
    root = lax.rsqrt(lane_sum(values * values) * (1.0 / HD) + EPS)
    head = values * root
    return root * (grad - head * (lane_sum(grad * head) * (1.0 / HD)))


def norm_heads_back(values, grads):
    heads, roots = norm_heads(values)
    out = []
    for par in range(2):
        grad = grads[:, par * HD : (par + 1) * HD]
        out.append(
            roots[par] * (grad - heads[par] * (lane_sum(grad * heads[par]) * (1.0 / HD)))
        )
    return jnp.concatenate(out, axis=1)


def kernel(
    len_in, hidden_in, w_in, gi_in, gu_in, send_in, pos_in,
    grad_ref, loss_ref,
    len_ref, hidden_ref, gi_ref, gu_ref, send_ref, pos_ref, in_sem,
    hd, selb, wt, sqx, sqy, ps, pr, oute, outq, bufe, bufq, gt, nrm, knb, sqo, sqi, sqm, rsm, q32,
    rcol, rscol, pos_s, hot, hott, sqf_s, sqc_s, gain_s,
    rc_s, kn_s, v_s, qn_s, w_s, wt_s, p_t, ds_t, o_s, st_r, dsc, dneg_s, dnegt_s, gfol, grow,
    dout_t, dq_t, dk_s, dv_s, drc_s, nbs, dqo, eo, rq, re, sco, sci,
    dqg, acc_s, gws, gwr, es, er, sdx, sdy,
    xs, xr, ys, yr, ring_s, ring_r, par_s, par_r, a2a_s, a2a_r, ps_s, ps_r, hello,
):
    me = lax.axis_index("sect")
    t = lax.axis_index("tp")
    z, y, c = me // 8, (me // 2) % 4, me % 2
    blk = z * 2 + c

    def send(src, dst, ssem, rsem, sect, tp):
        return pltpu.make_async_remote_copy(
            src_ref=src, dst_ref=dst, send_sem=ssem, recv_sem=rsem,
            device_id=(sect, tp), device_id_type=MESH,
        )

    def sect_of(zz, yy, cc):
        return zz * 8 + yy * 2 + cc

    def x_copy(k, src, dst, j):
        peer = (t + j) % NT
        return send(src(peer), dst.at[t], xs.at[k, peer], xr.at[k, t], me, peer)

    def x_from(k, src, dst, j):
        sender = (t + NT - j) % NT
        return send(src(t), dst.at[sender], xs.at[k, sender], xr.at[k, sender], me, sender)

    def y_copy(k, src, dst, j):
        peer = (y + j) % NY
        return send(src(peer), dst.at[y], ys.at[k, peer], yr.at[k, y], sect_of(z, peer, c), t)

    def y_from(k, src, dst, j):
        sender = (y + NY - j) % NY
        return send(
            src(y), dst.at[sender], ys.at[k, sender], yr.at[k, sender], sect_of(z, sender, c), t
        )

    def start3(copy, k, src, dst):
        for j in (2, 1, 3):
            copy(k, src, dst, j).start()

    def wait_in(came, k, src, dst):
        for j in (1, 3, 2):
            came(k, src, dst, j).wait_recv()

    def wait_out(copy, k, src, dst):
        for j in (1, 3, 2):
            copy(k, src, dst, j).wait_send()

    def rows_of(first):
        return pl.ds(pl.multiple_of(first * 16, 16), 16)

    def to_readers(k, out, buf, lanes):
        pltpu.make_async_copy(
            out.at[rows_of(me), lanes], buf.at[y, rows_of(blk), lanes], a2a_r.at[k]
        ).start()

        def step(j, carry):
            peer = (me + j) % NS
            send(
                out.at[rows_of(peer), lanes], buf.at[y, rows_of(blk), lanes],
                a2a_s.at[k], a2a_r.at[k], peer, t,
            ).start()
            return carry

        lax.fori_loop(1, NS, step, 0, unroll=7)

    def to_group(k, out, buf, group, same, lanes):
        def copy(j):
            b = (blk + j) % 16
            return send(
                out.at[group, rows_of(b), lanes], buf.at[rows_of(me), lanes],
                a2a_s.at[k], a2a_r.at[k], sect_of(b // 2, group, b % 2), t,
            )

        @pl.when(same)
        def _():
            pltpu.make_async_copy(
                out.at[group, rows_of(blk), lanes], buf.at[rows_of(me), lanes], a2a_r.at[k]
            ).start()

        @pl.when(jnp.logical_not(same))
        def _():
            copy(0).start()

        def step(j, carry):
            copy(j).start()
            return carry

        lax.fori_loop(1, 16, step, 0, unroll=5)

    def to_matched(k, src_of, dst):
        pltpu.make_async_copy(src_of(blk), dst.at[blk], a2a_r.at[k]).start()

        def step(j, carry):
            b = (blk + j) % 16
            send(
                src_of(b), dst.at[blk], a2a_s.at[k], a2a_r.at[k], sect_of(b // 2, y, b % 2), t
            ).start()
            return carry

        lax.fori_loop(1, 16, step, 0, unroll=5)

    def all_in(k, view):
        pltpu.make_async_copy(view, view, a2a_r.at[k]).wait()

    def all_out(k, view):
        pltpu.make_async_copy(view, view, a2a_s.at[k]).wait()

    def ring(stream, step):
        way = 1 if stream < 2 else NZ - 1
        block = (z + (NZ - way) * step) % NZ
        part = wt.at[block, c, pl.ds((stream % 2) * 32, 32)]
        return send(
            part, part, ring_s.at[stream, step], ring_r.at[stream, step],
            sect_of((z + way) % NZ, y, c), t,
        )

    def ring_from(stream, step):
        way = 1 if stream < 2 else NZ - 1
        block = (z + (NZ - way) * (step + 1)) % NZ
        part = wt.at[block, c, pl.ds((stream % 2) * 32, 32)]
        return block, send(
            part, part, ring_s.at[stream, step], ring_r.at[stream, step],
            sect_of((z + way) % NZ, y, c), t,
        )

    def partner(block, core, half):
        part = wt.at[block, core, pl.ds(half * 32, 32)]
        return send(
            part, part, par_s.at[block, half], par_r.at[block, half], sect_of(z, y, 1 - c), t
        )

    def partner_in(block, half):
        partner(block, 1 - c, half).wait_recv()

    def advance(step):
        for stream in (0, 2, 1, 3):
            if step >= RING[stream]:
                continue
            block, came = ring_from(stream, step)
            came.wait_recv()
            if step + 1 < RING[stream]:
                ring(stream, step + 1).start()
            partner(block, c, stream % 2).start()

    barrier = pltpu.get_barrier_semaphore()
    for j in range(1, 8):
        pl.semaphore_signal(
            barrier, inc=1, device_id=(z * 8 + (me + j) % 8, t), device_id_type=MESH
        )
    for j in (1, NZ - 1):
        pl.semaphore_signal(
            barrier, inc=1, device_id=(sect_of((z + j) % NZ, y, c), t), device_id_type=MESH
        )
    for j in range(1, NT):
        pl.semaphore_signal(barrier, inc=1, device_id=(me, (t + j) % NT), device_id_type=MESH)

    loads = [
        pltpu.make_async_copy(src, dst, in_sem.at[k])
        for k, (src, dst) in enumerate(
            (
                (send_in, send_ref), (w_in, wt.at[z, c]), (hidden_in, hd.at[y]),
                (gi_in, gi_ref), (gu_in, gu_ref), (hidden_in, hidden_ref), (pos_in, pos_ref),
                (len_in, len_ref),
            )
        )
    ]
    for load in loads:
        load.start()
    for load in loads:
        load.wait()
    sqx[t] = jnp.zeros((16, HIST), F32)
    spread = jnp.where((iota((64, 1024), 1) >> 4) == iota((64, 1024), 0), 1.0, 0.0).astype(BF16)
    named = mm(send_ref[...].astype(F32).astype(BF16), spread, 1, 0)
    lane = iota((1, 1024), 1)
    pick = jnp.full((1, 1024), -1.0, F32)
    for s in range(4):
        pick = jnp.where((lane & 3) == s, named[s : s + 1], pick)
    base = (jnp.zeros((1, 1024), jnp.int32) + y * 64).astype(F32)
    selb[y] = jnp.where((((lane >> 2) & 3) == y) & (pick >= 0.0), pick + base, -1.0)
    pl.semaphore_wait(barrier, 7 + 2 + NT - 1)

    def greet(step):
        for way in range(2):
            if step < 4 - way:
                peer = (z + 1) % NZ if way == 0 else (z + NZ - 1) % NZ
                pl.semaphore_signal(
                    hello.at[way, step], inc=1, device_id=(sect_of(peer, y, c), t),
                    device_id_type=MESH,
                )

    def relay(step):
        for way in range(2):
            if step < 4 - way:
                pl.semaphore_wait(hello.at[way, step], 1)
        greet(step + 1)

    greet(0)
    own_hd = lambda peer: hd.at[y]
    own_sel = lambda peer: selb.at[y]
    for stream in (0, 2, 1, 3):
        ring(stream, 0).start()
    start3(y_copy, 0, own_hd, hd)
    start3(y_copy, 1, own_sel, selb)
    for half in range(2):
        partner(z, c, half).start()

    gi = gi_ref[...].astype(F32).reshape(1, 1024)
    gu = gu_ref[...].astype(F32).reshape(1, 1024)
    hidden = hidden_ref[...].astype(F32)
    gained = hidden * gi
    sqx[t, pl.ds(0, 8), 0:64] = row_sums(hidden * hidden)
    sqx[t, pl.ds(8, 8), 0:64] = row_sums(gained * gained)
    own_sqx = lambda peer: sqx.at[t]
    start3(x_copy, 0, own_sqx, sqx)

    slots = pos_ref[...]
    owner = slots >> 2
    pos_s[...] = jnp.full(pos_s.shape, -1, jnp.int32)
    pos_s[:, 0 : HIST + CAND] = (
        ((owner >> 3) << 5) | ((owner & 1) << 4) | (((owner >> 1) & 3) << 2) | (slots & 3)
    )
    for u in range(4):
        for kind in range(2):
            row = pos_s[u : u + 1, kind * HIST : (kind + 1) * HIST]
            picked = one_hot(row, 256)
            first = (4 * kind + u) * HIST
            hot[:, first : first + HIST] = picked.astype(BF16)
            hott[first : first + HIST, :] = jnp.transpose(picked).astype(BF16)

    advance(0)
    relay(0)
    wait_in(x_from, 0, own_sqx, sqx)
    sums = sqx[0] + sqx[1] + sqx[2] + sqx[3]
    r_row = lax.rsqrt(sums[0:1] * (1.0 / D) + EPS)
    sq_item = r_row * r_row * sums[8:9]
    rs_row = lax.rsqrt(sq_item * (1.0 / D) + EPS)
    sqy[y] = jnp.concatenate([r_row, rs_row, sq_item] + [r_row] * 5, axis=0)
    own_sqy = lambda peer: sqy.at[y]
    start3(y_copy, 5, own_sqy, sqy)
    relay(1)
    advance(1)
    relay(2)
    wait_in(y_from, 0, own_hd, hd)
    lhs = (hd[...].reshape(256, 1024).astype(F32) * (gi * gu)).astype(BF16)

    def ps_copy(block):
        part, par = block // 2, block % 2
        return send(
            ps.at[block], pr.at[t, par], ps_s.at[block], ps_r.at[t, par], me, part
        )

    def project(block):
        ps[block] = mm(lhs, wt[block].reshape(HD, 1024), 1, 1).astype(BF16)

        @pl.when(block // 2 != t)
        def _():
            ps_copy(block).start()

    def project_step(step):
        if step == 0:
            project(z)
        for way in (1, NZ - 1)[: 2 if step < 3 else 1]:
            project((z + way * (step + 1)) % NZ)

    def partners_in(step):
        if step == 0:
            for half in range(2):
                partner_in(z, half)
        for stream in range(4):
            if step < RING[stream]:
                way = 1 if stream < 2 else NZ - 1
                partner_in((z + (NZ - way) * (step + 1)) % NZ, stream % 2)

    partners_in(0)
    project_step(0)
    wait_in(y_from, 1, own_sel, selb)
    picks = jnp.maximum(jnp.maximum(selb[0], selb[1]), jnp.maximum(selb[2], selb[3]))
    gt[...] = one_hot(picks.astype(jnp.int32), 256).astype(BF16)
    wait_in(y_from, 5, own_sqy, sqy)
    rcol[...] = jnp.concatenate([columns(sqy[b, 0:1])[0:64] for b in range(4)], axis=0)
    rscol[...] = jnp.concatenate([columns(sqy[b, 1:2])[0:64] for b in range(4)], axis=0)
    sq_out = jnp.zeros((8, 1024), F32)
    for b in range(4):
        sq_out = sq_out + mm(
            row_parts(sqy[b, 2:3])[:, 0:64], gt[b * 64 : (b + 1) * 64, :], 1, 0
        )
    sq_out = jnp.sum(sq_out, axis=0, keepdims=True)
    for b in range(NZ):
        sqo[b] = sq_out[:, b * HD : (b + 1) * HD]
    pieces = []
    for par in range(2):
        head = par * 4 + y
        lanes = pl.ds(pl.multiple_of(head * HD, HD), HD)
        piece = hd[:, :, lanes].reshape(256, HD).astype(F32)
        gain = jnp.zeros((1, HD), F32)
        for h in range(8):
            gain = gain + jnp.where(head == h, gi[:, h * HD : (h + 1) * HD], 0.0)
        pieces.append((piece * rcol[...] * gain).astype(BF16))
    oute[...] = mm(gt[...], jnp.concatenate(pieces, axis=1), 0, 0).astype(BF16)
    partners_in(1)
    project_step(1)
    advance(2)
    relay(3)
    both = slice(0, 256)
    to_matched(5, lambda b: sqo.at[b // 2], sqi)
    to_readers(0, oute, bufe, both)
    partners_in(2)
    project_step(2)
    advance(3)
    partners_in(3)
    project_step(3)
    for q in range(4):
        gain_s[q] = jnp.concatenate(
            [gu[:, q * HD : (q + 1) * HD], gu[:, (4 + q) * HD : (5 + q) * HD]], axis=1
        )
    for par in range(2):
        pr[t, par] = ps[2 * t + par]
    for par in range(2):
        for j in (1, 3, 2):
            sender = (t + j) % NT
            send(
                ps.at[2 * t + par], pr.at[sender, par], ps_s.at[2 * t + par],
                ps_r.at[sender, par], me, sender,
            ).wait_recv()
    total = jnp.concatenate(
        [
            pr[0, par].astype(F32) + pr[1, par].astype(F32)
            + pr[2, par].astype(F32) + pr[3, par].astype(F32)
            for par in range(2)
        ],
        axis=1,
    ) * (rcol[...] * rscol[...])[:, 0:1]
    q32[...] = total
    heads, _ = norm_heads(total)
    outq[...] = mm(gt[...], jnp.concatenate(heads, axis=1).astype(BF16), 0, 0).astype(BF16)
    halves = (slice(0, HD), slice(HD, 2 * HD))
    to_readers(1, outq, bufq, halves[0])
    to_readers(4, outq, bufq, halves[1])

    off = (me % 8) * 16
    blocks = jnp.where((iota((256, 16), 0) >> 4) == iota((256, 16), 1), 1.0, 0.0).astype(BF16)
    in_lane = iota((256, HD), 1) == off + (iota((256, HD), 0) & 15)
    all_in(5, sqi)
    came = jnp.concatenate([sqi[b] for b in range(16)], axis=0)
    high, mid, low = split3(came)
    wide = mm(blocks, high, 1, 0) + mm(blocks, mid, 1, 0) + mm(blocks, low, 1, 0)
    sqm[...] = jnp.broadcast_to(lane_sum(jnp.where(in_lane, wide, 0.0)), (256, HD))
    rsm[...] = lax.rsqrt(sqm[...] * (1.0 / D) + EPS)
    sqf_s[...] = jnp.broadcast_to(
        lane_sum(mm(hott[0:512], lane_parts(sqm[...]), 1, 0)), (512, HIST)
    )
    sqc = jnp.sum(mm(lane_parts(sqm[...]), hot[:, 512:1024], 0, 0), axis=0, keepdims=True)
    for u in range(4):
        sqc_s[u] = sqc[:, u * HIST : (u + 1) * HIST]
    twice = lambda values: jnp.concatenate([values, values], axis=1)
    all_in(0, bufe)
    for q in range(4):
        low = (bufe[q].astype(F32) * twice(rsm[...]) * gain_s[q]).astype(BF16)
        nrm[q] = low
        heads, _ = norm_heads(low.astype(F32))
        knb[q] = jnp.concatenate(heads, axis=1).astype(BF16)
    for q in range(4):
        kn_s[q] = mm(hott[0:512], knb[q], 1, 0).astype(BF16)
        v_s[q] = mm(hott[0:512], nrm[q], 1, 0).astype(BF16)
    for q in range(4):
        rc_s[q] = mm(hott[...], bufe[q], 1, 0).astype(BF16)

    scale = HD ** (-0.5)
    row_id = iota((HIST, HIST), 0)
    col_id = iota((HIST, HIST), 1)

    def follow_of(rows):
        moved = pltpu.roll(rows, HIST - 1, 0)
        return jnp.where(iota(rows.shape, 0) < HIST - 1, moved, 0.0)

    def st_copy(u, j):
        peer = (t + j) % NT
        return send(st_r.at[t, u], st_r.at[t, u], xs.at[6 + u, peer], xr.at[6 + u, t], me, peer)

    def st_from(u, j):
        sender = (t + NT - j) % NT
        return send(
            st_r.at[t, u], st_r.at[sender, u], xs.at[6 + u, sender], xr.at[6 + u, sender],
            me, sender,
        )

    def user_rows(u):
        return pl.ds(pl.multiple_of(u * HIST, HIST), HIST)

    def attend(first, par):
        lanes = halves[par]
        tasks = [(first + k, q, 4 * k + q) for k in range(2) for q in range(4)]
        for u, q, slot in tasks:
            span = user_rows(u)
            p_t[slot] = mm(qn_s[q, span, lanes], kn_s[q, span, lanes], 1, 1)
        for u, q, slot in tasks:
            mask = (col_id <= row_id) & (col_id < len_ref[u])
            weights = jnp.where(mask, jnp.exp(p_t[slot] * scale), 0.0)
            w_s[2 * q + par, user_rows(u)] = (weights * (1.0 / lane_sum(weights))).astype(BF16)
        for u, q, slot in tasks:
            span = user_rows(u)
            o_s[q, span, lanes] = rc_s[q, span, lanes].astype(F32) + mm(
                w_s[2 * q + par, span], v_s[q, span, lanes], 1, 0
            )

    def first_half(i, carry):
        attend(2 * i, 0)
        return carry

    def score(u):
        span = user_rows(u)
        cspan = user_rows(u + 4)
        own = jnp.zeros((HIST, 1), F32)
        hit = jnp.zeros((HIST, 1), F32)
        neg = jnp.zeros((HIST, HIST), F32)
        for q in range(4):
            out = o_s[q, span]
            own = own + lane_sum(out * out)
            hit = hit + lane_sum(out * follow_of(rc_s[q, span].astype(F32)))
            high = out.astype(BF16)
            low = (out - high.astype(F32)).astype(BF16)
            cands = rc_s[q, cspan]
            neg = neg + mm(high, cands, 1, 1) + mm(low, cands, 1, 1)
        stats = neg + jnp.where(col_id == CAND, own, 0.0) + jnp.where(col_id == CAND + 1, hit, 0.0)
        st_r[t, u] = stats.astype(BF16)
        for j in (2, 1, 3):
            st_copy(u, j).start()

    def second_half(i, carry):
        attend(2 * i, 1)
        score(2 * i)
        score(2 * i + 1)
        return carry

    def turn_weights(k, carry):
        for u in range(4):
            span = slice(u * HIST, (u + 1) * HIST)
            wt_s[k, span] = jnp.transpose(w_s[k, span].astype(F32)).astype(BF16)
        return carry

    for par, step in ((0, first_half), (1, second_half)):
        all_in(1 if par == 0 else 4, outq.at[:, halves[0]])
        for q in range(4):
            qn_s[q, :, halves[par]] = mm(hott[0:512], bufq[q, :, halves[par]], 1, 0).astype(BF16)
        lax.fori_loop(0, 2, step, 0)
    lax.fori_loop(0, 8, turn_weights, 0)

    def losses(u, carry):
        for j in (1, 3, 2):
            st_from(u, j).wait_recv()
        stats = (
            st_r[0, u].astype(F32) + st_r[1, u].astype(F32)
            + st_r[2, u].astype(F32) + st_r[3, u].astype(F32)
        )
        is_cand = col_id < CAND
        neg = jnp.where(is_cand, stats, 0.0)
        own = lane_sum(jnp.where(col_id == CAND, stats, 0.0))
        hit = lane_sum(jnp.where(col_id == CAND + 1, stats, 0.0))
        sq_follow = pltpu.roll(sqf_s[user_rows(u)], HIST - 1, 0)[:, 0:1]
        rn = lax.rsqrt(own + EPS)
        rf = lax.rsqrt(sq_follow + EPS)
        rc = lax.rsqrt(sqc_s[u] + EPS)
        tl = SOFT * hit * rn * rf
        nl = SOFT * neg * rn * rc
        en = jnp.where(is_cand, jnp.exp(nl), 0.0)
        et = jnp.exp(tl)
        whole = et + lane_sum(en)
        span = len_ref[u] - 1
        over = 1.0 / (jnp.full((HIST, 1), 0, jnp.int32) + span).astype(F32)
        valid = iota((HIST, 1), 0) < span
        terms = jnp.where(valid, (jnp.log(whole) - tl) * over, 0.0)
        loss_ref[u] = jnp.broadcast_to(jnp.sum(terms, axis=0, keepdims=True), (1, HIST))
        g = jnp.where(valid, float(D) * over, 0.0)
        dtl = g * (et / whole - 1.0)
        dnl = (g / whole) * en
        dsc[u, 0] = jnp.broadcast_to(
            -rn * rn * (dtl * tl + lane_sum(dnl * nl)), (HIST, HIST)
        )
        dsc[u, 1] = jnp.broadcast_to(dtl * (SOFT * rn * rf), (HIST, HIST))
        dneg = dnl * (SOFT * rn * rc)
        dneg_s[u] = dneg.astype(BF16)
        dnegt_s[u] = jnp.transpose(dneg).astype(BF16)
        dsqf = jnp.broadcast_to(-0.5 * dtl * tl * rf * rf, (HIST, HIST))
        gfol[user_rows(u)] = pltpu.roll(dsqf, 1, 0)
        grow[u] = -0.5 * rc * rc * jnp.sum(dnl * nl, axis=0, keepdims=True)
        return carry

    lax.fori_loop(0, 4, losses, 0)

    def backward_step(par, i):
        q = (y + 1 + i) % 4
        lanes = halves[par]
        spans = [(slice(u * HIST, (u + 1) * HIST), u) for u in range(4)]
        for span, u in spans:
            cspan = slice((4 + u) * HIST, (5 + u) * HIST)
            dhit = dsc[u, 1]
            out = o_s[q, span, lanes]
            rows = rc_s[q, span, lanes].astype(F32)
            dout = (
                dsc[u, 0] * out
                + dhit * follow_of(rows)
                + mm(dneg_s[u], rc_s[q, cspan, lanes], 1, 0)
            )
            dout_t[span, lanes] = dout.astype(BF16)
            drc_s[q, span, lanes] = (dout + pltpu.roll(dhit * out, 1, 0)).astype(BF16)
            drc_s[q, cspan, lanes] = mm(dnegt_s[u], out.astype(BF16), 1, 0).astype(BF16)
        for span, u in spans:
            p_t[u] = mm(dout_t[span, lanes], v_s[q, span, lanes], 1, 1)
        for span, u in spans:
            dw = p_t[u]
            wide = w_s[2 * q + par, span].astype(F32)
            ds_t[u] = (wide * (dw - lane_sum(dw * wide)) * scale).astype(BF16)
        for span, u in spans:
            dq_t[span, lanes] = mm(ds_t[u], kn_s[q, span, lanes], 1, 0).astype(BF16)
            dk_s[q, span, lanes] = mm(ds_t[u], qn_s[q, span, lanes], 0, 0).astype(BF16)
            dv_s[q, span, lanes] = mm(wt_s[2 * q + par, span], dout_t[span, lanes], 1, 0).astype(
                BF16
            )
        dqo[q, :, lanes] = mm(hot[:, 0:512], dq_t[:, lanes], 1, 0).astype(BF16)
        to_group((2, 7)[par], dqo, rq, q, i == 3, lanes)

    def backward_first(i, carry):
        backward_step(0, i)
        return carry

    def backward_second(i, carry):
        backward_step(1, i)
        return carry

    lax.fori_loop(0, 4, backward_first, 0)
    lax.fori_loop(0, 4, backward_second, 0)

    nbs[...] = jnp.zeros(nbs.shape, F32)

    def return_quarter(i, carry):
        q = (y + 1 + i) % 4
        dk = mm(hot[:, 0:512], dk_s[q], 1, 0)
        dn = mm(hot[:, 0:512], dv_s[q], 1, 0) + norm_heads_back(nrm[q].astype(F32), dk)
        dn = dn * gain_s[q]
        nbs[...] += jnp.broadcast_to(lane_sum(dn * bufe[q].astype(F32)), (256, HD))
        eo[q] = (mm(hot[...], drc_s[q], 1, 0) + dn * twice(rsm[...])).astype(BF16)
        return carry

    lax.fori_loop(0, 4, return_quarter, 0)
    gsq = lane_sum(mm(hot[:, 0:512], lane_parts(gfol[...]), 1, 0)) + lane_sum(
        mm(
            hot[:, 512:1024],
            row_parts(jnp.concatenate([grow[u] for u in range(4)], axis=1)), 1, 1,
        )
    )
    placed = []
    for values in (jnp.broadcast_to(gsq, (256, HD)), nbs[...]):
        high, mid, low = split3(jnp.where(in_lane, values, 0.0))
        placed.append(mm(blocks, high, 0, 0) + mm(blocks, mid, 0, 0) + mm(blocks, low, 0, 0))
    for b in range(16):
        sco[b] = jnp.concatenate([part[b : b + 1] for part in placed], axis=1)
    to_matched(6, lambda b: sco.at[b], sci)

    def return_group(i, carry):
        to_group(3, eo, re, (y + 1 + i) % 4, i == 3, both)
        return carry


    chunks = (((y + 2) % NY, (y + 1) % NY), ((y + 3) % NY, y))

    def dq_first(peer, sender):
        return send(
            dqg.at[t, 0], dqg.at[sender, 0], xs.at[2, peer], xr.at[2, sender], me, peer
        )

    def dq_second(part, k, peer, sender):
        b = chunks[part][k]
        index = (1, 3, 4, 10)[2 * part + k]
        return send(
            dqg.at[t, 1, b], dqg.at[sender, 1, b], xs.at[index, peer], xr.at[index, sender],
            me, peer,
        )

    def item_dq(par):
        lanes = halves[par]
        out = head_back(q32[:, lanes], mm(gt[...], rq[:, lanes], 1, 0)).astype(BF16)
        dqg[t, par] = out.reshape(4, 64, HD)
        return row_sums(out.astype(F32) * q32[:, lanes])

    all_in(2, rq.at[:, halves[0]])
    dots = item_dq(0)
    for j in (2, 1, 3):
        dq_first((t + j) % NT, t).start()
    all_in(6, sci)
    pairs = [sci[2 * b] + sci[2 * b + 1] for b in range(NZ)]
    item_terms = []
    for lanes in (slice(0, HD), slice(HD, 2 * HD)):
        row = jnp.concatenate([pair[:, lanes] for pair in pairs], axis=1)
        item_terms.append(jnp.sum(mm(row_parts(row), gt[...], 1, 1), axis=0, keepdims=True))
    sdy[y, pl.ds(8, 8), :] = jnp.broadcast_to(item_terms[0], (8, 256))
    rs_all = mm(jnp.ones((8, HD), BF16), lane_parts(rscol[...]), 1, 1)[0:1]
    all_in(7, rq.at[:, halves[1]])
    dots = dots + item_dq(1)
    sdx[t] = dots + rs_all * item_terms[1]
    own_sdx = lambda peer: sdx.at[t]
    start3(x_copy, 5, own_sdx, sdx)
    for part in range(2):
        for j in (2, 1, 3):
            for k in range(2):
                dq_second(part, k, (t + j) % NT, t).start()
    lax.fori_loop(0, 4, return_group, 0)
    for j in (1, 3, 2):
        sender = (t + j) % NT
        dq_first(sender, sender).wait_recv()
    acc = jnp.zeros((256, 1024), F32)
    for tt in range(NT):
        acc = acc + mm(dqg[tt, 0].reshape(256, HD), wt[2 * tt].reshape(HD, 1024), 1, 0)
    acc_s[...] = acc.reshape(4, 64, 1024)
    gws_of = lambda peer: gws.at[peer]
    for part in range(2):
        for j in (1, 3, 2):
            sender = (t + j) % NT
            for k in range(2):
                dq_second(part, k, sender, sender).wait_recv()
        acc = jnp.concatenate([acc_s[b] for b in chunks[part]], axis=0)
        for tt in range(NT):
            acc = acc + mm(
                jnp.concatenate([dqg[tt, 1, b] for b in chunks[part]], axis=0),
                wt[2 * tt + 1].reshape(HD, 1024), 1, 0,
            )
        acc = acc.astype(BF16)
        for k, b in enumerate(chunks[part]):
            gws[b] = acc[k * 64 : (k + 1) * 64]
        if part == 0:
            wait_in(x_from, 5, own_sdx, sdx)
            sdy[y, pl.ds(0, 8), :] = sdx[0] + sdx[1] + sdx[2] + sdx[3]
            own_sdy = lambda peer: sdy.at[y]
            start3(y_copy, 4, own_sdy, sdy)
        for j in ((2, 1), (3,))[part]:
            y_copy(2, gws_of, gwr, j).start()
    gwr[y] = gws[y]
    all_in(3, re)
    es[...] = mm(gt[...], re[...], 1, 0).astype(BF16).reshape(4, 64, 256)
    es_of = lambda peer: es.at[peer]
    start3(y_copy, 3, es_of, er)
    er[y] = es[y]

    mine = pl.ds(pl.multiple_of(y * 64, 64), 64)
    emb = (hidden_ref[...].astype(F32) * rcol[mine, 0:1] * gi).astype(BF16).astype(F32)
    rs_own = rscol[mine, 0:1]
    wait_in(y_from, 4, own_sdy, sdy)
    last = sdy[0] + sdy[1] + sdy[2] + sdy[3]
    sqm[...] = columns(2.0 * last[8:9] - (1.0 / D) * rs_all * rs_all * last[0:1])
    coef = sqm[mine, 0:1]
    direct = emb * coef
    wait_in(y_from, 2, gws_of, gwr)
    gw = (
        gwr[0].astype(F32) + gwr[1].astype(F32) + gwr[2].astype(F32) + gwr[3].astype(F32)
    ) * gu * rs_own + direct
    wait_in(y_from, 3, es_of, er)
    for h in range(8):
        lanes = slice(h * HD, (h + 1) * HD)
        par, q = h // 4, h % 4
        grad_ref[:, lanes] = er[q, :, halves[par]].astype(F32) + gw[:, lanes]

    for k, src, dst in (
        (0, own_hd, hd), (1, own_sel, selb), (2, gws_of, gwr), (3, es_of, er), (4, own_sdy, sdy),
        (5, own_sqy, sqy),
    ):
        wait_out(y_copy, k, src, dst)
    for k, src, dst in (
        (0, own_sqx, sqx), (5, own_sdx, sdx)
    ):
        wait_out(x_copy, k, src, dst)
    for j in (1, 3, 2):
        peer = (t + j) % NT
        dq_first(peer, t).wait_send()
        for part in range(2):
            for k in range(2):
                dq_second(part, k, peer, t).wait_send()
    for j in (1, 3, 2):
        for par in range(2):
            ps_copy((t + j) % NT * 2 + par).wait_send()
    for u in range(4):
        for j in (1, 3, 2):
            st_copy(u, j).wait_send()
    for stream in range(4):
        for step in range(RING[stream]):
            ring(stream, step).wait_send()
    for b in range(NZ):
        for half in range(2):
            partner(b, c, half).wait_send()
    most = pl.ds(0, (NS - 1) * 16)
    all_out(0, oute.at[most])
    all_out(1, outq.at[most, halves[0]])
    all_out(4, outq.at[most, halves[1]])
    all_out(2, rq.at[most, halves[0]])
    all_out(7, rq.at[most, halves[1]])
    all_out(3, re.at[most])
    all_out(5, sqi.at[pl.ds(0, 15)])
    all_out(6, sci.at[pl.ds(0, 15)])


def local(item_hidden, item_gain, send_item, pos_slot, hist_len, user_gain, query_weight):
    vmem = pltpu.VMEM
    dma = pltpu.SemaphoreType.DMA
    quarter = lambda kind: vmem((4, 256, 256), kind)
    grad, loss = pl.pallas_call(
        kernel,
        out_shape=(
            jax.ShapeDtypeStruct((64, 1024), F32),
            jax.ShapeDtypeStruct((4, 1, HIST), F32),
        ),
        in_specs=[pl.BlockSpec(memory_space=pltpu.HBM)] * 7,
        out_specs=(
            pl.BlockSpec(memory_space=pltpu.VMEM),
            pl.BlockSpec(memory_space=pltpu.VMEM),
        ),
        scratch_shapes=[
            pltpu.SMEM((4,), jnp.int32),
            vmem((64, 1024), BF16),
            vmem((1024,), BF16),
            vmem((1024,), BF16),
            vmem((4, 64), jnp.int32),
            vmem((4, HIST + CAND), jnp.int32),
            dma((8,)),
            vmem((4, 64, 1024), BF16),
            vmem((4, 1, 1024), F32),
            vmem((8, 2, 64, 1024), BF16),
            vmem((4, 16, HIST), F32),
            vmem((4, 8, HIST), F32),
            vmem((8, 256, HD), BF16),
            vmem((4, 2, 256, HD), BF16),
            vmem((1024, 256), BF16),
            vmem((1024, 256), BF16),
            quarter(BF16),
            quarter(BF16),
            vmem((256, 1024), BF16),
            quarter(BF16),
            quarter(BF16),
            vmem((8, 1, HIST), F32),
            vmem((16, 1, HIST), F32),
            vmem((256, HIST), F32),
            vmem((256, HIST), F32),
            vmem((256, 256), F32),
            vmem((256, HIST), F32),
            vmem((256, HIST), F32),
            vmem((4, 2 * HIST), jnp.int32),
            vmem((256, 1024), BF16),
            vmem((1024, 256), BF16),
            vmem((512, HIST), F32),
            vmem((4, 1, HIST), F32),
            vmem((4, 1, 256), F32),
            vmem((4, 1024, 256), BF16),
            vmem((4, 512, 256), BF16),
            vmem((4, 512, 256), BF16),
            vmem((4, 512, 256), BF16),
            vmem((8, 512, HIST), BF16),
            vmem((8, 512, HIST), BF16),
            vmem((8, HIST, HIST), F32),
            vmem((8, HIST, HIST), BF16),
            vmem((4, 512, 256), F32),
            vmem((4, 4, HIST, HIST), BF16),
            vmem((4, 2, HIST, HIST), F32),
            vmem((4, HIST, HIST), BF16),
            vmem((4, HIST, HIST), BF16),
            vmem((512, HIST), F32),
            vmem((4, 1, HIST), F32),
            vmem((512, 256), BF16),
            vmem((512, 256), BF16),
            vmem((4, 512, 256), BF16),
            vmem((4, 512, 256), BF16),
            vmem((4, 1024, 256), BF16),
            vmem((256, HIST), F32),
            quarter(BF16),
            quarter(BF16),
            vmem((1024, 256), BF16),
            vmem((1024, 256), BF16),
            vmem((16, 1, 256), F32),
            vmem((16, 1, 256), F32),
            vmem((4, 2, 4, 64, HD), BF16),
            vmem((4, 64, 1024), F32),
            vmem((4, 64, 1024), BF16),
            vmem((4, 64, 1024), BF16),
            vmem((4, 64, 256), BF16),
            vmem((4, 64, 256), BF16),
            vmem((4, 8, 256), F32),
            vmem((4, 16, 256), F32),
            dma((11, 4)),
            dma((11, 4)),
            dma((6, 4)),
            dma((6, 4)),
            dma((4, 4)),
            dma((4, 4)),
            dma((8, 2)),
            dma((8, 2)),
            dma((8,)),
            dma((8,)),
            dma((8,)),
            dma((4, 2)),
            pltpu.SemaphoreType.REGULAR((2, 4)),
        ],
        compiler_params=pltpu.CompilerParams(
            collective_id=0, has_side_effects=True, vmem_limit_bytes=40 * 1024 * 1024
        ),
    )(
        *[
            pltpu.with_memory_space_constraint(value, pltpu.HBM)
            for value in (
                hist_len, item_hidden, query_weight.T, item_gain, user_gain, send_item[0].T,
                pos_slot,
            )
        ]
    )
    return (grad, loss[:, 0, 0])


def solution(mesh):
    placed = (
        P("sect", "tp"),
        P("tp"),
        P("sect", None, None),
        P("sect", None),
        P("sect"),
        P("tp"),
        P("tp", "sect"),
    )
    return jax.shard_map(
        local, mesh=mesh, in_specs=placed, out_specs=(P("sect", "tp"), P("sect")), check_vma=False
    )
```

```python
import jax
import jax.numpy as jnp
from jax import lax
from jax.experimental import pallas as pl
from jax.experimental.pallas import tpu as pltpu
from jax.sharding import PartitionSpec as P

D = 4096
HD = 128
HIST = 128
CAND = 64
NZ, NY, NT = 8, 4, 4
NS = 64
EPS = 1e-06
SOFT = 20.0
F32, BF16 = jnp.float32, jnp.bfloat16
MESH = pl.DeviceIdType.MESH
RING = (4, 3, 3, 4)


def mm(a, b, ca, cb, precision=None):
    return lax.dot_general(
        a, b, (((ca,), (cb,)), ((), ())), preferred_element_type=F32, precision=precision
    )


def split3(values):
    high = values.astype(BF16)
    rest = values - high.astype(F32)
    mid = rest.astype(BF16)
    return high, mid, (rest - mid.astype(F32)).astype(BF16)


def row_parts(row):
    parts = split3(jnp.broadcast_to(row, (8, row.shape[1])))
    index = iota((8, row.shape[1]), 0)
    out = jnp.where(index == 0, parts[0].astype(F32), 0.0)
    out = jnp.where(index == 1, parts[1].astype(F32), out)
    return jnp.where(index == 2, parts[2].astype(F32), out).astype(BF16)


def lane_parts(values):
    parts = split3(values)
    index = iota(values.shape, 1)
    out = jnp.where(index == 0, parts[0].astype(F32), 0.0)
    out = jnp.where(index == 1, parts[1].astype(F32), out)
    return jnp.where(index == 2, parts[2].astype(F32), out).astype(BF16)


def columns(row):
    return mm(row_parts(row), jnp.ones((8, 128), BF16), 0, 0)


def row_sums(values):
    ones = jnp.ones((8, values.shape[1]), BF16)
    high, mid, low = split3(values)
    return mm(ones, high, 1, 1) + mm(ones, mid, 1, 1) + mm(ones, low, 1, 1)


def lane_sum(values):
    return jnp.sum(values, axis=1, keepdims=True)


def iota(shape, dim):
    return lax.broadcasted_iota(jnp.int32, shape, dim)


def one_hot(row, count):
    return jnp.where(iota((count, row.shape[1]), 0) == row, 1.0, 0.0)


def norm_heads(values):
    heads, roots = [], []
    for par in range(2):
        part = values[:, par * HD : (par + 1) * HD]
        root = lax.rsqrt(lane_sum(part * part) * (1.0 / HD) + EPS)
        heads.append(part * root)
        roots.append(root)
    return heads, roots


def head_back(values, grad):
    root = lax.rsqrt(lane_sum(values * values) * (1.0 / HD) + EPS)
    head = values * root
    return root * (grad - head * (lane_sum(grad * head) * (1.0 / HD)))


def norm_heads_back(values, grads):
    heads, roots = norm_heads(values)
    out = []
    for par in range(2):
        grad = grads[:, par * HD : (par + 1) * HD]
        out.append(
            roots[par] * (grad - heads[par] * (lane_sum(grad * heads[par]) * (1.0 / HD)))
        )
    return jnp.concatenate(out, axis=1)


def kernel(
    len_in, hidden_in, w_in, gi_in, gu_in, send_in, pos_in,
    grad_ref, loss_ref,
    len_ref, hidden_ref, gi_ref, gu_ref, send_ref, pos_ref, in_sem,
    hd, selb, wt, sqx, sqy, ps, pr, oute, outq, bufe, bufq, gt, nrm, knb, sqo, sqi, sqm, rsm, q32,
    rcol, rscol, pos_s, hot, hott, sqf_s, sqc_s, gain_s,
    rc_s, kn_s, v_s, qn_s, w_s, wt_s, p_t, ds_t, o_s, st_r, dsc, dneg_s, dnegt_s, gfol, grow,
    dout_t, dq_t, dk_s, dv_s, drc_s, nbs, dqo, eo, rq, re, sco, sci,
    dqg, acc_s, gws, gwr, es, er, sdx, sdy,
    xs, xr, ys, yr, ring_s, ring_r, par_s, par_r, a2a_s, a2a_r, ps_s, ps_r, hello,
):
    me = lax.axis_index("sect")
    t = lax.axis_index("tp")
    z, y, c = me // 8, (me // 2) % 4, me % 2
    blk = z * 2 + c

    def send(src, dst, ssem, rsem, sect, tp):
        return pltpu.make_async_remote_copy(
            src_ref=src, dst_ref=dst, send_sem=ssem, recv_sem=rsem,
            device_id=(sect, tp), device_id_type=MESH,
        )

    def sect_of(zz, yy, cc):
        return zz * 8 + yy * 2 + cc

    def x_copy(k, src, dst, j):
        peer = (t + j) % NT
        return send(src(peer), dst.at[t], xs.at[k, peer], xr.at[k, t], me, peer)

    def x_from(k, src, dst, j):
        sender = (t + NT - j) % NT
        return send(src(t), dst.at[sender], xs.at[k, sender], xr.at[k, sender], me, sender)

    def y_copy(k, src, dst, j):
        peer = (y + j) % NY
        return send(src(peer), dst.at[y], ys.at[k, peer], yr.at[k, y], sect_of(z, peer, c), t)

    def y_from(k, src, dst, j):
        sender = (y + NY - j) % NY
        return send(
            src(y), dst.at[sender], ys.at[k, sender], yr.at[k, sender], sect_of(z, sender, c), t
        )

    def start3(copy, k, src, dst):
        for j in (2, 1, 3):
            copy(k, src, dst, j).start()

    def wait_in(came, k, src, dst):
        for j in (1, 3, 2):
            came(k, src, dst, j).wait_recv()

    def wait_out(copy, k, src, dst):
        for j in (1, 3, 2):
            copy(k, src, dst, j).wait_send()

    def rows_of(first):
        return pl.ds(pl.multiple_of(first * 16, 16), 16)

    def to_readers(k, out, buf, lanes):
        pltpu.make_async_copy(
            out.at[rows_of(me), lanes], buf.at[y, rows_of(blk), lanes], a2a_r.at[k]
        ).start()

        def step(j, carry):
            peer = (me + j) % NS
            send(
                out.at[rows_of(peer), lanes], buf.at[y, rows_of(blk), lanes],
                a2a_s.at[k], a2a_r.at[k], peer, t,
            ).start()
            return carry

        lax.fori_loop(1, NS, step, 0, unroll=7)

    def to_group(k, out, buf, group, same, lanes):
        def copy(j):
            b = (blk + j) % 16
            return send(
                out.at[group, rows_of(b), lanes], buf.at[rows_of(me), lanes],
                a2a_s.at[k], a2a_r.at[k], sect_of(b // 2, group, b % 2), t,
            )

        @pl.when(same)
        def _():
            pltpu.make_async_copy(
                out.at[group, rows_of(blk), lanes], buf.at[rows_of(me), lanes], a2a_r.at[k]
            ).start()

        @pl.when(jnp.logical_not(same))
        def _():
            copy(0).start()

        def step(j, carry):
            copy(j).start()
            return carry

        lax.fori_loop(1, 16, step, 0, unroll=5)

    def to_matched(k, src_of, dst):
        pltpu.make_async_copy(src_of(blk), dst.at[blk], a2a_r.at[k]).start()

        def step(j, carry):
            b = (blk + j) % 16
            send(
                src_of(b), dst.at[blk], a2a_s.at[k], a2a_r.at[k], sect_of(b // 2, y, b % 2), t
            ).start()
            return carry

        lax.fori_loop(1, 16, step, 0, unroll=5)

    def all_in(k, view):
        pltpu.make_async_copy(view, view, a2a_r.at[k]).wait()

    def all_out(k, view):
        pltpu.make_async_copy(view, view, a2a_s.at[k]).wait()

    def ring(stream, step):
        way = 1 if stream < 2 else NZ - 1
        block = (z + (NZ - way) * step) % NZ
        part = wt.at[block, c, pl.ds((stream % 2) * 32, 32)]
        return send(
            part, part, ring_s.at[stream, step], ring_r.at[stream, step],
            sect_of((z + way) % NZ, y, c), t,
        )

    def ring_from(stream, step):
        way = 1 if stream < 2 else NZ - 1
        block = (z + (NZ - way) * (step + 1)) % NZ
        part = wt.at[block, c, pl.ds((stream % 2) * 32, 32)]
        return block, send(
            part, part, ring_s.at[stream, step], ring_r.at[stream, step],
            sect_of((z + way) % NZ, y, c), t,
        )

    def partner(block, core, half):
        part = wt.at[block, core, pl.ds(half * 32, 32)]
        return send(
            part, part, par_s.at[block, half], par_r.at[block, half], sect_of(z, y, 1 - c), t
        )

    def partner_in(block, half):
        partner(block, 1 - c, half).wait_recv()

    def advance(step):
        for stream in (0, 2, 1, 3):
            if step >= RING[stream]:
                continue
            block, came = ring_from(stream, step)
            came.wait_recv()
            if step + 1 < RING[stream]:
                ring(stream, step + 1).start()
            partner(block, c, stream % 2).start()

    barrier = pltpu.get_barrier_semaphore()
    for j in range(1, 8):
        pl.semaphore_signal(
            barrier, inc=1, device_id=(z * 8 + (me + j) % 8, t), device_id_type=MESH
        )
    for j in (1, NZ - 1):
        pl.semaphore_signal(
            barrier, inc=1, device_id=(sect_of((z + j) % NZ, y, c), t), device_id_type=MESH
        )
    for j in range(1, NT):
        pl.semaphore_signal(barrier, inc=1, device_id=(me, (t + j) % NT), device_id_type=MESH)

    loads = [
        pltpu.make_async_copy(src, dst, in_sem.at[k])
        for k, (src, dst) in enumerate(
            (
                (send_in, send_ref), (w_in, wt.at[z, c]), (hidden_in, hd.at[y]),
                (gi_in, gi_ref), (gu_in, gu_ref), (hidden_in, hidden_ref), (pos_in, pos_ref),
                (len_in, len_ref),
            )
        )
    ]
    for load in loads:
        load.start()
    for load in loads:
        load.wait()
    sqx[t] = jnp.zeros((16, HIST), F32)
    spread = jnp.where((iota((64, 1024), 1) >> 4) == iota((64, 1024), 0), 1.0, 0.0).astype(BF16)
    named = mm(send_ref[...].astype(F32).astype(BF16), spread, 1, 0)
    lane = iota((1, 1024), 1)
    pick = jnp.full((1, 1024), -1.0, F32)
    for s in range(4):
        pick = jnp.where((lane & 3) == s, named[s : s + 1], pick)
    base = (jnp.zeros((1, 1024), jnp.int32) + y * 64).astype(F32)
    selb[y] = jnp.where((((lane >> 2) & 3) == y) & (pick >= 0.0), pick + base, -1.0)
    pl.semaphore_wait(barrier, 7 + 2 + NT - 1)

    def greet(step):
        for way in range(2):
            if step < 4 - way:
                peer = (z + 1) % NZ if way == 0 else (z + NZ - 1) % NZ
                pl.semaphore_signal(
                    hello.at[way, step], inc=1, device_id=(sect_of(peer, y, c), t),
                    device_id_type=MESH,
                )

    def relay(step):
        for way in range(2):
            if step < 4 - way:
                pl.semaphore_wait(hello.at[way, step], 1)
        greet(step + 1)

    greet(0)
    own_hd = lambda peer: hd.at[y]
    own_sel = lambda peer: selb.at[y]
    for stream in (0, 2, 1, 3):
        ring(stream, 0).start()
    start3(y_copy, 0, own_hd, hd)
    start3(y_copy, 1, own_sel, selb)
    for half in range(2):
        partner(z, c, half).start()

    gi = gi_ref[...].astype(F32).reshape(1, 1024)
    gu = gu_ref[...].astype(F32).reshape(1, 1024)
    hidden = hidden_ref[...].astype(F32)
    gained = hidden * gi
    sqx[t, pl.ds(0, 8), 0:64] = row_sums(hidden * hidden)
    sqx[t, pl.ds(8, 8), 0:64] = row_sums(gained * gained)
    own_sqx = lambda peer: sqx.at[t]
    start3(x_copy, 0, own_sqx, sqx)

    slots = pos_ref[...]
    owner = slots >> 2
    pos_s[...] = jnp.full(pos_s.shape, -1, jnp.int32)
    pos_s[:, 0 : HIST + CAND] = (
        ((owner >> 3) << 5) | ((owner & 1) << 4) | (((owner >> 1) & 3) << 2) | (slots & 3)
    )
    for u in range(4):
        for kind in range(2):
            row = pos_s[u : u + 1, kind * HIST : (kind + 1) * HIST]
            picked = one_hot(row, 256)
            first = (4 * kind + u) * HIST
            hot[:, first : first + HIST] = picked.astype(BF16)
            hott[first : first + HIST, :] = jnp.transpose(picked).astype(BF16)

    advance(0)
    relay(0)
    wait_in(x_from, 0, own_sqx, sqx)
    sums = sqx[0] + sqx[1] + sqx[2] + sqx[3]
    r_row = lax.rsqrt(sums[0:1] * (1.0 / D) + EPS)
    sq_item = r_row * r_row * sums[8:9]
    rs_row = lax.rsqrt(sq_item * (1.0 / D) + EPS)
    sqy[y] = jnp.concatenate([r_row, rs_row, sq_item] + [r_row] * 5, axis=0)
    own_sqy = lambda peer: sqy.at[y]
    start3(y_copy, 5, own_sqy, sqy)
    relay(1)
    advance(1)
    relay(2)
    wait_in(y_from, 0, own_hd, hd)
    lhs = (hd[...].reshape(256, 1024).astype(F32) * (gi * gu)).astype(BF16)

    def ps_copy(block):
        part, par = block // 2, block % 2
        return send(
            ps.at[block], pr.at[t, par], ps_s.at[block], ps_r.at[t, par], me, part
        )

    def project(block):
        ps[block] = mm(lhs, wt[block].reshape(HD, 1024), 1, 1).astype(BF16)

        @pl.when(block // 2 != t)
        def _():
            ps_copy(block).start()

    def project_step(step):
        if step == 0:
            project(z)
        for way in (1, NZ - 1)[: 2 if step < 3 else 1]:
            project((z + way * (step + 1)) % NZ)

    def partners_in(step):
        if step == 0:
            for half in range(2):
                partner_in(z, half)
        for stream in range(4):
            if step < RING[stream]:
                way = 1 if stream < 2 else NZ - 1
                partner_in((z + (NZ - way) * (step + 1)) % NZ, stream % 2)

    partners_in(0)
    project_step(0)
    wait_in(y_from, 1, own_sel, selb)
    picks = jnp.maximum(jnp.maximum(selb[0], selb[1]), jnp.maximum(selb[2], selb[3]))
    gt[...] = one_hot(picks.astype(jnp.int32), 256).astype(BF16)
    wait_in(y_from, 5, own_sqy, sqy)
    rcol[...] = jnp.concatenate([columns(sqy[b, 0:1])[0:64] for b in range(4)], axis=0)
    rscol[...] = jnp.concatenate([columns(sqy[b, 1:2])[0:64] for b in range(4)], axis=0)
    sq_out = jnp.zeros((8, 1024), F32)
    for b in range(4):
        sq_out = sq_out + mm(
            row_parts(sqy[b, 2:3])[:, 0:64], gt[b * 64 : (b + 1) * 64, :], 1, 0
        )
    sq_out = jnp.sum(sq_out, axis=0, keepdims=True)
    for b in range(NZ):
        sqo[b] = sq_out[:, b * HD : (b + 1) * HD]
    pieces = []
    for par in range(2):
        head = par * 4 + y
        lanes = pl.ds(pl.multiple_of(head * HD, HD), HD)
        piece = hd[:, :, lanes].reshape(256, HD).astype(F32)
        gain = jnp.zeros((1, HD), F32)
        for h in range(8):
            gain = gain + jnp.where(head == h, gi[:, h * HD : (h + 1) * HD], 0.0)
        pieces.append((piece * rcol[...] * gain).astype(BF16))
    oute[...] = mm(gt[...], jnp.concatenate(pieces, axis=1), 0, 0).astype(BF16)
    partners_in(1)
    project_step(1)
    advance(2)
    relay(3)
    both = slice(0, 256)
    to_matched(5, lambda b: sqo.at[b // 2], sqi)
    to_readers(0, oute, bufe, both)
    partners_in(2)
    project_step(2)
    advance(3)
    partners_in(3)
    project_step(3)
    for q in range(4):
        gain_s[q] = jnp.concatenate(
            [gu[:, q * HD : (q + 1) * HD], gu[:, (4 + q) * HD : (5 + q) * HD]], axis=1
        )
    for par in range(2):
        pr[t, par] = ps[2 * t + par]
    for par in range(2):
        for j in (1, 3, 2):
            sender = (t + j) % NT
            send(
                ps.at[2 * t + par], pr.at[sender, par], ps_s.at[2 * t + par],
                ps_r.at[sender, par], me, sender,
            ).wait_recv()
    total = jnp.concatenate(
        [
            pr[0, par].astype(F32) + pr[1, par].astype(F32)
            + pr[2, par].astype(F32) + pr[3, par].astype(F32)
            for par in range(2)
        ],
        axis=1,
    ) * (rcol[...] * rscol[...])[:, 0:1]
    q32[...] = total
    heads, _ = norm_heads(total)
    outq[...] = mm(gt[...], jnp.concatenate(heads, axis=1).astype(BF16), 0, 0).astype(BF16)
    halves = (slice(0, HD), slice(HD, 2 * HD))
    to_readers(1, outq, bufq, halves[0])
    to_readers(4, outq, bufq, halves[1])

    off = (me % 8) * 16
    blocks = jnp.where((iota((256, 16), 0) >> 4) == iota((256, 16), 1), 1.0, 0.0).astype(BF16)
    in_lane = iota((256, HD), 1) == off + (iota((256, HD), 0) & 15)
    all_in(5, sqi)
    came = jnp.concatenate([sqi[b] for b in range(16)], axis=0)
    high, mid, low = split3(came)
    wide = mm(blocks, high, 1, 0) + mm(blocks, mid, 1, 0) + mm(blocks, low, 1, 0)
    sqm[...] = jnp.broadcast_to(lane_sum(jnp.where(in_lane, wide, 0.0)), (256, HD))
    rsm[...] = lax.rsqrt(sqm[...] * (1.0 / D) + EPS)
    sqf_s[...] = jnp.broadcast_to(
        lane_sum(mm(hott[0:512], lane_parts(sqm[...]), 1, 0)), (512, HIST)
    )
    sqc = jnp.sum(mm(lane_parts(sqm[...]), hot[:, 512:1024], 0, 0), axis=0, keepdims=True)
    for u in range(4):
        sqc_s[u] = sqc[:, u * HIST : (u + 1) * HIST]
    twice = lambda values: jnp.concatenate([values, values], axis=1)
    all_in(0, bufe)
    for q in range(4):
        low = (bufe[q].astype(F32) * twice(rsm[...]) * gain_s[q]).astype(BF16)
        nrm[q] = low
        heads, _ = norm_heads(low.astype(F32))
        knb[q] = jnp.concatenate(heads, axis=1).astype(BF16)
    for q in range(4):
        kn_s[q] = mm(hott[0:512], knb[q], 1, 0).astype(BF16)
        v_s[q] = mm(hott[0:512], nrm[q], 1, 0).astype(BF16)
    for q in range(4):
        rc_s[q] = mm(hott[...], bufe[q], 1, 0).astype(BF16)

    scale = HD ** (-0.5)
    row_id = iota((HIST, HIST), 0)
    col_id = iota((HIST, HIST), 1)

    def follow_of(rows):
        moved = pltpu.roll(rows, HIST - 1, 0)
        return jnp.where(iota(rows.shape, 0) < HIST - 1, moved, 0.0)

    def st_copy(u, j):
        peer = (t + j) % NT
        return send(st_r.at[t, u], st_r.at[t, u], xs.at[6 + u, peer], xr.at[6 + u, t], me, peer)

    def st_from(u, j):
        sender = (t + NT - j) % NT
        return send(
            st_r.at[t, u], st_r.at[sender, u], xs.at[6 + u, sender], xr.at[6 + u, sender],
            me, sender,
        )

    def user_rows(u):
        return pl.ds(pl.multiple_of(u * HIST, HIST), HIST)

    def attend(first, par):
        lanes = halves[par]
        tasks = [(first + k, q, 4 * k + q) for k in range(2) for q in range(4)]
        for u, q, slot in tasks:
            span = user_rows(u)
            p_t[slot] = mm(qn_s[q, span, lanes], kn_s[q, span, lanes], 1, 1)
        for u, q, slot in tasks:
            mask = (col_id <= row_id) & (col_id < len_ref[u])
            weights = jnp.where(mask, jnp.exp(p_t[slot] * scale), 0.0)
            w_s[2 * q + par, user_rows(u)] = (weights * (1.0 / lane_sum(weights))).astype(BF16)
        for u, q, slot in tasks:
            span = user_rows(u)
            o_s[q, span, lanes] = rc_s[q, span, lanes].astype(F32) + mm(
                w_s[2 * q + par, span], v_s[q, span, lanes], 1, 0
            )

    def first_half(i, carry):
        attend(2 * i, 0)
        return carry

    def score(u):
        span = user_rows(u)
        cspan = user_rows(u + 4)
        own = jnp.zeros((HIST, 1), F32)
        hit = jnp.zeros((HIST, 1), F32)
        neg = jnp.zeros((HIST, HIST), F32)
        for q in range(4):
            out = o_s[q, span]
            own = own + lane_sum(out * out)
            hit = hit + lane_sum(out * follow_of(rc_s[q, span].astype(F32)))
            high = out.astype(BF16)
            low = (out - high.astype(F32)).astype(BF16)
            cands = rc_s[q, cspan]
            neg = neg + mm(high, cands, 1, 1) + mm(low, cands, 1, 1)
        stats = neg + jnp.where(col_id == CAND, own, 0.0) + jnp.where(col_id == CAND + 1, hit, 0.0)
        st_r[t, u] = stats.astype(BF16)
        for j in (2, 1, 3):
            st_copy(u, j).start()

    def second_half(i, carry):
        attend(2 * i, 1)
        score(2 * i)
        score(2 * i + 1)
        return carry

    def turn_weights(k, carry):
        for u in range(4):
            span = slice(u * HIST, (u + 1) * HIST)
            wt_s[k, span] = jnp.transpose(w_s[k, span].astype(F32)).astype(BF16)
        return carry

    for par, step in ((0, first_half), (1, second_half)):
        all_in(1 if par == 0 else 4, outq.at[:, halves[0]])
        for q in range(4):
            qn_s[q, :, halves[par]] = mm(hott[0:512], bufq[q, :, halves[par]], 1, 0).astype(BF16)
        lax.fori_loop(0, 2, step, 0)
    lax.fori_loop(0, 8, turn_weights, 0)

    def losses(u, carry):
        for j in (1, 3, 2):
            st_from(u, j).wait_recv()
        stats = (
            st_r[0, u].astype(F32) + st_r[1, u].astype(F32)
            + st_r[2, u].astype(F32) + st_r[3, u].astype(F32)
        )
        is_cand = col_id < CAND
        neg = jnp.where(is_cand, stats, 0.0)
        own = lane_sum(jnp.where(col_id == CAND, stats, 0.0))
        hit = lane_sum(jnp.where(col_id == CAND + 1, stats, 0.0))
        sq_follow = pltpu.roll(sqf_s[user_rows(u)], HIST - 1, 0)[:, 0:1]
        rn = lax.rsqrt(own + EPS)
        rf = lax.rsqrt(sq_follow + EPS)
        rc = lax.rsqrt(sqc_s[u] + EPS)
        tl = SOFT * hit * rn * rf
        nl = SOFT * neg * rn * rc
        en = jnp.where(is_cand, jnp.exp(nl), 0.0)
        et = jnp.exp(tl)
        whole = et + lane_sum(en)
        span = len_ref[u] - 1
        over = 1.0 / (jnp.full((HIST, 1), 0, jnp.int32) + span).astype(F32)
        valid = iota((HIST, 1), 0) < span
        terms = jnp.where(valid, (jnp.log(whole) - tl) * over, 0.0)
        loss_ref[u] = jnp.broadcast_to(jnp.sum(terms, axis=0, keepdims=True), (1, HIST))
        g = jnp.where(valid, float(D) * over, 0.0)
        dtl = g * (et / whole - 1.0)
        dnl = (g / whole) * en
        dsc[u, 0] = jnp.broadcast_to(
            -rn * rn * (dtl * tl + lane_sum(dnl * nl)), (HIST, HIST)
        )
        dsc[u, 1] = jnp.broadcast_to(dtl * (SOFT * rn * rf), (HIST, HIST))
        dneg = dnl * (SOFT * rn * rc)
        dneg_s[u] = dneg.astype(BF16)
        dnegt_s[u] = jnp.transpose(dneg).astype(BF16)
        dsqf = jnp.broadcast_to(-0.5 * dtl * tl * rf * rf, (HIST, HIST))
        gfol[user_rows(u)] = pltpu.roll(dsqf, 1, 0)
        grow[u] = -0.5 * rc * rc * jnp.sum(dnl * nl, axis=0, keepdims=True)
        return carry

    lax.fori_loop(0, 4, losses, 0)

    def backward_step(par, i):
        lanes = halves[par]
        tasks = [
            ((y + 1 + 2 * i + k) % 4, k, slice(u * HIST, (u + 1) * HIST), u, 4 * k + u)
            for k in range(2)
            for u in range(4)
        ]
        for q, k, span, u, slot in tasks:
            cspan = slice((4 + u) * HIST, (5 + u) * HIST)
            dhit = dsc[u, 1]
            out = o_s[q, span, lanes]
            rows = rc_s[q, span, lanes].astype(F32)
            dout = (
                dsc[u, 0] * out
                + dhit * follow_of(rows)
                + mm(dneg_s[u], rc_s[q, cspan, lanes], 1, 0)
            )
            dout_t[k, span] = dout.astype(BF16)
            drc_s[q, span, lanes] = (dout + pltpu.roll(dhit * out, 1, 0)).astype(BF16)
            drc_s[q, cspan, lanes] = mm(dnegt_s[u], out.astype(BF16), 1, 0).astype(BF16)
        for q, k, span, u, slot in tasks:
            p_t[slot] = mm(dout_t[k, span], v_s[q, span, lanes], 1, 1)
        for q, k, span, u, slot in tasks:
            dw = p_t[slot]
            wide = w_s[2 * q + par, span].astype(F32)
            ds_t[slot] = (wide * (dw - lane_sum(dw * wide)) * scale).astype(BF16)
        for q, k, span, u, slot in tasks:
            dq_t[k, span] = mm(ds_t[slot], kn_s[q, span, lanes], 1, 0).astype(BF16)
            dk_s[q, span, lanes] = mm(ds_t[slot], qn_s[q, span, lanes], 0, 0).astype(BF16)
            dv_s[q, span, lanes] = mm(wt_s[2 * q + par, span], dout_t[k, span], 1, 0).astype(BF16)
        for k in range(2):
            q = tasks[4 * k][0]
            dqo[q, :, lanes] = mm(hot[:, 0:512], dq_t[k], 1, 0).astype(BF16)
        for k in range(2):
            to_group((2, 7)[par], dqo, rq, tasks[4 * k][0], i + k == 2, lanes)

    def backward_first(i, carry):
        backward_step(0, i)
        return carry

    def backward_second(i, carry):
        backward_step(1, i)
        return carry

    lax.fori_loop(0, 2, backward_first, 0)
    lax.fori_loop(0, 2, backward_second, 0)

    nbs[...] = jnp.zeros(nbs.shape, F32)

    def return_quarter(i, carry):
        q = (y + 1 + i) % 4
        dk = mm(hot[:, 0:512], dk_s[q], 1, 0)
        dn = mm(hot[:, 0:512], dv_s[q], 1, 0) + norm_heads_back(nrm[q].astype(F32), dk)
        dn = dn * gain_s[q]
        nbs[...] += jnp.broadcast_to(lane_sum(dn * bufe[q].astype(F32)), (256, HD))
        eo[q] = (mm(hot[...], drc_s[q], 1, 0) + dn * twice(rsm[...])).astype(BF16)
        return carry

    lax.fori_loop(0, 4, return_quarter, 0)
    gsq = lane_sum(mm(hot[:, 0:512], lane_parts(gfol[...]), 1, 0)) + lane_sum(
        mm(
            hot[:, 512:1024],
            row_parts(jnp.concatenate([grow[u] for u in range(4)], axis=1)), 1, 1,
        )
    )
    placed = []
    for values in (jnp.broadcast_to(gsq, (256, HD)), nbs[...]):
        high, mid, low = split3(jnp.where(in_lane, values, 0.0))
        placed.append(mm(blocks, high, 0, 0) + mm(blocks, mid, 0, 0) + mm(blocks, low, 0, 0))
    for b in range(16):
        sco[b] = jnp.concatenate([part[b : b + 1] for part in placed], axis=1)
    to_matched(6, lambda b: sco.at[b], sci)

    def return_group(i, carry):
        to_group(3, eo, re, (y + 1 + i) % 4, i == 3, both)
        return carry


    chunks = (((y + 2) % NY, (y + 1) % NY), ((y + 3) % NY, y))

    def dq_first(peer, sender):
        return send(
            dqg.at[t, 0], dqg.at[sender, 0], xs.at[2, peer], xr.at[2, sender], me, peer
        )

    def dq_second(part, k, peer, sender):
        b = chunks[part][k]
        index = (1, 3, 4, 10)[2 * part + k]
        return send(
            dqg.at[t, 1, b], dqg.at[sender, 1, b], xs.at[index, peer], xr.at[index, sender],
            me, peer,
        )

    def item_dq(par):
        lanes = halves[par]
        out = head_back(q32[:, lanes], mm(gt[...], rq[:, lanes], 1, 0)).astype(BF16)
        dqg[t, par] = out.reshape(4, 64, HD)
        return row_sums(out.astype(F32) * q32[:, lanes])

    lax.fori_loop(0, 4, return_group, 0)
    all_in(2, rq.at[:, halves[0]])
    dots = item_dq(0)
    for j in (2, 1, 3):
        dq_first((t + j) % NT, t).start()
    all_in(6, sci)
    pairs = [sci[2 * b] + sci[2 * b + 1] for b in range(NZ)]
    item_terms = []
    for lanes in (slice(0, HD), slice(HD, 2 * HD)):
        row = jnp.concatenate([pair[:, lanes] for pair in pairs], axis=1)
        item_terms.append(jnp.sum(mm(row_parts(row), gt[...], 1, 1), axis=0, keepdims=True))
    sdy[y, pl.ds(8, 8), :] = jnp.broadcast_to(item_terms[0], (8, 256))
    rs_all = mm(jnp.ones((8, HD), BF16), lane_parts(rscol[...]), 1, 1)[0:1]
    all_in(7, rq.at[:, halves[1]])
    dots = dots + item_dq(1)
    sdx[t] = dots + rs_all * item_terms[1]
    own_sdx = lambda peer: sdx.at[t]
    start3(x_copy, 5, own_sdx, sdx)
    for part in range(2):
        for j in (2, 1, 3):
            for k in range(2):
                dq_second(part, k, (t + j) % NT, t).start()
    for j in (1, 3, 2):
        sender = (t + j) % NT
        dq_first(sender, sender).wait_recv()
    acc = jnp.zeros((256, 1024), F32)
    for tt in range(NT):
        acc = acc + mm(dqg[tt, 0].reshape(256, HD), wt[2 * tt].reshape(HD, 1024), 1, 0)
    acc_s[...] = acc.reshape(4, 64, 1024)
    gws_of = lambda peer: gws.at[peer]
    for part in range(2):
        for j in (1, 3, 2):
            sender = (t + j) % NT
            for k in range(2):
                dq_second(part, k, sender, sender).wait_recv()
        acc = jnp.concatenate([acc_s[b] for b in chunks[part]], axis=0)
        for tt in range(NT):
            acc = acc + mm(
                jnp.concatenate([dqg[tt, 1, b] for b in chunks[part]], axis=0),
                wt[2 * tt + 1].reshape(HD, 1024), 1, 0,
            )
        acc = acc.astype(BF16)
        for k, b in enumerate(chunks[part]):
            gws[b] = acc[k * 64 : (k + 1) * 64]
        if part == 0:
            wait_in(x_from, 5, own_sdx, sdx)
            sdy[y, pl.ds(0, 8), :] = sdx[0] + sdx[1] + sdx[2] + sdx[3]
            own_sdy = lambda peer: sdy.at[y]
            start3(y_copy, 4, own_sdy, sdy)
        for j in ((2, 1), (3,))[part]:
            y_copy(2, gws_of, gwr, j).start()
    gwr[y] = gws[y]
    all_in(3, re)
    es[...] = mm(gt[...], re[...], 1, 0).astype(BF16).reshape(4, 64, 256)
    es_of = lambda peer: es.at[peer]
    start3(y_copy, 3, es_of, er)
    er[y] = es[y]

    mine = pl.ds(pl.multiple_of(y * 64, 64), 64)
    emb = (hidden_ref[...].astype(F32) * rcol[mine, 0:1] * gi).astype(BF16).astype(F32)
    rs_own = rscol[mine, 0:1]
    wait_in(y_from, 4, own_sdy, sdy)
    last = sdy[0] + sdy[1] + sdy[2] + sdy[3]
    sqm[...] = columns(2.0 * last[8:9] - (1.0 / D) * rs_all * rs_all * last[0:1])
    coef = sqm[mine, 0:1]
    direct = emb * coef
    wait_in(y_from, 2, gws_of, gwr)
    gw = (
        gwr[0].astype(F32) + gwr[1].astype(F32) + gwr[2].astype(F32) + gwr[3].astype(F32)
    ) * gu * rs_own + direct
    wait_in(y_from, 3, es_of, er)
    for h in range(8):
        lanes = slice(h * HD, (h + 1) * HD)
        par, q = h // 4, h % 4
        grad_ref[:, lanes] = er[q, :, halves[par]].astype(F32) + gw[:, lanes]

    for k, src, dst in (
        (0, own_hd, hd), (1, own_sel, selb), (2, gws_of, gwr), (3, es_of, er), (4, own_sdy, sdy),
        (5, own_sqy, sqy),
    ):
        wait_out(y_copy, k, src, dst)
    for k, src, dst in (
        (0, own_sqx, sqx), (5, own_sdx, sdx)
    ):
        wait_out(x_copy, k, src, dst)
    for j in (1, 3, 2):
        peer = (t + j) % NT
        dq_first(peer, t).wait_send()
        for part in range(2):
            for k in range(2):
                dq_second(part, k, peer, t).wait_send()
    for j in (1, 3, 2):
        for par in range(2):
            ps_copy((t + j) % NT * 2 + par).wait_send()
    for u in range(4):
        for j in (1, 3, 2):
            st_copy(u, j).wait_send()
    for stream in range(4):
        for step in range(RING[stream]):
            ring(stream, step).wait_send()
    for b in range(NZ):
        for half in range(2):
            partner(b, c, half).wait_send()
    most = pl.ds(0, (NS - 1) * 16)
    all_out(0, oute.at[most])
    all_out(1, outq.at[most, halves[0]])
    all_out(4, outq.at[most, halves[1]])
    all_out(2, rq.at[most, halves[0]])
    all_out(7, rq.at[most, halves[1]])
    all_out(3, re.at[most])
    all_out(5, sqi.at[pl.ds(0, 15)])
    all_out(6, sci.at[pl.ds(0, 15)])


def local(item_hidden, item_gain, send_item, pos_slot, hist_len, user_gain, query_weight):
    vmem = pltpu.VMEM
    dma = pltpu.SemaphoreType.DMA
    quarter = lambda kind: vmem((4, 256, 256), kind)
    grad, loss = pl.pallas_call(
        kernel,
        out_shape=(
            jax.ShapeDtypeStruct((64, 1024), F32),
            jax.ShapeDtypeStruct((4, 1, HIST), F32),
        ),
        in_specs=[pl.BlockSpec(memory_space=pltpu.HBM)] * 7,
        out_specs=(
            pl.BlockSpec(memory_space=pltpu.VMEM),
            pl.BlockSpec(memory_space=pltpu.VMEM),
        ),
        scratch_shapes=[
            pltpu.SMEM((4,), jnp.int32),
            vmem((64, 1024), BF16),
            vmem((1024,), BF16),
            vmem((1024,), BF16),
            vmem((4, 64), jnp.int32),
            vmem((4, HIST + CAND), jnp.int32),
            dma((8,)),
            vmem((4, 64, 1024), BF16),
            vmem((4, 1, 1024), F32),
            vmem((8, 2, 64, 1024), BF16),
            vmem((4, 16, HIST), F32),
            vmem((4, 8, HIST), F32),
            vmem((8, 256, HD), BF16),
            vmem((4, 2, 256, HD), BF16),
            vmem((1024, 256), BF16),
            vmem((1024, 256), BF16),
            quarter(BF16),
            quarter(BF16),
            vmem((256, 1024), BF16),
            quarter(BF16),
            quarter(BF16),
            vmem((8, 1, HIST), F32),
            vmem((16, 1, HIST), F32),
            vmem((256, HIST), F32),
            vmem((256, HIST), F32),
            vmem((256, 256), F32),
            vmem((256, HIST), F32),
            vmem((256, HIST), F32),
            vmem((4, 2 * HIST), jnp.int32),
            vmem((256, 1024), BF16),
            vmem((1024, 256), BF16),
            vmem((512, HIST), F32),
            vmem((4, 1, HIST), F32),
            vmem((4, 1, 256), F32),
            vmem((4, 1024, 256), BF16),
            vmem((4, 512, 256), BF16),
            vmem((4, 512, 256), BF16),
            vmem((4, 512, 256), BF16),
            vmem((8, 512, HIST), BF16),
            vmem((8, 512, HIST), BF16),
            vmem((8, HIST, HIST), F32),
            vmem((8, HIST, HIST), BF16),
            vmem((4, 512, 256), F32),
            vmem((4, 4, HIST, HIST), BF16),
            vmem((4, 2, HIST, HIST), F32),
            vmem((4, HIST, HIST), BF16),
            vmem((4, HIST, HIST), BF16),
            vmem((512, HIST), F32),
            vmem((4, 1, HIST), F32),
            vmem((2, 512, HD), BF16),
            vmem((2, 512, HD), BF16),
            vmem((4, 512, 256), BF16),
            vmem((4, 512, 256), BF16),
            vmem((4, 1024, 256), BF16),
            vmem((256, HIST), F32),
            quarter(BF16),
            quarter(BF16),
            vmem((1024, 256), BF16),
            vmem((1024, 256), BF16),
            vmem((16, 1, 256), F32),
            vmem((16, 1, 256), F32),
            vmem((4, 2, 4, 64, HD), BF16),
            vmem((4, 64, 1024), F32),
            vmem((4, 64, 1024), BF16),
            vmem((4, 64, 1024), BF16),
            vmem((4, 64, 256), BF16),
            vmem((4, 64, 256), BF16),
            vmem((4, 8, 256), F32),
            vmem((4, 16, 256), F32),
            dma((11, 4)),
            dma((11, 4)),
            dma((6, 4)),
            dma((6, 4)),
            dma((4, 4)),
            dma((4, 4)),
            dma((8, 2)),
            dma((8, 2)),
            dma((8,)),
            dma((8,)),
            dma((8,)),
            dma((4, 2)),
            pltpu.SemaphoreType.REGULAR((2, 4)),
        ],
        compiler_params=pltpu.CompilerParams(
            collective_id=0, has_side_effects=True, vmem_limit_bytes=40 * 1024 * 1024
        ),
    )(
        *[
            pltpu.with_memory_space_constraint(value, pltpu.HBM)
            for value in (
                hist_len, item_hidden, query_weight.T, item_gain, user_gain, send_item[0].T,
                pos_slot,
            )
        ]
    )
    return (grad, loss[:, 0, 0])


def solution(mesh):
    placed = (
        P("sect", "tp"),
        P("tp"),
        P("sect", None, None),
        P("sect", None),
        P("sect"),
        P("tp"),
        P("tp", "sect"),
    )
    return jax.shard_map(
        local, mesh=mesh, in_specs=placed, out_specs=(P("sect", "tp"), P("sect")), check_vma=False
    )
```

```python
import jax
import jax.numpy as jnp
from jax import lax
from jax.experimental import pallas as pl
from jax.experimental.pallas import tpu as pltpu
from jax.sharding import PartitionSpec as P

D = 4096
HD = 128
HIST = 128
CAND = 64
NZ, NY, NT = 8, 4, 4
NS = 64
EPS = 1e-06
SOFT = 20.0
F32, BF16 = jnp.float32, jnp.bfloat16
MESH = pl.DeviceIdType.MESH
RING = (4, 3, 3, 4)


def mm(a, b, ca, cb, precision=None):
    return lax.dot_general(
        a, b, (((ca,), (cb,)), ((), ())), preferred_element_type=F32, precision=precision
    )


def split3(values):
    high = values.astype(BF16)
    rest = values - high.astype(F32)
    mid = rest.astype(BF16)
    return high, mid, (rest - mid.astype(F32)).astype(BF16)


def row_parts(row):
    parts = split3(jnp.broadcast_to(row, (8, row.shape[1])))
    index = iota((8, row.shape[1]), 0)
    out = jnp.where(index == 0, parts[0].astype(F32), 0.0)
    out = jnp.where(index == 1, parts[1].astype(F32), out)
    return jnp.where(index == 2, parts[2].astype(F32), out).astype(BF16)


def lane_parts(values):
    parts = split3(values)
    index = iota(values.shape, 1)
    out = jnp.where(index == 0, parts[0].astype(F32), 0.0)
    out = jnp.where(index == 1, parts[1].astype(F32), out)
    return jnp.where(index == 2, parts[2].astype(F32), out).astype(BF16)


def columns(row):
    return mm(row_parts(row), jnp.ones((8, 128), BF16), 0, 0)


def row_sums(values):
    ones = jnp.ones((8, values.shape[1]), BF16)
    high, mid, low = split3(values)
    return mm(ones, high, 1, 1) + mm(ones, mid, 1, 1) + mm(ones, low, 1, 1)


def lane_sum(values):
    return jnp.sum(values, axis=1, keepdims=True)


def iota(shape, dim):
    return lax.broadcasted_iota(jnp.int32, shape, dim)


def one_hot(row, count):
    return jnp.where(iota((count, row.shape[1]), 0) == row, 1.0, 0.0)


def norm_heads(values):
    heads, roots = [], []
    for par in range(2):
        part = values[:, par * HD : (par + 1) * HD]
        root = lax.rsqrt(lane_sum(part * part) * (1.0 / HD) + EPS)
        heads.append(part * root)
        roots.append(root)
    return heads, roots


def head_back(values, grad):
    root = lax.rsqrt(lane_sum(values * values) * (1.0 / HD) + EPS)
    head = values * root
    return root * (grad - head * (lane_sum(grad * head) * (1.0 / HD)))


def norm_heads_back(values, grads):
    heads, roots = norm_heads(values)
    out = []
    for par in range(2):
        grad = grads[:, par * HD : (par + 1) * HD]
        out.append(
            roots[par] * (grad - heads[par] * (lane_sum(grad * heads[par]) * (1.0 / HD)))
        )
    return jnp.concatenate(out, axis=1)


def kernel(
    len_in, hidden_in, w_in, gi_in, gu_in, send_in, pos_in,
    grad_ref, loss_ref,
    len_ref, hidden_ref, gi_ref, gu_ref, send_ref, pos_ref, in_sem,
    hd, selb, wt, sqx, sqy, ps, pr, oute, outq, bufe, bufq, gt, nrm, knb, sqo, sqi, sqm, rsm, q32,
    rcol, rscol, pos_s, hot, hott, sqf_s, sqc_s, gain_s,
    rc_s, kn_s, v_s, qn_s, w_s, wt_s, p_t, ds_t, o_s, st_r, dsc, dneg_s, dnegt_s, gfol, grow,
    dout_t, dq_t, dk_s, dv_s, drc_s, nbs, dqo, eo, rq, re, sco, sci,
    dqg, acc_s, gws, gwr, es, er, sdx, sdy,
    xs, xr, ys, yr, ring_s, ring_r, par_s, par_r, a2a_s, a2a_r, ps_s, ps_r, hello,
):
    me = lax.axis_index("sect")
    t = lax.axis_index("tp")
    z, y, c = me // 8, (me // 2) % 4, me % 2
    blk = z * 2 + c

    def send(src, dst, ssem, rsem, sect, tp):
        return pltpu.make_async_remote_copy(
            src_ref=src, dst_ref=dst, send_sem=ssem, recv_sem=rsem,
            device_id=(sect, tp), device_id_type=MESH,
        )

    def sect_of(zz, yy, cc):
        return zz * 8 + yy * 2 + cc

    def x_copy(k, src, dst, j):
        peer = (t + j) % NT
        return send(src(peer), dst.at[t], xs.at[k, peer], xr.at[k, t], me, peer)

    def x_from(k, src, dst, j):
        sender = (t + NT - j) % NT
        return send(src(t), dst.at[sender], xs.at[k, sender], xr.at[k, sender], me, sender)

    def y_copy(k, src, dst, j):
        peer = (y + j) % NY
        return send(src(peer), dst.at[y], ys.at[k, peer], yr.at[k, y], sect_of(z, peer, c), t)

    def y_from(k, src, dst, j):
        sender = (y + NY - j) % NY
        return send(
            src(y), dst.at[sender], ys.at[k, sender], yr.at[k, sender], sect_of(z, sender, c), t
        )

    def start3(copy, k, src, dst):
        for j in (2, 1, 3):
            copy(k, src, dst, j).start()

    def wait_in(came, k, src, dst):
        for j in (1, 3, 2):
            came(k, src, dst, j).wait_recv()

    def wait_out(copy, k, src, dst):
        for j in (1, 3, 2):
            copy(k, src, dst, j).wait_send()

    def rows_of(first):
        return pl.ds(pl.multiple_of(first * 16, 16), 16)

    def to_readers(k, out, buf, lanes):
        pltpu.make_async_copy(
            out.at[rows_of(me), lanes], buf.at[y, rows_of(blk), lanes], a2a_r.at[k]
        ).start()

        def step(j, carry):
            peer = (me + j) % NS
            send(
                out.at[rows_of(peer), lanes], buf.at[y, rows_of(blk), lanes],
                a2a_s.at[k], a2a_r.at[k], peer, t,
            ).start()
            return carry

        lax.fori_loop(1, NS, step, 0, unroll=7)

    def to_group(k, out, buf, group, same, lanes):
        def copy(j):
            b = (blk + j) % 16
            return send(
                out.at[group, rows_of(b), lanes], buf.at[rows_of(me), lanes],
                a2a_s.at[k], a2a_r.at[k], sect_of(b // 2, group, b % 2), t,
            )

        @pl.when(same)
        def _():
            pltpu.make_async_copy(
                out.at[group, rows_of(blk), lanes], buf.at[rows_of(me), lanes], a2a_r.at[k]
            ).start()

        @pl.when(jnp.logical_not(same))
        def _():
            copy(0).start()

        def step(j, carry):
            copy(j).start()
            return carry

        lax.fori_loop(1, 16, step, 0, unroll=5)

    def to_matched(k, src_of, dst):
        pltpu.make_async_copy(src_of(blk), dst.at[blk], a2a_r.at[k]).start()

        def step(j, carry):
            b = (blk + j) % 16
            send(
                src_of(b), dst.at[blk], a2a_s.at[k], a2a_r.at[k], sect_of(b // 2, y, b % 2), t
            ).start()
            return carry

        lax.fori_loop(1, 16, step, 0, unroll=5)

    def all_in(k, view):
        pltpu.make_async_copy(view, view, a2a_r.at[k]).wait()

    def all_out(k, view):
        pltpu.make_async_copy(view, view, a2a_s.at[k]).wait()

    def ring(stream, step):
        way = 1 if stream < 2 else NZ - 1
        block = (z + (NZ - way) * step) % NZ
        part = wt.at[block, c, pl.ds((stream % 2) * 32, 32)]
        return send(
            part, part, ring_s.at[stream, step], ring_r.at[stream, step],
            sect_of((z + way) % NZ, y, c), t,
        )

    def ring_from(stream, step):
        way = 1 if stream < 2 else NZ - 1
        block = (z + (NZ - way) * (step + 1)) % NZ
        part = wt.at[block, c, pl.ds((stream % 2) * 32, 32)]
        return block, send(
            part, part, ring_s.at[stream, step], ring_r.at[stream, step],
            sect_of((z + way) % NZ, y, c), t,
        )

    def partner(block, core, half):
        part = wt.at[block, core, pl.ds(half * 32, 32)]
        return send(
            part, part, par_s.at[block, half], par_r.at[block, half], sect_of(z, y, 1 - c), t
        )

    def partner_in(block, half):
        partner(block, 1 - c, half).wait_recv()

    def advance(step):
        for stream in (0, 2, 1, 3):
            if step >= RING[stream]:
                continue
            block, came = ring_from(stream, step)
            came.wait_recv()
            if step + 1 < RING[stream]:
                ring(stream, step + 1).start()
            partner(block, c, stream % 2).start()

    barrier = pltpu.get_barrier_semaphore()
    for j in range(1, 8):
        pl.semaphore_signal(
            barrier, inc=1, device_id=(z * 8 + (me + j) % 8, t), device_id_type=MESH
        )
    for j in (1, NZ - 1):
        pl.semaphore_signal(
            barrier, inc=1, device_id=(sect_of((z + j) % NZ, y, c), t), device_id_type=MESH
        )
    for j in range(1, NT):
        pl.semaphore_signal(barrier, inc=1, device_id=(me, (t + j) % NT), device_id_type=MESH)

    loads = [
        pltpu.make_async_copy(src, dst, in_sem.at[k])
        for k, (src, dst) in enumerate(
            (
                (send_in, send_ref), (w_in, wt.at[z, c]), (hidden_in, hd.at[y]),
                (gi_in, gi_ref), (gu_in, gu_ref), (hidden_in, hidden_ref), (pos_in, pos_ref),
                (len_in, len_ref),
            )
        )
    ]
    for load in loads:
        load.start()
    for load in loads:
        load.wait()
    sqx[t] = jnp.zeros((16, HIST), F32)
    spread = jnp.where((iota((64, 1024), 1) >> 4) == iota((64, 1024), 0), 1.0, 0.0).astype(BF16)
    named = mm(send_ref[...].astype(F32).astype(BF16), spread, 1, 0)
    lane = iota((1, 1024), 1)
    pick = jnp.full((1, 1024), -1.0, F32)
    for s in range(4):
        pick = jnp.where((lane & 3) == s, named[s : s + 1], pick)
    base = (jnp.zeros((1, 1024), jnp.int32) + y * 64).astype(F32)
    selb[y] = jnp.where((((lane >> 2) & 3) == y) & (pick >= 0.0), pick + base, -1.0)
    pl.semaphore_wait(barrier, 7 + 2 + NT - 1)

    def greet(step):
        for way in range(2):
            if step < 4 - way:
                peer = (z + 1) % NZ if way == 0 else (z + NZ - 1) % NZ
                pl.semaphore_signal(
                    hello.at[way, step], inc=1, device_id=(sect_of(peer, y, c), t),
                    device_id_type=MESH,
                )

    def relay(step):
        for way in range(2):
            if step < 4 - way:
                pl.semaphore_wait(hello.at[way, step], 1)
        greet(step + 1)

    greet(0)
    own_hd = lambda peer: hd.at[y]
    own_sel = lambda peer: selb.at[y]
    for stream in (0, 2, 1, 3):
        ring(stream, 0).start()
    start3(y_copy, 0, own_hd, hd)
    start3(y_copy, 1, own_sel, selb)
    for half in range(2):
        partner(z, c, half).start()

    gi = gi_ref[...].astype(F32).reshape(1, 1024)
    gu = gu_ref[...].astype(F32).reshape(1, 1024)
    hidden = hidden_ref[...].astype(F32)
    gained = hidden * gi
    sqx[t, pl.ds(0, 8), 0:64] = row_sums(hidden * hidden)
    sqx[t, pl.ds(8, 8), 0:64] = row_sums(gained * gained)
    own_sqx = lambda peer: sqx.at[t]
    start3(x_copy, 0, own_sqx, sqx)

    slots = pos_ref[...]
    owner = slots >> 2
    pos_s[...] = jnp.full(pos_s.shape, -1, jnp.int32)
    pos_s[:, 0 : HIST + CAND] = (
        ((owner >> 3) << 5) | ((owner & 1) << 4) | (((owner >> 1) & 3) << 2) | (slots & 3)
    )
    for u in range(4):
        for kind in range(2):
            row = pos_s[u : u + 1, kind * HIST : (kind + 1) * HIST]
            picked = one_hot(row, 256)
            first = (4 * kind + u) * HIST
            hot[:, first : first + HIST] = picked.astype(BF16)
            hott[first : first + HIST, :] = jnp.transpose(picked).astype(BF16)

    advance(0)
    relay(0)
    wait_in(x_from, 0, own_sqx, sqx)
    sums = sqx[0] + sqx[1] + sqx[2] + sqx[3]
    r_row = lax.rsqrt(sums[0:1] * (1.0 / D) + EPS)
    sq_item = r_row * r_row * sums[8:9]
    rs_row = lax.rsqrt(sq_item * (1.0 / D) + EPS)
    sqy[y] = jnp.concatenate([r_row, rs_row, sq_item] + [r_row] * 5, axis=0)
    own_sqy = lambda peer: sqy.at[y]
    start3(y_copy, 5, own_sqy, sqy)
    relay(1)
    advance(1)
    relay(2)
    wait_in(y_from, 0, own_hd, hd)
    lhs = (hd[...].reshape(256, 1024).astype(F32) * (gi * gu)).astype(BF16)

    def ps_copy(block):
        part, par = block // 2, block % 2
        return send(
            ps.at[block], pr.at[t, par], ps_s.at[block], ps_r.at[t, par], me, part
        )

    def project(block):
        ps[block] = mm(lhs, wt[block].reshape(HD, 1024), 1, 1).astype(BF16)

        @pl.when(block // 2 != t)
        def _():
            ps_copy(block).start()

    def project_step(step):
        if step == 0:
            project(z)
        for way in (1, NZ - 1)[: 2 if step < 3 else 1]:
            project((z + way * (step + 1)) % NZ)

    def partners_in(step):
        if step == 0:
            for half in range(2):
                partner_in(z, half)
        for stream in range(4):
            if step < RING[stream]:
                way = 1 if stream < 2 else NZ - 1
                partner_in((z + (NZ - way) * (step + 1)) % NZ, stream % 2)

    partners_in(0)
    project_step(0)
    wait_in(y_from, 1, own_sel, selb)
    picks = jnp.maximum(jnp.maximum(selb[0], selb[1]), jnp.maximum(selb[2], selb[3]))
    gt[...] = one_hot(picks.astype(jnp.int32), 256).astype(BF16)
    wait_in(y_from, 5, own_sqy, sqy)
    rcol[...] = jnp.concatenate([columns(sqy[b, 0:1])[0:64] for b in range(4)], axis=0)
    rscol[...] = jnp.concatenate([columns(sqy[b, 1:2])[0:64] for b in range(4)], axis=0)
    sq_out = jnp.zeros((8, 1024), F32)
    for b in range(4):
        sq_out = sq_out + mm(
            row_parts(sqy[b, 2:3])[:, 0:64], gt[b * 64 : (b + 1) * 64, :], 1, 0
        )
    sq_out = jnp.sum(sq_out, axis=0, keepdims=True)
    for b in range(NZ):
        sqo[b] = sq_out[:, b * HD : (b + 1) * HD]
    pieces = []
    for par in range(2):
        head = par * 4 + y
        lanes = pl.ds(pl.multiple_of(head * HD, HD), HD)
        piece = hd[:, :, lanes].reshape(256, HD).astype(F32)
        gain = jnp.zeros((1, HD), F32)
        for h in range(8):
            gain = gain + jnp.where(head == h, gi[:, h * HD : (h + 1) * HD], 0.0)
        pieces.append((piece * rcol[...] * gain).astype(BF16))
    oute[...] = mm(gt[...], jnp.concatenate(pieces, axis=1), 0, 0).astype(BF16)
    partners_in(1)
    project_step(1)
    advance(2)
    relay(3)
    both = slice(0, 256)
    to_matched(5, lambda b: sqo.at[b // 2], sqi)
    to_readers(0, oute, bufe, both)
    partners_in(2)
    project_step(2)
    advance(3)
    partners_in(3)
    project_step(3)
    for q in range(4):
        gain_s[q] = jnp.concatenate(
            [gu[:, q * HD : (q + 1) * HD], gu[:, (4 + q) * HD : (5 + q) * HD]], axis=1
        )
    for par in range(2):
        pr[t, par] = ps[2 * t + par]
    for par in range(2):
        for j in (1, 3, 2):
            sender = (t + j) % NT
            send(
                ps.at[2 * t + par], pr.at[sender, par], ps_s.at[2 * t + par],
                ps_r.at[sender, par], me, sender,
            ).wait_recv()
    total = jnp.concatenate(
        [
            pr[0, par].astype(F32) + pr[1, par].astype(F32)
            + pr[2, par].astype(F32) + pr[3, par].astype(F32)
            for par in range(2)
        ],
        axis=1,
    ) * (rcol[...] * rscol[...])[:, 0:1]
    q32[...] = total
    heads, _ = norm_heads(total)
    outq[...] = mm(gt[...], jnp.concatenate(heads, axis=1).astype(BF16), 0, 0).astype(BF16)
    halves = (slice(0, HD), slice(HD, 2 * HD))
    to_readers(1, outq, bufq, halves[0])
    to_readers(4, outq, bufq, halves[1])

    off = (me % 8) * 16
    blocks = jnp.where((iota((256, 16), 0) >> 4) == iota((256, 16), 1), 1.0, 0.0).astype(BF16)
    in_lane = iota((256, HD), 1) == off + (iota((256, HD), 0) & 15)
    all_in(5, sqi)
    came = jnp.concatenate([sqi[b] for b in range(16)], axis=0)
    high, mid, low = split3(came)
    wide = mm(blocks, high, 1, 0) + mm(blocks, mid, 1, 0) + mm(blocks, low, 1, 0)
    sqm[...] = jnp.broadcast_to(lane_sum(jnp.where(in_lane, wide, 0.0)), (256, HD))
    rsm[...] = lax.rsqrt(sqm[...] * (1.0 / D) + EPS)
    sqf_s[...] = jnp.broadcast_to(
        lane_sum(mm(hott[0:512], lane_parts(sqm[...]), 1, 0)), (512, HIST)
    )
    sqc = jnp.sum(mm(lane_parts(sqm[...]), hot[:, 512:1024], 0, 0), axis=0, keepdims=True)
    for u in range(4):
        sqc_s[u] = sqc[:, u * HIST : (u + 1) * HIST]
    twice = lambda values: jnp.concatenate([values, values], axis=1)
    all_in(0, bufe)
    for q in range(4):
        low = (bufe[q].astype(F32) * twice(rsm[...]) * gain_s[q]).astype(BF16)
        nrm[q] = low
        heads, _ = norm_heads(low.astype(F32))
        knb[q] = jnp.concatenate(heads, axis=1).astype(BF16)
    for q in range(4):
        kn_s[q] = mm(hott[0:512], knb[q], 1, 0).astype(BF16)
        v_s[q] = mm(hott[0:512], nrm[q], 1, 0).astype(BF16)
    for q in range(4):
        rc_s[q] = mm(hott[...], bufe[q], 1, 0).astype(BF16)

    scale = HD ** (-0.5)
    row_id = iota((HIST, HIST), 0)
    col_id = iota((HIST, HIST), 1)

    def follow_of(rows):
        moved = pltpu.roll(rows, HIST - 1, 0)
        return jnp.where(iota(rows.shape, 0) < HIST - 1, moved, 0.0)

    def st_copy(u, j):
        peer = (t + j) % NT
        return send(st_r.at[t, u], st_r.at[t, u], xs.at[6 + u, peer], xr.at[6 + u, t], me, peer)

    def st_from(u, j):
        sender = (t + NT - j) % NT
        return send(
            st_r.at[t, u], st_r.at[sender, u], xs.at[6 + u, sender], xr.at[6 + u, sender],
            me, sender,
        )

    def user_rows(u):
        return pl.ds(pl.multiple_of(u * HIST, HIST), HIST)

    def attend(first, par):
        lanes = halves[par]
        tasks = [(first + k, q, 4 * k + q) for k in range(2) for q in range(4)]
        for u, q, slot in tasks:
            span = user_rows(u)
            p_t[slot] = mm(qn_s[q, span, lanes], kn_s[q, span, lanes], 1, 1)
        for u, q, slot in tasks:
            mask = (col_id <= row_id) & (col_id < len_ref[u])
            weights = jnp.where(mask, jnp.exp(p_t[slot] * scale), 0.0)
            w_s[2 * q + par, user_rows(u)] = (weights * (1.0 / lane_sum(weights))).astype(BF16)
        for u, q, slot in tasks:
            span = user_rows(u)
            o_s[q, span, lanes] = rc_s[q, span, lanes].astype(F32) + mm(
                w_s[2 * q + par, span], v_s[q, span, lanes], 1, 0
            )

    def first_half(i, carry):
        attend(2 * i, 0)
        return carry

    def score(u):
        span = user_rows(u)
        cspan = user_rows(u + 4)
        own = jnp.zeros((HIST, 1), F32)
        hit = jnp.zeros((HIST, 1), F32)
        neg = jnp.zeros((HIST, HIST), F32)
        for q in range(4):
            out = o_s[q, span]
            own = own + lane_sum(out * out)
            hit = hit + lane_sum(out * follow_of(rc_s[q, span].astype(F32)))
            high = out.astype(BF16)
            low = (out - high.astype(F32)).astype(BF16)
            cands = rc_s[q, cspan]
            neg = neg + mm(high, cands, 1, 1) + mm(low, cands, 1, 1)
        stats = neg + jnp.where(col_id == CAND, own, 0.0) + jnp.where(col_id == CAND + 1, hit, 0.0)
        st_r[t, u] = stats.astype(BF16)
        for j in (2, 1, 3):
            st_copy(u, j).start()

    def second_half(i, carry):
        attend(2 * i, 1)
        score(2 * i)
        score(2 * i + 1)
        return carry

    def turn_weights(par):
        def step(q, carry):
            for u in range(4):
                span = slice(u * HIST, (u + 1) * HIST)
                wt_s[2 * q + par, span] = jnp.transpose(
                    w_s[2 * q + par, span].astype(F32)
                ).astype(BF16)
            return carry

        lax.fori_loop(0, 4, step, 0)

    for par, step in ((0, first_half), (1, second_half)):
        all_in(1 if par == 0 else 4, outq.at[:, halves[0]])
        for q in range(4):
            qn_s[q, :, halves[par]] = mm(hott[0:512], bufq[q, :, halves[par]], 1, 0).astype(BF16)
        lax.fori_loop(0, 2, step, 0)
        turn_weights(par)

    def losses(u, carry):
        for j in (1, 3, 2):
            st_from(u, j).wait_recv()
        stats = (
            st_r[0, u].astype(F32) + st_r[1, u].astype(F32)
            + st_r[2, u].astype(F32) + st_r[3, u].astype(F32)
        )
        is_cand = col_id < CAND
        neg = jnp.where(is_cand, stats, 0.0)
        own = lane_sum(jnp.where(col_id == CAND, stats, 0.0))
        hit = lane_sum(jnp.where(col_id == CAND + 1, stats, 0.0))
        sq_follow = pltpu.roll(sqf_s[user_rows(u)], HIST - 1, 0)[:, 0:1]
        rn = lax.rsqrt(own + EPS)
        rf = lax.rsqrt(sq_follow + EPS)
        rc = lax.rsqrt(sqc_s[u] + EPS)
        tl = SOFT * hit * rn * rf
        nl = SOFT * neg * rn * rc
        en = jnp.where(is_cand, jnp.exp(nl), 0.0)
        et = jnp.exp(tl)
        whole = et + lane_sum(en)
        span = len_ref[u] - 1
        over = 1.0 / (jnp.full((HIST, 1), 0, jnp.int32) + span).astype(F32)
        valid = iota((HIST, 1), 0) < span
        terms = jnp.where(valid, (jnp.log(whole) - tl) * over, 0.0)
        loss_ref[u] = jnp.broadcast_to(jnp.sum(terms, axis=0, keepdims=True), (1, HIST))
        g = jnp.where(valid, float(D) * over, 0.0)
        dtl = g * (et / whole - 1.0)
        dnl = (g / whole) * en
        dsc[u, 0] = jnp.broadcast_to(
            -rn * rn * (dtl * tl + lane_sum(dnl * nl)), (HIST, HIST)
        )
        dsc[u, 1] = jnp.broadcast_to(dtl * (SOFT * rn * rf), (HIST, HIST))
        dneg = dnl * (SOFT * rn * rc)
        dneg_s[u] = dneg.astype(BF16)
        dnegt_s[u] = jnp.transpose(dneg).astype(BF16)
        dsqf = jnp.broadcast_to(-0.5 * dtl * tl * rf * rf, (HIST, HIST))
        gfol[user_rows(u)] = pltpu.roll(dsqf, 1, 0)
        grow[u] = -0.5 * rc * rc * jnp.sum(dnl * nl, axis=0, keepdims=True)
        return carry

    lax.fori_loop(0, 4, losses, 0)

    def backward_step(par, i):
        lanes = halves[par]
        tasks = [
            ((y + 1 + 2 * i + k) % 4, k, slice(u * HIST, (u + 1) * HIST), u, 4 * k + u)
            for k in range(2)
            for u in range(4)
        ]
        for q, k, span, u, slot in tasks:
            cspan = slice((4 + u) * HIST, (5 + u) * HIST)
            dhit = dsc[u, 1]
            out = o_s[q, span, lanes]
            rows = rc_s[q, span, lanes].astype(F32)
            dout = (
                dsc[u, 0] * out
                + dhit * follow_of(rows)
                + mm(dneg_s[u], rc_s[q, cspan, lanes], 1, 0)
            )
            dout_t[k, span] = dout.astype(BF16)
            drc_s[q, span, lanes] = (dout + pltpu.roll(dhit * out, 1, 0)).astype(BF16)
            drc_s[q, cspan, lanes] = mm(dnegt_s[u], out.astype(BF16), 1, 0).astype(BF16)
        for q, k, span, u, slot in tasks:
            p_t[slot] = mm(dout_t[k, span], v_s[q, span, lanes], 1, 1)
        for q, k, span, u, slot in tasks:
            dw = p_t[slot]
            wide = w_s[2 * q + par, span].astype(F32)
            ds_t[slot] = (wide * (dw - lane_sum(dw * wide)) * scale).astype(BF16)
        for q, k, span, u, slot in tasks:
            dq_t[k, span] = mm(ds_t[slot], kn_s[q, span, lanes], 1, 0).astype(BF16)
            dk_s[q, span, lanes] = mm(ds_t[slot], qn_s[q, span, lanes], 0, 0).astype(BF16)
            dv_s[q, span, lanes] = mm(wt_s[2 * q + par, span], dout_t[k, span], 1, 0).astype(BF16)
        for k in range(2):
            q = tasks[4 * k][0]
            dqo[q, :, lanes] = mm(hot[:, 0:512], dq_t[k], 1, 0).astype(BF16)
        for k in range(2):
            to_group((2, 7)[par], dqo, rq, tasks[4 * k][0], i + k == 2, lanes)

    def backward_first(i, carry):
        backward_step(0, i)
        return carry

    def backward_second(i, carry):
        backward_step(1, i)
        return carry

    lax.fori_loop(0, 2, backward_first, 0)
    lax.fori_loop(0, 2, backward_second, 0)

    nbs[...] = jnp.zeros(nbs.shape, F32)

    def return_quarter(i, carry):
        q = (y + 1 + i) % 4
        dk = mm(hot[:, 0:512], dk_s[q], 1, 0)
        dn = mm(hot[:, 0:512], dv_s[q], 1, 0) + norm_heads_back(nrm[q].astype(F32), dk)
        dn = dn * gain_s[q]
        nbs[...] += jnp.broadcast_to(lane_sum(dn * bufe[q].astype(F32)), (256, HD))
        eo[q] = (mm(hot[...], drc_s[q], 1, 0) + dn * twice(rsm[...])).astype(BF16)
        return carry

    lax.fori_loop(0, 4, return_quarter, 0)
    gsq = lane_sum(mm(hot[:, 0:512], lane_parts(gfol[...]), 1, 0)) + lane_sum(
        mm(
            hot[:, 512:1024],
            row_parts(jnp.concatenate([grow[u] for u in range(4)], axis=1)), 1, 1,
        )
    )
    placed = []
    for values in (jnp.broadcast_to(gsq, (256, HD)), nbs[...]):
        high, mid, low = split3(jnp.where(in_lane, values, 0.0))
        placed.append(mm(blocks, high, 0, 0) + mm(blocks, mid, 0, 0) + mm(blocks, low, 0, 0))
    for b in range(16):
        sco[b] = jnp.concatenate([part[b : b + 1] for part in placed], axis=1)
    to_matched(6, lambda b: sco.at[b], sci)

    def return_group(i, carry):
        to_group(3, eo, re, (y + 1 + i) % 4, i == 3, both)
        return carry


    chunks = (((y + 2) % NY, (y + 1) % NY), ((y + 3) % NY, y))

    def dq_first(peer, sender):
        return send(
            dqg.at[t, 0], dqg.at[sender, 0], xs.at[2, peer], xr.at[2, sender], me, peer
        )

    def dq_second(part, k, peer, sender):
        b = chunks[part][k]
        index = (1, 3, 4, 10)[2 * part + k]
        return send(
            dqg.at[t, 1, b], dqg.at[sender, 1, b], xs.at[index, peer], xr.at[index, sender],
            me, peer,
        )

    def item_dq(par):
        lanes = halves[par]
        out = head_back(q32[:, lanes], mm(gt[...], rq[:, lanes], 1, 0)).astype(BF16)
        dqg[t, par] = out.reshape(4, 64, HD)
        return row_sums(out.astype(F32) * q32[:, lanes])

    lax.fori_loop(0, 4, return_group, 0)
    all_in(2, rq.at[:, halves[0]])
    dots = item_dq(0)
    for j in (2, 1, 3):
        dq_first((t + j) % NT, t).start()
    all_in(7, rq.at[:, halves[1]])
    dots = dots + item_dq(1)
    for part in range(2):
        for j in (2, 1, 3):
            for k in range(2):
                dq_second(part, k, (t + j) % NT, t).start()
    all_in(6, sci)
    pairs = [sci[2 * b] + sci[2 * b + 1] for b in range(NZ)]
    item_terms = []
    for lanes in (slice(0, HD), slice(HD, 2 * HD)):
        row = jnp.concatenate([pair[:, lanes] for pair in pairs], axis=1)
        item_terms.append(jnp.sum(mm(row_parts(row), gt[...], 1, 1), axis=0, keepdims=True))
    sdy[y, pl.ds(8, 8), :] = jnp.broadcast_to(item_terms[0], (8, 256))
    rs_all = mm(jnp.ones((8, HD), BF16), lane_parts(rscol[...]), 1, 1)[0:1]
    sdx[t] = dots + rs_all * item_terms[1]
    own_sdx = lambda peer: sdx.at[t]
    start3(x_copy, 5, own_sdx, sdx)
    for j in (1, 3, 2):
        sender = (t + j) % NT
        dq_first(sender, sender).wait_recv()
    acc = jnp.zeros((256, 1024), F32)
    for tt in range(NT):
        acc = acc + mm(dqg[tt, 0].reshape(256, HD), wt[2 * tt].reshape(HD, 1024), 1, 0)
    acc_s[...] = acc.reshape(4, 64, 1024)
    gws_of = lambda peer: gws.at[peer]
    for part in range(2):
        for j in (1, 3, 2):
            sender = (t + j) % NT
            for k in range(2):
                dq_second(part, k, sender, sender).wait_recv()
        acc = jnp.concatenate([acc_s[b] for b in chunks[part]], axis=0)
        for tt in range(NT):
            acc = acc + mm(
                jnp.concatenate([dqg[tt, 1, b] for b in chunks[part]], axis=0),
                wt[2 * tt + 1].reshape(HD, 1024), 1, 0,
            )
        acc = acc.astype(BF16)
        for k, b in enumerate(chunks[part]):
            gws[b] = acc[k * 64 : (k + 1) * 64]
        if part == 0:
            wait_in(x_from, 5, own_sdx, sdx)
            sdy[y, pl.ds(0, 8), :] = sdx[0] + sdx[1] + sdx[2] + sdx[3]
            own_sdy = lambda peer: sdy.at[y]
            start3(y_copy, 4, own_sdy, sdy)
        for j in ((2, 1), (3,))[part]:
            y_copy(2, gws_of, gwr, j).start()
    gwr[y] = gws[y]
    all_in(3, re)
    es[...] = mm(gt[...], re[...], 1, 0).astype(BF16).reshape(4, 64, 256)
    es_of = lambda peer: es.at[peer]
    start3(y_copy, 3, es_of, er)
    er[y] = es[y]

    mine = pl.ds(pl.multiple_of(y * 64, 64), 64)
    emb = (hidden_ref[...].astype(F32) * rcol[mine, 0:1] * gi).astype(BF16).astype(F32)
    rs_own = rscol[mine, 0:1]
    wait_in(y_from, 4, own_sdy, sdy)
    last = sdy[0] + sdy[1] + sdy[2] + sdy[3]
    sqm[...] = columns(2.0 * last[8:9] - (1.0 / D) * rs_all * rs_all * last[0:1])
    coef = sqm[mine, 0:1]
    direct = emb * coef
    wait_in(y_from, 2, gws_of, gwr)
    gw = (
        gwr[0].astype(F32) + gwr[1].astype(F32) + gwr[2].astype(F32) + gwr[3].astype(F32)
    ) * gu * rs_own + direct
    wait_in(y_from, 3, es_of, er)
    for h in range(8):
        lanes = slice(h * HD, (h + 1) * HD)
        par, q = h // 4, h % 4
        grad_ref[:, lanes] = er[q, :, halves[par]].astype(F32) + gw[:, lanes]

    for k, src, dst in (
        (0, own_hd, hd), (1, own_sel, selb), (2, gws_of, gwr), (3, es_of, er), (4, own_sdy, sdy),
        (5, own_sqy, sqy),
    ):
        wait_out(y_copy, k, src, dst)
    for k, src, dst in (
        (0, own_sqx, sqx), (5, own_sdx, sdx)
    ):
        wait_out(x_copy, k, src, dst)
    for j in (1, 3, 2):
        peer = (t + j) % NT
        dq_first(peer, t).wait_send()
        for part in range(2):
            for k in range(2):
                dq_second(part, k, peer, t).wait_send()
    for j in (1, 3, 2):
        for par in range(2):
            ps_copy((t + j) % NT * 2 + par).wait_send()
    for u in range(4):
        for j in (1, 3, 2):
            st_copy(u, j).wait_send()
    for stream in range(4):
        for step in range(RING[stream]):
            ring(stream, step).wait_send()
    for b in range(NZ):
        for half in range(2):
            partner(b, c, half).wait_send()
    most = pl.ds(0, (NS - 1) * 16)
    all_out(0, oute.at[most])
    all_out(1, outq.at[most, halves[0]])
    all_out(4, outq.at[most, halves[1]])
    all_out(2, rq.at[most, halves[0]])
    all_out(7, rq.at[most, halves[1]])
    all_out(3, re.at[most])
    all_out(5, sqi.at[pl.ds(0, 15)])
    all_out(6, sci.at[pl.ds(0, 15)])


def local(item_hidden, item_gain, send_item, pos_slot, hist_len, user_gain, query_weight):
    vmem = pltpu.VMEM
    dma = pltpu.SemaphoreType.DMA
    quarter = lambda kind: vmem((4, 256, 256), kind)
    grad, loss = pl.pallas_call(
        kernel,
        out_shape=(
            jax.ShapeDtypeStruct((64, 1024), F32),
            jax.ShapeDtypeStruct((4, 1, HIST), F32),
        ),
        in_specs=[pl.BlockSpec(memory_space=pltpu.HBM)] * 7,
        out_specs=(
            pl.BlockSpec(memory_space=pltpu.VMEM),
            pl.BlockSpec(memory_space=pltpu.VMEM),
        ),
        scratch_shapes=[
            pltpu.SMEM((4,), jnp.int32),
            vmem((64, 1024), BF16),
            vmem((1024,), BF16),
            vmem((1024,), BF16),
            vmem((4, 64), jnp.int32),
            vmem((4, HIST + CAND), jnp.int32),
            dma((8,)),
            vmem((4, 64, 1024), BF16),
            vmem((4, 1, 1024), F32),
            vmem((8, 2, 64, 1024), BF16),
            vmem((4, 16, HIST), F32),
            vmem((4, 8, HIST), F32),
            vmem((8, 256, HD), BF16),
            vmem((4, 2, 256, HD), BF16),
            vmem((1024, 256), BF16),
            vmem((1024, 256), BF16),
            quarter(BF16),
            quarter(BF16),
            vmem((256, 1024), BF16),
            quarter(BF16),
            quarter(BF16),
            vmem((8, 1, HIST), F32),
            vmem((16, 1, HIST), F32),
            vmem((256, HIST), F32),
            vmem((256, HIST), F32),
            vmem((256, 256), F32),
            vmem((256, HIST), F32),
            vmem((256, HIST), F32),
            vmem((4, 2 * HIST), jnp.int32),
            vmem((256, 1024), BF16),
            vmem((1024, 256), BF16),
            vmem((512, HIST), F32),
            vmem((4, 1, HIST), F32),
            vmem((4, 1, 256), F32),
            vmem((4, 1024, 256), BF16),
            vmem((4, 512, 256), BF16),
            vmem((4, 512, 256), BF16),
            vmem((4, 512, 256), BF16),
            vmem((8, 512, HIST), BF16),
            vmem((8, 512, HIST), BF16),
            vmem((8, HIST, HIST), F32),
            vmem((8, HIST, HIST), BF16),
            vmem((4, 512, 256), F32),
            vmem((4, 4, HIST, HIST), BF16),
            vmem((4, 2, HIST, HIST), F32),
            vmem((4, HIST, HIST), BF16),
            vmem((4, HIST, HIST), BF16),
            vmem((512, HIST), F32),
            vmem((4, 1, HIST), F32),
            vmem((2, 512, HD), BF16),
            vmem((2, 512, HD), BF16),
            vmem((4, 512, 256), BF16),
            vmem((4, 512, 256), BF16),
            vmem((4, 1024, 256), BF16),
            vmem((256, HIST), F32),
            quarter(BF16),
            quarter(BF16),
            vmem((1024, 256), BF16),
            vmem((1024, 256), BF16),
            vmem((16, 1, 256), F32),
            vmem((16, 1, 256), F32),
            vmem((4, 2, 4, 64, HD), BF16),
            vmem((4, 64, 1024), F32),
            vmem((4, 64, 1024), BF16),
            vmem((4, 64, 1024), BF16),
            vmem((4, 64, 256), BF16),
            vmem((4, 64, 256), BF16),
            vmem((4, 8, 256), F32),
            vmem((4, 16, 256), F32),
            dma((11, 4)),
            dma((11, 4)),
            dma((6, 4)),
            dma((6, 4)),
            dma((4, 4)),
            dma((4, 4)),
            dma((8, 2)),
            dma((8, 2)),
            dma((8,)),
            dma((8,)),
            dma((8,)),
            dma((4, 2)),
            pltpu.SemaphoreType.REGULAR((2, 4)),
        ],
        compiler_params=pltpu.CompilerParams(
            collective_id=0, has_side_effects=True, vmem_limit_bytes=40 * 1024 * 1024
        ),
    )(
        *[
            pltpu.with_memory_space_constraint(value, pltpu.HBM)
            for value in (
                hist_len, item_hidden, query_weight.T, item_gain, user_gain, send_item[0].T,
                pos_slot,
            )
        ]
    )
    return (grad, loss[:, 0, 0])


def solution(mesh):
    placed = (
        P("sect", "tp"),
        P("tp"),
        P("sect", None, None),
        P("sect", None),
        P("sect"),
        P("tp"),
        P("tp", "sect"),
    )
    return jax.shard_map(
        local, mesh=mesh, in_specs=placed, out_specs=(P("sect", "tp"), P("sect")), check_vma=False
    )
```

```python
import jax
import jax.numpy as jnp
from jax import lax
from jax.experimental import pallas as pl
from jax.experimental.pallas import tpu as pltpu
from jax.sharding import PartitionSpec as P

D = 4096
HD = 128
HIST = 128
CAND = 64
NZ, NY, NT = 8, 4, 4
NS = 64
EPS = 1e-06
SOFT = 20.0
F32, BF16 = jnp.float32, jnp.bfloat16
MESH = pl.DeviceIdType.MESH
RING = (4, 3, 3, 4)


def mm(a, b, ca, cb, precision=None):
    return lax.dot_general(
        a, b, (((ca,), (cb,)), ((), ())), preferred_element_type=F32, precision=precision
    )


def split3(values):
    high = values.astype(BF16)
    rest = values - high.astype(F32)
    mid = rest.astype(BF16)
    return high, mid, (rest - mid.astype(F32)).astype(BF16)


def row_parts(row):
    parts = split3(jnp.broadcast_to(row, (8, row.shape[1])))
    index = iota((8, row.shape[1]), 0)
    out = jnp.where(index == 0, parts[0].astype(F32), 0.0)
    out = jnp.where(index == 1, parts[1].astype(F32), out)
    return jnp.where(index == 2, parts[2].astype(F32), out).astype(BF16)


def lane_parts(values):
    parts = split3(values)
    index = iota(values.shape, 1)
    out = jnp.where(index == 0, parts[0].astype(F32), 0.0)
    out = jnp.where(index == 1, parts[1].astype(F32), out)
    return jnp.where(index == 2, parts[2].astype(F32), out).astype(BF16)


def columns(row):
    return mm(row_parts(row), jnp.ones((8, 128), BF16), 0, 0)


def row_sums(values):
    ones = jnp.ones((8, values.shape[1]), BF16)
    high, mid, low = split3(values)
    return mm(ones, high, 1, 1) + mm(ones, mid, 1, 1) + mm(ones, low, 1, 1)


def lane_sum(values):
    return jnp.sum(values, axis=1, keepdims=True)


def iota(shape, dim):
    return lax.broadcasted_iota(jnp.int32, shape, dim)


def one_hot(row, count):
    return jnp.where(iota((count, row.shape[1]), 0) == row, 1.0, 0.0)


def norm_heads(values):
    heads, roots = [], []
    for par in range(2):
        part = values[:, par * HD : (par + 1) * HD]
        root = lax.rsqrt(lane_sum(part * part) * (1.0 / HD) + EPS)
        heads.append(part * root)
        roots.append(root)
    return heads, roots


def head_back(values, grad):
    root = lax.rsqrt(lane_sum(values * values) * (1.0 / HD) + EPS)
    head = values * root
    return root * (grad - head * (lane_sum(grad * head) * (1.0 / HD)))


def norm_heads_back(values, grads):
    heads, roots = norm_heads(values)
    out = []
    for par in range(2):
        grad = grads[:, par * HD : (par + 1) * HD]
        out.append(
            roots[par] * (grad - heads[par] * (lane_sum(grad * heads[par]) * (1.0 / HD)))
        )
    return jnp.concatenate(out, axis=1)


def kernel(
    len_in, hidden_in, w_in, gi_in, gu_in, send_in, pos_in,
    grad_ref, loss_ref,
    len_ref, hidden_ref, gi_ref, gu_ref, send_ref, pos_ref, in_sem,
    hd, selb, wt, sqx, sqy, ps, pr, oute, outq, bufe, bufq, gt, nrm, knb, sqo, sqi, sqm, rsm, q32,
    rcol, rscol, pos_s, hot, hott, sqf_s, sqc_s, gain_s,
    rc_s, kn_s, v_s, qn_s, w_s, wt_s, p_t, ds_t, o_s, st_r, dsc, dneg_s, dnegt_s, gfol, grow,
    dout_t, dq_t, dk_s, dv_s, drc_s, nbs, dqo, eo, rq, re, sco, sci,
    dqg, acc_s, gws, gwr, es, er, sdx, sdy,
    xs, xr, ys, yr, ring_s, ring_r, par_s, par_r, a2a_s, a2a_r, ps_s, ps_r, hello,
):
    me = lax.axis_index("sect")
    t = lax.axis_index("tp")
    z, y, c = me // 8, (me // 2) % 4, me % 2
    blk = z * 2 + c

    def send(src, dst, ssem, rsem, sect, tp):
        return pltpu.make_async_remote_copy(
            src_ref=src, dst_ref=dst, send_sem=ssem, recv_sem=rsem,
            device_id=(sect, tp), device_id_type=MESH,
        )

    def sect_of(zz, yy, cc):
        return zz * 8 + yy * 2 + cc

    def x_copy(k, src, dst, j):
        peer = (t + j) % NT
        return send(src(peer), dst.at[t], xs.at[k, peer], xr.at[k, t], me, peer)

    def x_from(k, src, dst, j):
        sender = (t + NT - j) % NT
        return send(src(t), dst.at[sender], xs.at[k, sender], xr.at[k, sender], me, sender)

    def y_copy(k, src, dst, j):
        peer = (y + j) % NY
        return send(src(peer), dst.at[y], ys.at[k, peer], yr.at[k, y], sect_of(z, peer, c), t)

    def y_from(k, src, dst, j):
        sender = (y + NY - j) % NY
        return send(
            src(y), dst.at[sender], ys.at[k, sender], yr.at[k, sender], sect_of(z, sender, c), t
        )

    def start3(copy, k, src, dst):
        for j in (2, 1, 3):
            copy(k, src, dst, j).start()

    def wait_in(came, k, src, dst):
        for j in (1, 3, 2):
            came(k, src, dst, j).wait_recv()

    def wait_out(copy, k, src, dst):
        for j in (1, 3, 2):
            copy(k, src, dst, j).wait_send()

    def rows_of(first):
        return pl.ds(pl.multiple_of(first * 16, 16), 16)

    def to_readers(k, out, buf, lanes):
        pltpu.make_async_copy(
            out.at[rows_of(me), lanes], buf.at[y, rows_of(blk), lanes], a2a_r.at[k]
        ).start()

        def step(j, carry):
            peer = (me + j) % NS
            send(
                out.at[rows_of(peer), lanes], buf.at[y, rows_of(blk), lanes],
                a2a_s.at[k], a2a_r.at[k], peer, t,
            ).start()
            return carry

        lax.fori_loop(1, NS, step, 0, unroll=7)

    def to_group(k, out, buf, group, same, lanes):
        def copy(j):
            b = (blk + j) % 16
            return send(
                out.at[group, rows_of(b), lanes], buf.at[rows_of(me), lanes],
                a2a_s.at[k], a2a_r.at[k], sect_of(b // 2, group, b % 2), t,
            )

        @pl.when(same)
        def _():
            pltpu.make_async_copy(
                out.at[group, rows_of(blk), lanes], buf.at[rows_of(me), lanes], a2a_r.at[k]
            ).start()

        @pl.when(jnp.logical_not(same))
        def _():
            copy(0).start()

        def step(j, carry):
            copy(j).start()
            return carry

        lax.fori_loop(1, 16, step, 0, unroll=5)

    def to_matched(k, src_of, dst):
        pltpu.make_async_copy(src_of(blk), dst.at[blk], a2a_r.at[k]).start()

        def step(j, carry):
            b = (blk + j) % 16
            send(
                src_of(b), dst.at[blk], a2a_s.at[k], a2a_r.at[k], sect_of(b // 2, y, b % 2), t
            ).start()
            return carry

        lax.fori_loop(1, 16, step, 0, unroll=5)

    def all_in(k, view):
        pltpu.make_async_copy(view, view, a2a_r.at[k]).wait()

    def all_out(k, view):
        pltpu.make_async_copy(view, view, a2a_s.at[k]).wait()

    def ring(stream, step):
        way = 1 if stream < 2 else NZ - 1
        block = (z + (NZ - way) * step) % NZ
        part = wt.at[block, c, pl.ds((stream % 2) * 32, 32)]
        return send(
            part, part, ring_s.at[stream, step], ring_r.at[stream, step],
            sect_of((z + way) % NZ, y, c), t,
        )

    def ring_from(stream, step):
        way = 1 if stream < 2 else NZ - 1
        block = (z + (NZ - way) * (step + 1)) % NZ
        part = wt.at[block, c, pl.ds((stream % 2) * 32, 32)]
        return block, send(
            part, part, ring_s.at[stream, step], ring_r.at[stream, step],
            sect_of((z + way) % NZ, y, c), t,
        )

    def partner(block, core, half):
        part = wt.at[block, core, pl.ds(half * 32, 32)]
        return send(
            part, part, par_s.at[block, half], par_r.at[block, half], sect_of(z, y, 1 - c), t
        )

    def partner_in(block, half):
        partner(block, 1 - c, half).wait_recv()

    def advance(step):
        for stream in (0, 2, 1, 3):
            if step >= RING[stream]:
                continue
            block, came = ring_from(stream, step)
            came.wait_recv()
            if step + 1 < RING[stream]:
                ring(stream, step + 1).start()
            partner(block, c, stream % 2).start()

    barrier = pltpu.get_barrier_semaphore()
    for j in range(1, 8):
        pl.semaphore_signal(
            barrier, inc=1, device_id=(z * 8 + (me + j) % 8, t), device_id_type=MESH
        )
    for j in (1, NZ - 1):
        pl.semaphore_signal(
            barrier, inc=1, device_id=(sect_of((z + j) % NZ, y, c), t), device_id_type=MESH
        )
    for j in range(1, NT):
        pl.semaphore_signal(barrier, inc=1, device_id=(me, (t + j) % NT), device_id_type=MESH)

    loads = [
        pltpu.make_async_copy(src, dst, in_sem.at[k])
        for k, (src, dst) in enumerate(
            (
                (send_in, send_ref), (w_in, wt.at[z, c]), (hidden_in, hd.at[y]),
                (gi_in, gi_ref), (gu_in, gu_ref), (hidden_in, hidden_ref), (pos_in, pos_ref),
                (len_in, len_ref),
            )
        )
    ]
    for load in loads:
        load.start()
    for load in loads:
        load.wait()
    sqx[t] = jnp.zeros((16, HIST), F32)
    spread = jnp.where((iota((64, 1024), 1) >> 4) == iota((64, 1024), 0), 1.0, 0.0).astype(BF16)
    named = mm(send_ref[...].astype(F32).astype(BF16), spread, 1, 0)
    lane = iota((1, 1024), 1)
    pick = jnp.full((1, 1024), -1.0, F32)
    for s in range(4):
        pick = jnp.where((lane & 3) == s, named[s : s + 1], pick)
    base = (jnp.zeros((1, 1024), jnp.int32) + y * 64).astype(F32)
    selb[y] = jnp.where((((lane >> 2) & 3) == y) & (pick >= 0.0), pick + base, -1.0)
    pl.semaphore_wait(barrier, 7 + 2 + NT - 1)

    def greet(step):
        for way in range(2):
            if step < 4 - way:
                peer = (z + 1) % NZ if way == 0 else (z + NZ - 1) % NZ
                pl.semaphore_signal(
                    hello.at[way, step], inc=1, device_id=(sect_of(peer, y, c), t),
                    device_id_type=MESH,
                )

    def relay(step):
        for way in range(2):
            if step < 4 - way:
                pl.semaphore_wait(hello.at[way, step], 1)
        greet(step + 1)

    greet(0)
    own_hd = lambda peer: hd.at[y]
    own_sel = lambda peer: selb.at[y]
    for stream in (0, 2, 1, 3):
        ring(stream, 0).start()
    start3(y_copy, 0, own_hd, hd)
    start3(y_copy, 1, own_sel, selb)
    for half in range(2):
        partner(z, c, half).start()

    gi = gi_ref[...].astype(F32).reshape(1, 1024)
    gu = gu_ref[...].astype(F32).reshape(1, 1024)
    hidden = hidden_ref[...].astype(F32)
    gained = hidden * gi
    sqx[t, pl.ds(0, 8), 0:64] = row_sums(hidden * hidden)
    sqx[t, pl.ds(8, 8), 0:64] = row_sums(gained * gained)
    own_sqx = lambda peer: sqx.at[t]
    start3(x_copy, 0, own_sqx, sqx)

    slots = pos_ref[...]
    owner = slots >> 2
    pos_s[...] = jnp.full(pos_s.shape, -1, jnp.int32)
    pos_s[:, 0 : HIST + CAND] = (
        ((owner >> 3) << 5) | ((owner & 1) << 4) | (((owner >> 1) & 3) << 2) | (slots & 3)
    )
    for u in range(4):
        for kind in range(2):
            row = pos_s[u : u + 1, kind * HIST : (kind + 1) * HIST]
            picked = one_hot(row, 256)
            first = (4 * kind + u) * HIST
            hot[:, first : first + HIST] = picked.astype(BF16)
            hott[first : first + HIST, :] = jnp.transpose(picked).astype(BF16)

    advance(0)
    relay(0)
    wait_in(x_from, 0, own_sqx, sqx)
    sums = sqx[0] + sqx[1] + sqx[2] + sqx[3]
    r_row = lax.rsqrt(sums[0:1] * (1.0 / D) + EPS)
    sq_item = r_row * r_row * sums[8:9]
    rs_row = lax.rsqrt(sq_item * (1.0 / D) + EPS)
    sqy[y] = jnp.concatenate([r_row, rs_row, sq_item] + [r_row] * 5, axis=0)
    own_sqy = lambda peer: sqy.at[y]
    start3(y_copy, 5, own_sqy, sqy)
    relay(1)
    advance(1)
    relay(2)
    wait_in(y_from, 0, own_hd, hd)
    lhs = (hd[...].reshape(256, 1024).astype(F32) * (gi * gu)).astype(BF16)

    def ps_copy(block):
        part, par = block // 2, block % 2
        return send(
            ps.at[block], pr.at[t, par], ps_s.at[block], ps_r.at[t, par], me, part
        )

    def project(block):
        ps[block] = mm(lhs, wt[block].reshape(HD, 1024), 1, 1).astype(BF16)

        @pl.when(block // 2 != t)
        def _():
            ps_copy(block).start()

    def project_step(step):
        if step == 0:
            project(z)
        for way in (1, NZ - 1)[: 2 if step < 3 else 1]:
            project((z + way * (step + 1)) % NZ)

    def partners_in(step):
        if step == 0:
            for half in range(2):
                partner_in(z, half)
        for stream in range(4):
            if step < RING[stream]:
                way = 1 if stream < 2 else NZ - 1
                partner_in((z + (NZ - way) * (step + 1)) % NZ, stream % 2)

    partners_in(0)
    project_step(0)
    wait_in(y_from, 1, own_sel, selb)
    picks = jnp.maximum(jnp.maximum(selb[0], selb[1]), jnp.maximum(selb[2], selb[3]))
    gt[...] = one_hot(picks.astype(jnp.int32), 256).astype(BF16)
    wait_in(y_from, 5, own_sqy, sqy)
    rcol[...] = jnp.concatenate([columns(sqy[b, 0:1])[0:64] for b in range(4)], axis=0)
    rscol[...] = jnp.concatenate([columns(sqy[b, 1:2])[0:64] for b in range(4)], axis=0)
    sq_out = jnp.zeros((8, 1024), F32)
    for b in range(4):
        sq_out = sq_out + mm(
            row_parts(sqy[b, 2:3])[:, 0:64], gt[b * 64 : (b + 1) * 64, :], 1, 0
        )
    sq_out = jnp.sum(sq_out, axis=0, keepdims=True)
    for b in range(NZ):
        sqo[b] = sq_out[:, b * HD : (b + 1) * HD]
    pieces = []
    for par in range(2):
        head = par * 4 + y
        lanes = pl.ds(pl.multiple_of(head * HD, HD), HD)
        piece = hd[:, :, lanes].reshape(256, HD).astype(F32)
        gain = jnp.zeros((1, HD), F32)
        for h in range(8):
            gain = gain + jnp.where(head == h, gi[:, h * HD : (h + 1) * HD], 0.0)
        pieces.append((piece * rcol[...] * gain).astype(BF16))
    oute[...] = mm(gt[...], jnp.concatenate(pieces, axis=1), 0, 0).astype(BF16)
    partners_in(1)
    project_step(1)
    advance(2)
    relay(3)
    both = slice(0, 256)
    to_matched(5, lambda b: sqo.at[b // 2], sqi)
    to_readers(0, oute, bufe, both)
    partners_in(2)
    project_step(2)
    advance(3)
    partners_in(3)
    project_step(3)
    for q in range(4):
        gain_s[q] = jnp.concatenate(
            [gu[:, q * HD : (q + 1) * HD], gu[:, (4 + q) * HD : (5 + q) * HD]], axis=1
        )
    for par in range(2):
        pr[t, par] = ps[2 * t + par]
    for par in range(2):
        for j in (1, 3, 2):
            sender = (t + j) % NT
            send(
                ps.at[2 * t + par], pr.at[sender, par], ps_s.at[2 * t + par],
                ps_r.at[sender, par], me, sender,
            ).wait_recv()
    total = jnp.concatenate(
        [
            pr[0, par].astype(F32) + pr[1, par].astype(F32)
            + pr[2, par].astype(F32) + pr[3, par].astype(F32)
            for par in range(2)
        ],
        axis=1,
    ) * (rcol[...] * rscol[...])[:, 0:1]
    q32[...] = total
    heads, _ = norm_heads(total)
    outq[...] = mm(gt[...], jnp.concatenate(heads, axis=1).astype(BF16), 0, 0).astype(BF16)
    halves = (slice(0, HD), slice(HD, 2 * HD))
    to_readers(1, outq, bufq, halves[0])
    to_readers(4, outq, bufq, halves[1])

    off = (me % 8) * 16
    blocks = jnp.where((iota((256, 16), 0) >> 4) == iota((256, 16), 1), 1.0, 0.0).astype(BF16)
    in_lane = iota((256, HD), 1) == off + (iota((256, HD), 0) & 15)
    all_in(5, sqi)
    came = jnp.concatenate([sqi[b] for b in range(16)], axis=0)
    high, mid, low = split3(came)
    wide = mm(blocks, high, 1, 0) + mm(blocks, mid, 1, 0) + mm(blocks, low, 1, 0)
    sqm[...] = jnp.broadcast_to(lane_sum(jnp.where(in_lane, wide, 0.0)), (256, HD))
    rsm[...] = lax.rsqrt(sqm[...] * (1.0 / D) + EPS)
    sqf_s[...] = jnp.broadcast_to(
        lane_sum(mm(hott[0:512], lane_parts(sqm[...]), 1, 0)), (512, HIST)
    )
    sqc = jnp.sum(mm(lane_parts(sqm[...]), hot[:, 512:1024], 0, 0), axis=0, keepdims=True)
    for u in range(4):
        sqc_s[u] = sqc[:, u * HIST : (u + 1) * HIST]
    twice = lambda values: jnp.concatenate([values, values], axis=1)
    all_in(0, bufe)
    for q in range(4):
        low = (bufe[q].astype(F32) * twice(rsm[...]) * gain_s[q]).astype(BF16)
        nrm[q] = low
        heads, _ = norm_heads(low.astype(F32))
        knb[q] = jnp.concatenate(heads, axis=1).astype(BF16)
    for q in range(4):
        kn_s[q] = mm(hott[0:512], knb[q], 1, 0).astype(BF16)
        v_s[q] = mm(hott[0:512], nrm[q], 1, 0).astype(BF16)
    for q in range(4):
        rc_s[q] = mm(hott[...], bufe[q], 1, 0).astype(BF16)

    scale = HD ** (-0.5)
    row_id = iota((HIST, HIST), 0)
    col_id = iota((HIST, HIST), 1)

    def follow_of(rows):
        moved = pltpu.roll(rows, HIST - 1, 0)
        return jnp.where(iota(rows.shape, 0) < HIST - 1, moved, 0.0)

    def st_copy(u, j):
        peer = (t + j) % NT
        return send(st_r.at[t, u], st_r.at[t, u], xs.at[6 + u, peer], xr.at[6 + u, t], me, peer)

    def st_from(u, j):
        sender = (t + NT - j) % NT
        return send(
            st_r.at[t, u], st_r.at[sender, u], xs.at[6 + u, sender], xr.at[6 + u, sender],
            me, sender,
        )

    def user_rows(u):
        return pl.ds(pl.multiple_of(u * HIST, HIST), HIST)

    def attend(first, par):
        lanes = halves[par]
        tasks = [(first + k, q, 4 * k + q) for k in range(2) for q in range(4)]
        for u, q, slot in tasks:
            span = user_rows(u)
            p_t[slot] = mm(qn_s[q, span, lanes], kn_s[q, span, lanes], 1, 1)
        for u, q, slot in tasks:
            mask = (col_id <= row_id) & (col_id < len_ref[u])
            weights = jnp.where(mask, jnp.exp(p_t[slot] * scale), 0.0)
            w_s[2 * q + par, user_rows(u)] = (weights * (1.0 / lane_sum(weights))).astype(BF16)
        for u, q, slot in tasks:
            span = user_rows(u)
            o_s[q, span, lanes] = rc_s[q, span, lanes].astype(F32) + mm(
                w_s[2 * q + par, span], v_s[q, span, lanes], 1, 0
            )

    def first_half(i, carry):
        attend(2 * i, 0)
        return carry

    def score(u):
        span = user_rows(u)
        cspan = user_rows(u + 4)
        own = jnp.zeros((HIST, 1), F32)
        hit = jnp.zeros((HIST, 1), F32)
        neg = jnp.zeros((HIST, HIST), F32)
        for q in range(4):
            out = o_s[q, span]
            own = own + lane_sum(out * out)
            hit = hit + lane_sum(out * follow_of(rc_s[q, span].astype(F32)))
            high = out.astype(BF16)
            low = (out - high.astype(F32)).astype(BF16)
            cands = rc_s[q, cspan]
            neg = neg + mm(high, cands, 1, 1) + mm(low, cands, 1, 1)
        stats = neg + jnp.where(col_id == CAND, own, 0.0) + jnp.where(col_id == CAND + 1, hit, 0.0)
        st_r[t, u] = stats.astype(BF16)
        for j in (2, 1, 3):
            st_copy(u, j).start()

    def second_half(i, carry):
        attend(2 * i, 1)
        score(2 * i)
        score(2 * i + 1)
        return carry

    def turn_weights(par):
        def step(q, carry):
            for u in range(4):
                span = slice(u * HIST, (u + 1) * HIST)
                wt_s[2 * q + par, span] = jnp.transpose(
                    w_s[2 * q + par, span].astype(F32)
                ).astype(BF16)
            return carry

        lax.fori_loop(0, 4, step, 0)

    for par, step in ((0, first_half), (1, second_half)):
        all_in(1 if par == 0 else 4, outq.at[:, halves[0]])
        for q in range(4):
            qn_s[q, :, halves[par]] = mm(hott[0:512], bufq[q, :, halves[par]], 1, 0).astype(BF16)
        lax.fori_loop(0, 2, step, 0)
        turn_weights(par)

    def losses(u):
        stats = (
            st_r[0, u].astype(F32) + st_r[1, u].astype(F32)
            + st_r[2, u].astype(F32) + st_r[3, u].astype(F32)
        )
        is_cand = col_id < CAND
        neg = jnp.where(is_cand, stats, 0.0)
        own = lane_sum(jnp.where(col_id == CAND, stats, 0.0))
        hit = lane_sum(jnp.where(col_id == CAND + 1, stats, 0.0))
        sq_follow = pltpu.roll(sqf_s[user_rows(u)], HIST - 1, 0)[:, 0:1]
        rn = lax.rsqrt(own + EPS)
        rf = lax.rsqrt(sq_follow + EPS)
        rc = lax.rsqrt(sqc_s[u] + EPS)
        tl = SOFT * hit * rn * rf
        nl = SOFT * neg * rn * rc
        en = jnp.where(is_cand, jnp.exp(nl), 0.0)
        et = jnp.exp(tl)
        whole = et + lane_sum(en)
        span = len_ref[u] - 1
        over = 1.0 / (jnp.full((HIST, 1), 0, jnp.int32) + span).astype(F32)
        valid = iota((HIST, 1), 0) < span
        terms = jnp.where(valid, (jnp.log(whole) - tl) * over, 0.0)
        loss_ref[u] = jnp.broadcast_to(jnp.sum(terms, axis=0, keepdims=True), (1, HIST))
        g = jnp.where(valid, float(D) * over, 0.0)
        dtl = g * (et / whole - 1.0)
        dnl = (g / whole) * en
        dsc[u, 0] = jnp.broadcast_to(
            -rn * rn * (dtl * tl + lane_sum(dnl * nl)), (HIST, HIST)
        )
        dsc[u, 1] = jnp.broadcast_to(dtl * (SOFT * rn * rf), (HIST, HIST))
        dneg = dnl * (SOFT * rn * rc)
        dneg_s[u] = dneg.astype(BF16)
        dnegt_s[u] = jnp.transpose(dneg).astype(BF16)
        dsqf = jnp.broadcast_to(-0.5 * dtl * tl * rf * rf, (HIST, HIST))
        gfol[user_rows(u)] = pltpu.roll(dsqf, 1, 0)
        grow[u] = -0.5 * rc * rc * jnp.sum(dnl * nl, axis=0, keepdims=True)

    def losses_pair(i, carry):
        for k in range(2):
            for j in (1, 3, 2):
                st_from(2 * i + k, j).wait_recv()
        for k in range(2):
            losses(2 * i + k)
        return carry

    lax.fori_loop(0, 2, losses_pair, 0)

    def backward_step(par, i):
        lanes = halves[par]
        tasks = [
            ((y + 1 + 2 * i + k) % 4, k, slice(u * HIST, (u + 1) * HIST), u, 4 * k + u)
            for k in range(2)
            for u in range(4)
        ]
        for q, k, span, u, slot in tasks:
            cspan = slice((4 + u) * HIST, (5 + u) * HIST)
            dhit = dsc[u, 1]
            out = o_s[q, span, lanes]
            rows = rc_s[q, span, lanes].astype(F32)
            dout = (
                dsc[u, 0] * out
                + dhit * follow_of(rows)
                + mm(dneg_s[u], rc_s[q, cspan, lanes], 1, 0)
            )
            dout_t[k, span] = dout.astype(BF16)
            drc_s[q, span, lanes] = (dout + pltpu.roll(dhit * out, 1, 0)).astype(BF16)
            drc_s[q, cspan, lanes] = mm(dnegt_s[u], out.astype(BF16), 1, 0).astype(BF16)
        for q, k, span, u, slot in tasks:
            p_t[slot] = mm(dout_t[k, span], v_s[q, span, lanes], 1, 1)
        for q, k, span, u, slot in tasks:
            dw = p_t[slot]
            wide = w_s[2 * q + par, span].astype(F32)
            ds_t[slot] = (wide * (dw - lane_sum(dw * wide)) * scale).astype(BF16)
        for q, k, span, u, slot in tasks:
            dq_t[k, span] = mm(ds_t[slot], kn_s[q, span, lanes], 1, 0).astype(BF16)
            dk_s[q, span, lanes] = mm(ds_t[slot], qn_s[q, span, lanes], 0, 0).astype(BF16)
            dv_s[q, span, lanes] = mm(wt_s[2 * q + par, span], dout_t[k, span], 1, 0).astype(BF16)
        for k in range(2):
            q = tasks[4 * k][0]
            dqo[q, :, lanes] = mm(hot[:, 0:512], dq_t[k], 1, 0).astype(BF16)
        for k in range(2):
            to_group((2, 7)[par], dqo, rq, tasks[4 * k][0], i + k == 2, lanes)

    def backward_first(i, carry):
        backward_step(0, i)
        return carry

    def backward_second(i, carry):
        backward_step(1, i)
        return carry

    lax.fori_loop(0, 2, backward_first, 0)
    lax.fori_loop(0, 2, backward_second, 0)

    nbs[...] = jnp.zeros(nbs.shape, F32)

    def return_quarter(i, carry):
        q = (y + 1 + i) % 4
        dk = mm(hot[:, 0:512], dk_s[q], 1, 0)
        dn = mm(hot[:, 0:512], dv_s[q], 1, 0) + norm_heads_back(nrm[q].astype(F32), dk)
        dn = dn * gain_s[q]
        nbs[...] += jnp.broadcast_to(lane_sum(dn * bufe[q].astype(F32)), (256, HD))
        eo[q] = (mm(hot[...], drc_s[q], 1, 0) + dn * twice(rsm[...])).astype(BF16)
        return carry

    lax.fori_loop(0, 4, return_quarter, 0)
    gsq = lane_sum(mm(hot[:, 0:512], lane_parts(gfol[...]), 1, 0)) + lane_sum(
        mm(
            hot[:, 512:1024],
            row_parts(jnp.concatenate([grow[u] for u in range(4)], axis=1)), 1, 1,
        )
    )
    placed = []
    for values in (jnp.broadcast_to(gsq, (256, HD)), nbs[...]):
        high, mid, low = split3(jnp.where(in_lane, values, 0.0))
        placed.append(mm(blocks, high, 0, 0) + mm(blocks, mid, 0, 0) + mm(blocks, low, 0, 0))
    for b in range(16):
        sco[b] = jnp.concatenate([part[b : b + 1] for part in placed], axis=1)
    to_matched(6, lambda b: sco.at[b], sci)

    def return_group(i, carry):
        to_group(3, eo, re, (y + 1 + i) % 4, i == 3, both)
        return carry


    chunks = (((y + 2) % NY, (y + 1) % NY), ((y + 3) % NY, y))

    def dq_first(peer, sender):
        return send(
            dqg.at[t, 0], dqg.at[sender, 0], xs.at[2, peer], xr.at[2, sender], me, peer
        )

    def dq_second(part, k, peer, sender):
        b = chunks[part][k]
        index = (1, 3, 4, 10)[2 * part + k]
        return send(
            dqg.at[t, 1, b], dqg.at[sender, 1, b], xs.at[index, peer], xr.at[index, sender],
            me, peer,
        )

    def item_dq(par):
        lanes = halves[par]
        out = head_back(q32[:, lanes], mm(gt[...], rq[:, lanes], 1, 0)).astype(BF16)
        dqg[t, par] = out.reshape(4, 64, HD)
        return row_sums(out.astype(F32) * q32[:, lanes])

    lax.fori_loop(0, 4, return_group, 0)
    all_in(2, rq.at[:, halves[0]])
    dots = item_dq(0)
    for j in (2, 1, 3):
        dq_first((t + j) % NT, t).start()
    all_in(7, rq.at[:, halves[1]])
    dots = dots + item_dq(1)
    for part in range(2):
        for j in (2, 1, 3):
            for k in range(2):
                dq_second(part, k, (t + j) % NT, t).start()
    all_in(6, sci)
    pairs = [sci[2 * b] + sci[2 * b + 1] for b in range(NZ)]
    item_terms = []
    for lanes in (slice(0, HD), slice(HD, 2 * HD)):
        row = jnp.concatenate([pair[:, lanes] for pair in pairs], axis=1)
        item_terms.append(jnp.sum(mm(row_parts(row), gt[...], 1, 1), axis=0, keepdims=True))
    sdy[y, pl.ds(8, 8), :] = jnp.broadcast_to(item_terms[0], (8, 256))
    rs_all = mm(jnp.ones((8, HD), BF16), lane_parts(rscol[...]), 1, 1)[0:1]
    sdx[t] = dots + rs_all * item_terms[1]
    own_sdx = lambda peer: sdx.at[t]
    start3(x_copy, 5, own_sdx, sdx)
    for j in (1, 3, 2):
        sender = (t + j) % NT
        dq_first(sender, sender).wait_recv()
    acc = jnp.zeros((256, 1024), F32)
    for tt in range(NT):
        acc = acc + mm(dqg[tt, 0].reshape(256, HD), wt[2 * tt].reshape(HD, 1024), 1, 0)
    acc_s[...] = acc.reshape(4, 64, 1024)
    gws_of = lambda peer: gws.at[peer]
    for part in range(2):
        for j in (1, 3, 2):
            sender = (t + j) % NT
            for k in range(2):
                dq_second(part, k, sender, sender).wait_recv()
        acc = jnp.concatenate([acc_s[b] for b in chunks[part]], axis=0)
        for tt in range(NT):
            acc = acc + mm(
                jnp.concatenate([dqg[tt, 1, b] for b in chunks[part]], axis=0),
                wt[2 * tt + 1].reshape(HD, 1024), 1, 0,
            )
        acc = acc.astype(BF16)
        for k, b in enumerate(chunks[part]):
            gws[b] = acc[k * 64 : (k + 1) * 64]
        if part == 0:
            wait_in(x_from, 5, own_sdx, sdx)
            sdy[y, pl.ds(0, 8), :] = sdx[0] + sdx[1] + sdx[2] + sdx[3]
            own_sdy = lambda peer: sdy.at[y]
            start3(y_copy, 4, own_sdy, sdy)
        for j in ((2, 1), (3,))[part]:
            y_copy(2, gws_of, gwr, j).start()
    gwr[y] = gws[y]
    all_in(3, re)
    es[...] = mm(gt[...], re[...], 1, 0).astype(BF16).reshape(4, 64, 256)
    es_of = lambda peer: es.at[peer]
    start3(y_copy, 3, es_of, er)
    er[y] = es[y]

    mine = pl.ds(pl.multiple_of(y * 64, 64), 64)
    emb = (hidden_ref[...].astype(F32) * rcol[mine, 0:1] * gi).astype(BF16).astype(F32)
    rs_own = rscol[mine, 0:1]
    wait_in(y_from, 4, own_sdy, sdy)
    last = sdy[0] + sdy[1] + sdy[2] + sdy[3]
    sqm[...] = columns(2.0 * last[8:9] - (1.0 / D) * rs_all * rs_all * last[0:1])
    coef = sqm[mine, 0:1]
    direct = emb * coef
    wait_in(y_from, 2, gws_of, gwr)
    gw = (
        gwr[0].astype(F32) + gwr[1].astype(F32) + gwr[2].astype(F32) + gwr[3].astype(F32)
    ) * gu * rs_own + direct
    wait_in(y_from, 3, es_of, er)
    for h in range(8):
        lanes = slice(h * HD, (h + 1) * HD)
        par, q = h // 4, h % 4
        grad_ref[:, lanes] = er[q, :, halves[par]].astype(F32) + gw[:, lanes]

    for k, src, dst in (
        (0, own_hd, hd), (1, own_sel, selb), (2, gws_of, gwr), (3, es_of, er), (4, own_sdy, sdy),
        (5, own_sqy, sqy),
    ):
        wait_out(y_copy, k, src, dst)
    for k, src, dst in (
        (0, own_sqx, sqx), (5, own_sdx, sdx)
    ):
        wait_out(x_copy, k, src, dst)
    for j in (1, 3, 2):
        peer = (t + j) % NT
        dq_first(peer, t).wait_send()
        for part in range(2):
            for k in range(2):
                dq_second(part, k, peer, t).wait_send()
    for j in (1, 3, 2):
        for par in range(2):
            ps_copy((t + j) % NT * 2 + par).wait_send()
    for u in range(4):
        for j in (1, 3, 2):
            st_copy(u, j).wait_send()
    for stream in range(4):
        for step in range(RING[stream]):
            ring(stream, step).wait_send()
    for b in range(NZ):
        for half in range(2):
            partner(b, c, half).wait_send()
    most = pl.ds(0, (NS - 1) * 16)
    all_out(0, oute.at[most])
    all_out(1, outq.at[most, halves[0]])
    all_out(4, outq.at[most, halves[1]])
    all_out(2, rq.at[most, halves[0]])
    all_out(7, rq.at[most, halves[1]])
    all_out(3, re.at[most])
    all_out(5, sqi.at[pl.ds(0, 15)])
    all_out(6, sci.at[pl.ds(0, 15)])


def local(item_hidden, item_gain, send_item, pos_slot, hist_len, user_gain, query_weight):
    vmem = pltpu.VMEM
    dma = pltpu.SemaphoreType.DMA
    quarter = lambda kind: vmem((4, 256, 256), kind)
    grad, loss = pl.pallas_call(
        kernel,
        out_shape=(
            jax.ShapeDtypeStruct((64, 1024), F32),
            jax.ShapeDtypeStruct((4, 1, HIST), F32),
        ),
        in_specs=[pl.BlockSpec(memory_space=pltpu.HBM)] * 7,
        out_specs=(
            pl.BlockSpec(memory_space=pltpu.VMEM),
            pl.BlockSpec(memory_space=pltpu.VMEM),
        ),
        scratch_shapes=[
            pltpu.SMEM((4,), jnp.int32),
            vmem((64, 1024), BF16),
            vmem((1024,), BF16),
            vmem((1024,), BF16),
            vmem((4, 64), jnp.int32),
            vmem((4, HIST + CAND), jnp.int32),
            dma((8,)),
            vmem((4, 64, 1024), BF16),
            vmem((4, 1, 1024), F32),
            vmem((8, 2, 64, 1024), BF16),
            vmem((4, 16, HIST), F32),
            vmem((4, 8, HIST), F32),
            vmem((8, 256, HD), BF16),
            vmem((4, 2, 256, HD), BF16),
            vmem((1024, 256), BF16),
            vmem((1024, 256), BF16),
            quarter(BF16),
            quarter(BF16),
            vmem((256, 1024), BF16),
            quarter(BF16),
            quarter(BF16),
            vmem((8, 1, HIST), F32),
            vmem((16, 1, HIST), F32),
            vmem((256, HIST), F32),
            vmem((256, HIST), F32),
            vmem((256, 256), F32),
            vmem((256, HIST), F32),
            vmem((256, HIST), F32),
            vmem((4, 2 * HIST), jnp.int32),
            vmem((256, 1024), BF16),
            vmem((1024, 256), BF16),
            vmem((512, HIST), F32),
            vmem((4, 1, HIST), F32),
            vmem((4, 1, 256), F32),
            vmem((4, 1024, 256), BF16),
            vmem((4, 512, 256), BF16),
            vmem((4, 512, 256), BF16),
            vmem((4, 512, 256), BF16),
            vmem((8, 512, HIST), BF16),
            vmem((8, 512, HIST), BF16),
            vmem((8, HIST, HIST), F32),
            vmem((8, HIST, HIST), BF16),
            vmem((4, 512, 256), F32),
            vmem((4, 4, HIST, HIST), BF16),
            vmem((4, 2, HIST, HIST), F32),
            vmem((4, HIST, HIST), BF16),
            vmem((4, HIST, HIST), BF16),
            vmem((512, HIST), F32),
            vmem((4, 1, HIST), F32),
            vmem((2, 512, HD), BF16),
            vmem((2, 512, HD), BF16),
            vmem((4, 512, 256), BF16),
            vmem((4, 512, 256), BF16),
            vmem((4, 1024, 256), BF16),
            vmem((256, HIST), F32),
            quarter(BF16),
            quarter(BF16),
            vmem((1024, 256), BF16),
            vmem((1024, 256), BF16),
            vmem((16, 1, 256), F32),
            vmem((16, 1, 256), F32),
            vmem((4, 2, 4, 64, HD), BF16),
            vmem((4, 64, 1024), F32),
            vmem((4, 64, 1024), BF16),
            vmem((4, 64, 1024), BF16),
            vmem((4, 64, 256), BF16),
            vmem((4, 64, 256), BF16),
            vmem((4, 8, 256), F32),
            vmem((4, 16, 256), F32),
            dma((11, 4)),
            dma((11, 4)),
            dma((6, 4)),
            dma((6, 4)),
            dma((4, 4)),
            dma((4, 4)),
            dma((8, 2)),
            dma((8, 2)),
            dma((8,)),
            dma((8,)),
            dma((8,)),
            dma((4, 2)),
            pltpu.SemaphoreType.REGULAR((2, 4)),
        ],
        compiler_params=pltpu.CompilerParams(
            collective_id=0, has_side_effects=True, vmem_limit_bytes=40 * 1024 * 1024
        ),
    )(
        *[
            pltpu.with_memory_space_constraint(value, pltpu.HBM)
            for value in (
                hist_len, item_hidden, query_weight.T, item_gain, user_gain, send_item[0].T,
                pos_slot,
            )
        ]
    )
    return (grad, loss[:, 0, 0])


def solution(mesh):
    placed = (
        P("sect", "tp"),
        P("tp"),
        P("sect", None, None),
        P("sect", None),
        P("sect"),
        P("tp"),
        P("tp", "sect"),
    )
    return jax.shard_map(
        local, mesh=mesh, in_specs=placed, out_specs=(P("sect", "tp"), P("sect")), check_vma=False
    )
```
